32 devices in a mesh: dp: 16 (over z, x, core), tensor: 2 (over y).
Axes of the slice: x: 2, y: 2, z: 4, core: 2. Of those that a mesh axis runs over, the one named last changes fastest.
Arguments:
- tokens: bfloat16 [16384, 1024], P(('dp', 'tensor')), may hold values from -6 to 6
- query_weight: bfloat16 [1024, 1024], P('dp', 'tensor'), may hold values from -0.1875 to 0.1875
- key_weight: bfloat16 [1024, 1024], P('dp', 'tensor'), may hold values from -0.1875 to 0.1875
- value_weight: bfloat16 [1024, 1024], P('dp', 'tensor'), may hold values from -0.1875 to 0.1875
- out_weight: bfloat16 [1024, 1024], P('tensor', 'dp'), may hold values from -0.1875 to 0.1875
- gate_weight: bfloat16 [1024, 2816], P('dp', 'tensor'), may hold values from -0.1875 to 0.1875
- up_weight: bfloat16 [1024, 2816], P('dp', 'tensor'), may hold values from -0.1875 to 0.1875
- down_weight: bfloat16 [2816, 1024], P('tensor', 'dp'), may hold values from -0.109375 to 0.109375
- gain_attn_in: bfloat16 [1024], P('dp'), may hold values from 0.5 to 1.5
- gain_attn_out: bfloat16 [1024], P('dp'), may hold values from 0.5 to 1.5
- gain_ff_in: bfloat16 [1024], P('dp'), may hold values from 0.5 to 1.5
- gain_ff_out: bfloat16 [1024], P('dp'), may hold values from 0.5 to 1.5
- piece_starts: int32 [16, 2], P('dp'), may hold values from 0 to 768, as said below
- out_grad: bfloat16 [16384, 1024], P(('dp', 'tensor')), may hold values from -6 to 6
Outputs:
- layer_out: bfloat16 [16384, 1024], P(('dp', 'tensor'))
- input_grad: float32 [16384, 1024], P(('dp', 'tensor'))
- grad_query: float32 [1024, 1024], P('dp', 'tensor')
- grad_key: float32 [1024, 1024], P('dp', 'tensor')
- grad_value: float32 [1024, 1024], P('dp', 'tensor')
- grad_out: float32 [1024, 1024], P('tensor', 'dp')
- grad_gate: float32 [1024, 2816], P('dp', 'tensor')
- grad_up: float32 [1024, 2816], P('dp', 'tensor')
- grad_down: float32 [2816, 1024], P('tensor', 'dp')
- grad_gain_attn_in: float32 [1024], P('dp')
- grad_gain_attn_out: float32 [1024], P('dp')
- grad_gain_ff_in: float32 [1024], P('dp')
- grad_gain_ff_out: float32 [1024], P('dp')
The draws below stay inside these ranges and needn't reach their ends.
Inputs may be any that keep to these rules, and one draw needn't show every extreme that they name: `piece_starts`: each sequence's 2 pieces of 256 tokens are disjoint and in order: piece number k starts between k * 512 and (k + 1) * 512 - 256. In the first sequence the first piece starts at 0 and the last piece ends at the sequence's end.
All inputs are finite; a program needn't handle non-finite values.
Results may differ from the reference program's by a relative error of at most 0.023.
Values may be sent and summed in bfloat16 or wider, within the bound.
A program may use at most 192 MiB of HBM per device.

```python
import math
import jax
import jax.numpy as jnp
from jax import lax

D = 1024
HEADS = 8
HEAD_DIM = 128
FF = 2816
SEQ_LEN = 1024
PIECE = 256
PICS = 2
NSEQ = 16
TOKENS = 16384


def draw_piece_starts(key, part):
    slot_len = SEQ_LEN // PICS
    offsets = jax.random.randint(key, (NSEQ, PICS), 0, slot_len - PIECE + 1, dtype=jnp.int32)
    starts = offsets + jnp.arange(PICS, dtype=jnp.int32)[None, :] * slot_len
    row_index = jnp.arange(NSEQ, dtype=jnp.int32)[:, None]
    col_index = jnp.arange(PICS, dtype=jnp.int32)[None, :]
    starts = jnp.where((row_index == 0) & (col_index == 0), 0, starts)
    starts = jnp.where((row_index == 0) & (col_index == PICS - 1), SEQ_LEN - PIECE, starts)
    return starts.astype(jnp.int32)


def steps_of(rng, dims, cuts, least, top_value):
    def one(dim, parts):
        steps = jax.random.uniform(jax.random.fold_in(jax.random.fold_in(rng, 6), dim), (parts,), jnp.float32, least / len(cuts), top_value / len(cuts))
        return jnp.repeat(jnp.exp(steps), dims[dim] // parts).reshape((-1,) + (1,) * (len(dims) - dim - 1))

    gain = one(*cuts[0])
    for cut in cuts[1:]:
        gain = gain * one(*cut)
    return gain


def bell_draw(stream_key, shape, width, bound, shards=(), kind=jnp.bfloat16):
    drawn = jax.random.normal(stream_key, shape, jnp.float32) * width
    if len(shards) > 0:
        drawn = steps_of(stream_key, shape, shards, -0.22, 0.18) * drawn
    return jnp.clip(drawn, min=-bound, max=bound).astype(kind)


def setup_inputs(seed: int = 0) -> dict:
    keys = jax.random.split(jax.random.key(seed), 15)
    return {
        "tokens": bell_draw(keys[0], (TOKENS, D), 1.0, 6.0, ((0, 32),)),
        "query_weight": bell_draw(keys[1], (D, HEADS * HEAD_DIM), D ** -0.5, 0.1875, ((0, 16), (1, 2))),
        "key_weight": bell_draw(keys[2], (D, HEADS * HEAD_DIM), D ** -0.5, 0.1875, ((0, 16), (1, 2))),
        "value_weight": bell_draw(keys[3], (D, HEADS * HEAD_DIM), D ** -0.5, 0.1875, ((0, 16), (1, 2))),
        "out_weight": bell_draw(keys[4], (HEADS * HEAD_DIM, D), (HEADS * HEAD_DIM) ** -0.5, 0.1875, ((0, 2), (1, 16))),
        "gate_weight": bell_draw(keys[5], (D, FF), D ** -0.5, 0.1875, ((0, 16), (1, 2))),
        "up_weight": bell_draw(keys[6], (D, FF), D ** -0.5, 0.1875, ((0, 16), (1, 2))),
        "down_weight": bell_draw(keys[7], (FF, D), FF ** -0.5, 0.109375, ((0, 2), (1, 16))),
        "gain_attn_in": jnp.clip(1.0 + 0.1 * jax.random.normal(keys[8], (D,), jnp.float32), 0.5, 1.5).astype(jnp.bfloat16),
        "gain_attn_out": jnp.clip(1.0 + 0.1 * jax.random.normal(keys[9], (D,), jnp.float32), 0.5, 1.5).astype(jnp.bfloat16),
        "gain_ff_in": jnp.clip(1.0 + 0.1 * jax.random.normal(keys[10], (D,), jnp.float32), 0.5, 1.5).astype(jnp.bfloat16),
        "gain_ff_out": jnp.clip(1.0 + 0.1 * jax.random.normal(keys[11], (D,), jnp.float32), 0.5, 1.5).astype(jnp.bfloat16),
        "piece_starts": draw_piece_starts(jax.random.fold_in(keys[14], 71), 0),
        "out_grad": bell_draw(keys[13], (TOKENS, D), 1.0, 6.0, ((0, 32),)),
    }


norm_eps = 1e-06
rope_base = 50000.0

@jax.custom_vjp
def low(v):
    return lax.optimization_barrier(v.astype(jnp.bfloat16)).astype(jnp.float32)

@jax.custom_vjp
def low_back(v):
    return v

def low_keep(v):
    return (low(v), None)

def low_pass(kept, grad):
    return (grad,)

def back_keep(v):
    return (v, None)

def back_low(kept, grad):
    return (low(grad),)
low.defvjp(low_keep, low_pass)
low_back.defvjp(back_keep, back_low)

def rms_scale(values):
    return lax.rsqrt(lax.optimization_barrier(jnp.mean(values * values, axis=-1, keepdims=True)) + norm_eps)

def rotate(values, cosine, sine):
    half_dim = values.shape[-1] // 2
    lower_half = values[..., :half_dim]
    upper_half = values[..., half_dim:]
    return jnp.concatenate([lower_half * cosine - upper_half * sine, upper_half * cosine + lower_half * sine], axis=-1)

def piece_ids(starts):
    places = jnp.arange(SEQ_LEN, dtype=jnp.int32)
    inside = (places[:, None] >= starts[None, :]) & (places[:, None] < starts[None, :] + PIECE)
    labels = jnp.arange(1, PICS + 1, dtype=jnp.int32)
    return lax.optimization_barrier(jnp.sum(jnp.where(inside, labels[None, :], 0), axis=1)).astype(jnp.int32)

def layer(tok_rows, query_weight, key_weight, value_weight, out_weight, gate_weight, up_weight, down_weight, gain_attn_in, gain_attn_out, gain_ff_in, gain_ff_out, piece_id):
    highest = lax.Precision.HIGHEST
    half_dim = HEAD_DIM // 2
    inverse = rope_base ** (-(jnp.arange(half_dim, dtype=jnp.float32) * 2.0) / HEAD_DIM)
    places_f = jnp.arange(SEQ_LEN, dtype=jnp.float32)
    angles = places_f[:, None, None] * inverse[None, None, :]
    cosine = jnp.cos(angles)
    sine = jnp.sin(angles)
    places = jnp.arange(SEQ_LEN, dtype=jnp.int32)
    allowed = (places[None, :] <= places[:, None]) | (piece_id[:, None] == piece_id[None, :]) & (piece_id[:, None] > 0)

    def matmul(left, right):
        return jnp.dot(left, right, precision=highest)
    normed_in = low(tok_rows * rms_scale(tok_rows) * gain_attn_in)
    queries = low(rotate(low_back(matmul(normed_in, query_weight)).reshape(SEQ_LEN, HEADS, HEAD_DIM), cosine, sine))
    key_vecs = low(rotate(low_back(matmul(normed_in, key_weight)).reshape(SEQ_LEN, HEADS, HEAD_DIM), cosine, sine))
    values = low(low_back(matmul(normed_in, value_weight))).reshape(SEQ_LEN, HEADS, HEAD_DIM)
    raw_scores = low_back(jnp.einsum('qhd,khd->hqk', queries, key_vecs, precision=highest))
    logits = jnp.where(allowed[None], raw_scores * (1.0 / math.sqrt(HEAD_DIM)), -1e+30)
    probs = low(jax.nn.softmax(logits, axis=-1))
    attended = low_back(low(jnp.einsum('hqk,khd->qhd', probs, values, precision=highest))).reshape(SEQ_LEN, HEADS * HEAD_DIM)
    branch_attn = low_back(matmul(attended, out_weight))
    mid_rows = tok_rows + branch_attn * rms_scale(branch_attn) * gain_attn_out
    normed_ff = low(mid_rows * rms_scale(mid_rows) * gain_ff_in)
    gate_pre = low_back(matmul(normed_ff, gate_weight))
    up_pre = low_back(matmul(normed_ff, up_weight))
    hidden = low(jax.nn.silu(gate_pre) * up_pre)
    branch_ff = low_back(matmul(hidden, down_weight))
    return mid_rows + branch_ff * rms_scale(branch_ff) * gain_ff_out

def reference(tokens, query_weight, key_weight, value_weight, out_weight, gate_weight, up_weight, down_weight, gain_attn_in, gain_attn_out, gain_ff_in, gain_ff_out, piece_starts, out_grad):
    weights = tuple((item.astype(jnp.float32) for item in (query_weight, key_weight, value_weight, out_weight, gate_weight, up_weight, down_weight, gain_attn_in, gain_attn_out, gain_ff_in, gain_ff_out)))
    seq_rows = tokens.astype(jnp.float32).reshape(NSEQ, SEQ_LEN, D)
    seq_grads = out_grad.astype(jnp.float32).reshape(NSEQ, SEQ_LEN, D)

    def step(totals, seq_items):
        row_block, grad_block, starts = seq_items
        piece_id = piece_ids(starts)

        def forward(tok_rows, *params):
            return layer(tok_rows, *params, piece_id)
        result, pull = jax.vjp(forward, row_block, *weights)
        grads = pull(grad_block)
        totals = tuple((running + fresh for running, fresh in zip(totals, grads[1:])))
        return (totals, (result.astype(jnp.bfloat16), grads[0]))
    start_sums = tuple((jnp.zeros(item.shape, jnp.float32) for item in weights))
    sums, (outputs, input_grads) = lax.scan(step, start_sums, (seq_rows, seq_grads, piece_starts))
    return (outputs.reshape(TOKENS, D), input_grads.reshape(TOKENS, D), sums[0], sums[1], sums[2], sums[3], sums[4], sums[5], sums[6], sums[7], sums[8], sums[9], sums[10])
```

```python
import functools
import math

import jax
import jax.numpy as jnp
from jax import lax
from jax.experimental import pallas as pl
from jax.experimental.pallas import tpu as pltpu
from jax.sharding import PartitionSpec as P

HEAD_DIM = 128
PIECE = 256


norm_eps = 1e-06
rope_base = 50000.0
masked = -1e30


def rms_scale(values):
    return lax.rsqrt(jnp.mean(values * values, axis=-1, keepdims=True) + norm_eps)


def norm_back(values, scale, gain, incoming):
    weighted = gain * incoming
    row_inner = jnp.mean(values * weighted, axis=-1, keepdims=True)
    backward = scale * weighted - values * (scale * scale * scale) * row_inner
    return (backward, jnp.sum(values * scale * incoming, axis=0))


def rope_at(places):
    half_dim = HEAD_DIM // 2
    inverse = rope_base ** (-(jnp.arange(half_dim, dtype=jnp.float32) * 2.0) / HEAD_DIM)
    angles = places.astype(jnp.float32)[:, None, None] * inverse[None, None, :]
    return (jnp.cos(angles), jnp.sin(angles))


def rope_tables(count, length):
    return rope_at(jnp.arange(count, dtype=jnp.int32) % length)


def rotate(values, cosine, sine):
    half_dim = values.shape[-1] // 2
    lower_half = values[..., :half_dim]
    upper_half = values[..., half_dim:]
    return jnp.concatenate(
        [lower_half * cosine - upper_half * sine, upper_half * cosine + lower_half * sine], axis=-1
    )


def unrotate(grads, cosine, sine):
    half_dim = grads.shape[-1] // 2
    lower_half = grads[..., :half_dim]
    upper_half = grads[..., half_dim:]
    return jnp.concatenate(
        [lower_half * cosine + upper_half * sine, upper_half * cosine - lower_half * sine], axis=-1
    )


def piece_ids(starts, length):
    places = jnp.arange(length, dtype=jnp.int32)
    inside = (places[None, :, None] >= starts[:, None, :]) & (
        places[None, :, None] < starts[:, None, :] + PIECE
    )
    labels = jnp.arange(1, starts.shape[1] + 1, dtype=jnp.int32)
    return jnp.sum(jnp.where(inside, labels, 0), axis=2)


def visible(piece_id, offset, count):
    length = piece_id.shape[0]
    query_place = offset + jnp.arange(count, dtype=jnp.int32)
    key_place = jnp.arange(length, dtype=jnp.int32)
    query_ids = piece_id[offset : offset + count]
    return (key_place[None, :] <= query_place[:, None]) | (
        query_ids[:, None] == piece_id[None, :]
    ) & (query_ids[:, None] > 0)


def block_scores(queries, key_vecs, piece_id, offset, count):
    attn_scale = 1.0 / math.sqrt(queries.shape[-1])
    q_block = queries[offset : offset + count]
    scores = (
        jnp.einsum("qhd,khd->hqk", q_block, key_vecs, preferred_element_type=jnp.float32)
        * attn_scale
    )
    return (jnp.where(visible(piece_id, offset, count)[None], scores, masked), q_block)


def attend_one(seq_items):
    queries, key_vecs, values, piece_id = seq_items
    length = queries.shape[0]
    block_rows = min(512, length)
    outputs = []
    log_totals = []
    for offset in range(0, length, block_rows):
        logits, q_block = block_scores(queries, key_vecs, piece_id, offset, block_rows)
        row_max = jnp.max(logits, axis=-1, keepdims=True)
        log_total = row_max + jnp.log(jnp.sum(jnp.exp(logits - row_max), axis=-1, keepdims=True))
        probs = jnp.exp(logits - log_total).astype(jnp.bfloat16)
        mixed = jnp.einsum("hqk,khd->qhd", probs, values, preferred_element_type=jnp.float32)
        outputs.append(mixed.astype(jnp.bfloat16))
        log_totals.append(log_total)
    return (jnp.concatenate(outputs, axis=0), jnp.concatenate(log_totals, axis=1))


def attend_back(seq_items):
    queries, key_vecs, values, piece_id, log_totals, grad_mixed = seq_items
    length = queries.shape[0]
    block_rows = min(512, length)
    attn_scale = 1.0 / math.sqrt(queries.shape[-1])
    grad_keys = jnp.zeros(key_vecs.shape, jnp.float32)
    grad_values = jnp.zeros(values.shape, jnp.float32)
    grad_queries = []
    for offset in range(0, length, block_rows):
        logits, q_block = block_scores(queries, key_vecs, piece_id, offset, block_rows)
        probs = jnp.exp(logits - log_totals[:, offset : offset + block_rows])
        grad_block = grad_mixed[offset : offset + block_rows]
        grad_values = grad_values + jnp.einsum(
            "hqk,qhd->khd",
            probs.astype(jnp.bfloat16),
            grad_block,
            preferred_element_type=jnp.float32,
        )
        grad_probs = jnp.einsum(
            "qhd,khd->hqk", grad_block, values, preferred_element_type=jnp.float32
        )
        row_inner = jnp.sum(probs * grad_probs, axis=-1, keepdims=True)
        grad_scores = (probs * (grad_probs - row_inner) * attn_scale).astype(jnp.bfloat16)
        grad_queries.append(
            jnp.einsum("hqk,khd->qhd", grad_scores, key_vecs, preferred_element_type=jnp.float32)
        )
        grad_keys = grad_keys + jnp.einsum(
            "hqk,qhd->khd", grad_scores, q_block, preferred_element_type=jnp.float32
        )
    return (jnp.concatenate(grad_queries, axis=0), grad_keys, grad_values)


def times_trans(left, right):
    return lax.dot_general(
        left, right, (((1,), (1,)), ((), ())), preferred_element_type=jnp.float32
    )


def trans_times(left, right):
    return lax.dot_general(
        left, right, (((0,), (0,)), ((), ())), preferred_element_type=jnp.float32
    )


def fetch_weights(shards):
    gathered = (
        lax.all_gather(shards[0], "dp", axis=0, tiled=True),
        lax.all_gather(shards[1], "dp", axis=0, tiled=True),
        lax.all_gather(shards[2], "dp", axis=0, tiled=True),
        lax.all_gather(shards[3], "dp", axis=1, tiled=True),
        lax.all_gather(shards[4], "dp", axis=0, tiled=True),
        lax.all_gather(shards[5], "dp", axis=0, tiled=True),
        lax.all_gather(shards[6], "dp", axis=1, tiled=True),
        lax.all_gather(shards[7], "dp", axis=1, tiled=True),
    )
    return gathered


def gather_rows(normed):
    return lax.all_gather(normed, "tensor", axis=0, tiled=True)


def sum_rows(sum_terms):
    return lax.psum_scatter(sum_terms, "tensor", scatter_dimension=0, tiled=True)


def gather_grads(grad_terms):
    return lax.all_gather(grad_terms, "tensor", axis=0, tiled=True)


def sum_grads(grad_terms):
    return lax.psum_scatter(
        grad_terms.astype(jnp.bfloat16), "tensor", scatter_dimension=0, tiled=True
    ).astype(jnp.float32)


def by_sequence(values, seq_count):
    return values.reshape(seq_count, values.shape[0] // seq_count, values.shape[1], values.shape[2])


def attention_part(normed, gathered, cosine, sine, piece_id):
    whole_rows = gather_rows(normed)
    group_rows = whole_rows.shape[0]
    seq_count = piece_id.shape[0]

    def project(weight):
        return jnp.dot(whole_rows, weight, preferred_element_type=jnp.float32).reshape(
            group_rows, -1, HEAD_DIM
        )

    queries = rotate(project(gathered[0]), cosine, sine).astype(jnp.bfloat16)
    key_vecs = rotate(project(gathered[1]), cosine, sine).astype(jnp.bfloat16)
    values = project(gathered[2]).astype(jnp.bfloat16)
    outputs, log_totals = lax.map(
        attend_one,
        (
            by_sequence(queries, seq_count),
            by_sequence(key_vecs, seq_count),
            by_sequence(values, seq_count),
            piece_id,
        ),
    )
    return (whole_rows, queries, key_vecs, values, outputs.reshape(group_rows, -1), log_totals)


def feed_part(normed, gathered):
    whole_rows = gather_rows(normed)
    gate_pre = jnp.dot(whole_rows, gathered[4], preferred_element_type=jnp.float32)
    up_pre = jnp.dot(whole_rows, gathered[5], preferred_element_type=jnp.float32)
    hidden = (jax.nn.silu(gate_pre) * up_pre).astype(jnp.bfloat16)
    return (whole_rows, gate_pre, up_pre, hidden)


def on_device(
    tokens,
    query_weight,
    key_weight,
    value_weight,
    out_weight,
    gate_weight,
    up_weight,
    down_weight,
    gain_attn_in,
    gain_attn_out,
    gain_ff_in,
    gain_ff_out,
    piece_starts,
    out_grad,
):
    shards = (
        query_weight,
        key_weight,
        value_weight,
        out_weight,
        gate_weight,
        up_weight,
        down_weight,
        jnp.stack([gain_attn_in, gain_attn_out, gain_ff_in, gain_ff_out]),
    )
    gathered = fetch_weights(shards)
    gain_rows = gathered[7].astype(jnp.float32)
    tok_rows = tokens.astype(jnp.float32)
    seq_count = piece_starts.shape[0]
    own_rows = tokens.shape[0]
    group_rows = own_rows * lax.axis_size("tensor")
    length = group_rows // seq_count
    piece_id = piece_ids(piece_starts, length)
    incoming = out_grad.astype(jnp.float32)
    scale_in = rms_scale(tok_rows)
    normed_in = (tok_rows * scale_in * gain_rows[0]).astype(jnp.bfloat16)
    cosine, sine = rope_tables(group_rows, length)
    attn_parts = attention_part(normed_in, gathered, cosine, sine, piece_id)
    branch_attn = sum_rows(jnp.dot(attn_parts[4], gathered[3], preferred_element_type=jnp.float32))
    scale_attn = rms_scale(branch_attn)
    mid_rows = tok_rows + branch_attn * scale_attn * gain_rows[1]
    scale_mid = rms_scale(mid_rows)
    normed_ff = (mid_rows * scale_mid * gain_rows[2]).astype(jnp.bfloat16)
    feed_parts = feed_part(normed_ff, gathered)
    branch_ff = sum_rows(jnp.dot(feed_parts[3], gathered[6], preferred_element_type=jnp.float32))
    scale_ff = rms_scale(branch_ff)
    result = (mid_rows + branch_ff * scale_ff * gain_rows[3]).astype(jnp.bfloat16)
    gathered = fetch_weights(shards)
    feed_parts = feed_part(normed_ff, gathered)
    whole_ff, gate_pre, up_pre, hidden = feed_parts
    back_ff, gain_grad_ff_out = norm_back(branch_ff, scale_ff, gain_rows[3], incoming)
    wide_back_ff = gather_grads(back_ff.astype(jnp.bfloat16))
    grad_down = trans_times(hidden, wide_back_ff)
    back_hidden = times_trans(wide_back_ff, gathered[6])
    sigmoid_gate = jax.nn.sigmoid(gate_pre)
    back_gate = (
        back_hidden * up_pre * sigmoid_gate * (1.0 + gate_pre * (1.0 - sigmoid_gate))
    ).astype(jnp.bfloat16)
    back_up = (back_hidden * gate_pre * sigmoid_gate).astype(jnp.bfloat16)
    grad_gate = trans_times(whole_ff, back_gate)
    grad_up = trans_times(whole_ff, back_up)
    back_normed_ff = sum_grads(
        times_trans(back_gate, gathered[4]) + times_trans(back_up, gathered[5])
    )
    back_from_ff, gain_grad_ff_in = norm_back(mid_rows, scale_mid, gain_rows[2], back_normed_ff)
    back_mid = incoming + back_from_ff
    back_attn, gain_grad_attn_out = norm_back(branch_attn, scale_attn, gain_rows[1], back_mid)
    wide_back_attn = gather_grads(back_attn.astype(jnp.bfloat16))
    attn_parts = attention_part(normed_in, gathered, cosine, sine, piece_id)
    whole_in, queries, key_vecs, values, attended, log_totals = attn_parts
    grad_out = trans_times(attended, wide_back_attn)
    back_attended = times_trans(wide_back_attn, gathered[3]).astype(jnp.bfloat16)
    back_queries, back_keys, back_values = lax.map(
        attend_back,
        (
            by_sequence(queries, seq_count),
            by_sequence(key_vecs, seq_count),
            by_sequence(values, seq_count),
            piece_id,
            log_totals,
            by_sequence(back_attended.reshape(group_rows, -1, HEAD_DIM), seq_count),
        ),
    )
    back_queries = (
        unrotate(back_queries.reshape(group_rows, -1, HEAD_DIM), cosine, sine)
        .reshape(group_rows, -1)
        .astype(jnp.bfloat16)
    )
    back_keys = (
        unrotate(back_keys.reshape(group_rows, -1, HEAD_DIM), cosine, sine)
        .reshape(group_rows, -1)
        .astype(jnp.bfloat16)
    )
    back_values = back_values.reshape(group_rows, -1).astype(jnp.bfloat16)
    grad_query = trans_times(whole_in, back_queries)
    grad_key = trans_times(whole_in, back_keys)
    grad_value = trans_times(whole_in, back_values)
    back_normed_in = sum_grads(
        times_trans(back_queries, gathered[0])
        + times_trans(back_keys, gathered[1])
        + times_trans(back_values, gathered[2])
    )
    back_from_in, gain_grad_attn_in = norm_back(tok_rows, scale_in, gain_rows[0], back_normed_in)
    input_grad = back_mid + back_from_in
    weight_terms = (grad_query, grad_key, grad_value, grad_out, grad_gate, grad_up, grad_down)
    gain_grads = lax.psum(
        jnp.stack([gain_grad_attn_in, gain_grad_attn_out, gain_grad_ff_in, gain_grad_ff_out]),
        "tensor",
    )
    grad_sums = (
        lax.psum_scatter(
            weight_terms[0].astype(jnp.bfloat16), "dp", scatter_dimension=0, tiled=True
        ).astype(jnp.float32),
        lax.psum_scatter(
            weight_terms[1].astype(jnp.bfloat16), "dp", scatter_dimension=0, tiled=True
        ).astype(jnp.float32),
        lax.psum_scatter(
            weight_terms[2].astype(jnp.bfloat16), "dp", scatter_dimension=0, tiled=True
        ).astype(jnp.float32),
        lax.psum_scatter(
            weight_terms[3].astype(jnp.bfloat16), "dp", scatter_dimension=1, tiled=True
        ).astype(jnp.float32),
        lax.psum_scatter(
            weight_terms[4].astype(jnp.bfloat16), "dp", scatter_dimension=0, tiled=True
        ).astype(jnp.float32),
        lax.psum_scatter(
            weight_terms[5].astype(jnp.bfloat16), "dp", scatter_dimension=0, tiled=True
        ).astype(jnp.float32),
        lax.psum_scatter(
            weight_terms[6].astype(jnp.bfloat16), "dp", scatter_dimension=1, tiled=True
        ).astype(jnp.float32),
        lax.psum_scatter(
            gain_grads.astype(jnp.bfloat16), "dp", scatter_dimension=1, tiled=True
        ).astype(jnp.float32),
    )
    return (
        result,
        input_grad,
        grad_sums[0],
        grad_sums[1],
        grad_sums[2],
        grad_sums[3],
        grad_sums[4],
        grad_sums[5],
        grad_sums[6],
        grad_sums[7][0],
        grad_sums[7][1],
        grad_sums[7][2],
        grad_sums[7][3],
    )


LANES = 128
HALF = HEAD_DIM // 2
MESH = pl.DeviceIdType.MESH
f32 = jnp.float32
bf16 = jnp.bfloat16


class Plan:
    def __init__(self, rows, width, head_cols, ff_cols, shard_rows):
        self.rows = rows
        self.width = width
        self.head_cols = head_cols
        self.ff_cols = ff_cols
        self.shard_rows = shard_rows
        self.heads = 2 * head_cols // HEAD_DIM
        self.k_at = LANES
        self.v_at = self.k_at + head_cols
        self.q_at = self.v_at + head_cols
        self.o_at = self.q_at + head_cols
        self.gu_at = self.o_at + head_cols
        self.d_at = self.gu_at + 2 * ff_cols
        self.cols = self.d_at + ff_cols
        self.kvq = 3 * head_cols

        def cuts(start, total):
            pieces = []
            while total > 0:
                size = min(512, total)
                pieces.append((start, size))
                start, total = start + size, total - size
            return pieces

        self.gu_cuts = cuts(self.gu_at, 2 * ff_cols)
        self.d_cuts = cuts(self.d_at, ff_cols)
        self.gather = (
            [(0, LANES + head_cols), (self.v_at, head_cols), (self.q_at, head_cols), (self.o_at, head_cols)]
            + self.gu_cuts
            + self.d_cuts
        )
        self.reduce = (
            self.d_cuts
            + self.gu_cuts
            + [(self.o_at, head_cols), (self.q_at, head_cols), (self.v_at, head_cols), (self.k_at, head_cols), (0, LANES)]
        )


def sigmoid(v):
    return 0.5 * jnp.tanh(0.5 * v) + 0.5


def dot_nn(left, right):
    return lax.dot_general(left, right, (((1,), (0,)), ((), ())), preferred_element_type=f32)


def dot_nt(left, right):
    return lax.dot_general(left, right, (((1,), (1,)), ((), ())), preferred_element_type=f32)


def dot_tn(left, right):
    return lax.dot_general(left, right, (((0,), (0,)), ((), ())), preferred_element_type=f32)


def fused_layer(
    plan,
    shard_ref, tok_hbm, og_hbm, starts_ref, cos_ref, sin_ref,
    out_hbm, ig_hbm, gr_hbm,
    W, KVQ, KVp, xo, xp, T, att, ba, mid, bff, nf, GU, HID, BF, TB, LO, MK, gains, dgains, stat_a, stat_b,
    R1, R2A, R2B, R3A, R3B, R4, ST,
    ag_s, ag_r, rs_s, rs_r, loc, extra_s, extra_r, credit,
):
    p = plan
    dp = lax.axis_index("dp")
    y = lax.axis_index("tensor")
    c = lax.rem(dp, 2)
    x = lax.rem(dp // 2, 2)
    z = dp // 4
    rows, width, hc, ff = p.rows, p.width, p.head_cols, p.ff_cols
    first = y == 0
    second = y == 1

    def dev(zz, xx, cc, yy):
        return (zz * 4 + xx * 2 + cc, yy)

    def up(step):
        return lax.rem(z + step, 4)

    core_peer = dev(z, x, 1 - c, y)
    x_peer = dev(z, 1 - x, c, y)
    y_peer = dev(z, x, c, 1 - y)
    z_peers = [dev(up(d), x, c, y) for d in (1, 2, 3)]
    z_sources = [dev(up(4 - d), x, c, y) for d in (1, 2, 3)]

    def remote(src, dst, send, recv, to):
        return pltpu.make_async_remote_copy(
            src_ref=src, dst_ref=dst, send_sem=send, recv_sem=recv, device_id=to, device_id_type=MESH
        )

    def cut(at, size):
        return pl.ds(at if isinstance(at, int) else pl.multiple_of(at, LANES), size)

    def weight(yy, at, size, zz=None):
        if zz is None:
            return W[yy, :, :, :, :, cut(at, size)].reshape(width, size)
        return W[yy, zz, :, :, :, cut(at, size)].reshape(width // 4, size)

    def put_weight(yy, at, size, value):
        W[yy, :, :, :, :, cut(at, size)] = value.astype(bf16).reshape(4, 2, 2, p.shard_rows, size)

    def rms(v):
        return lax.rsqrt(jnp.mean(v * v, axis=-1, keepdims=True) + norm_eps)

    def norm_grad(v, scale, gain, e):
        weighted = gain * e
        inner = jnp.mean(v * weighted, axis=-1, keepdims=True)
        return scale * weighted - v * (scale * scale * scale) * inner

    def by_rows(body, size=64):
        def step(i, carry):
            body(pl.ds(pl.multiple_of(i * size, size), size))
            return carry

        lax.fori_loop(0, rows // size, step, 0)

    def loop(count, body):
        def step(i, carry):
            body(i)
            return carry

        lax.fori_loop(0, count, step, 0)

    def ag(k, m):
        at, size = p.gather[k]
        cols = pl.ds(at, size)
        sem = (ag_s.at[k, m], ag_r.at[k, m])
        if m < 3:
            return remote(shard_ref.at[:, cols], W.at[y, z, x, c, :, cols], *sem, z_peers[m])
        if m == 3:
            ref = W.at[y, pl.ds(0, 2), x, c, :, cols]
            return remote(ref, ref, *sem, x_peer)
        if m == 4:
            ref = W.at[y, pl.ds(2, 2), x, c, :, cols]
            return remote(ref, ref, *sem, y_peer)
        if m == 5:
            ref = W.at[y, pl.ds(0, 2), :, c, :, cols]
            return remote(ref, ref, *sem, y_peer)
        if m == 6:
            ref = W.at[:, pl.ds(2, 2), x, c, :, cols]
            return remote(ref, ref, *sem, x_peer)
        ref = W.at[:, :, :, c, :, cols]
        return remote(ref, ref, *sem, core_peer)

    n_gather = len(p.gather)

    def ag_step(s):
        if 0 <= s < n_gather:
            for m in (0, 1, 2):
                ag(s, m).wait_recv()
            ag(s, 3).start()
            ag(s, 4).start()
        if 0 <= s - 1 < n_gather:
            ag(s - 1, 3).wait_recv()
            ag(s - 1, 5).start()
            ag(s - 1, 4).wait_recv()
            ag(s - 1, 6).start()
        if 0 <= s - 2 < n_gather:
            ag(s - 2, 5).wait_recv()
            ag(s - 2, 6).wait_recv()
            ag(s - 2, 7).start()
        if 0 <= s - 3 < n_gather:
            ag(s - 3, 7).wait_recv()

    load_tok = pltpu.make_async_copy(tok_hbm, TB, loc.at[0])
    load_tok.start()
    own_w = pltpu.make_async_copy(shard_ref, W.at[y, z, x, c], loc.at[1])
    own_w.start()
    barrier = pltpu.get_barrier_semaphore()
    for peer in [core_peer, x_peer, y_peer] + z_peers:
        pl.semaphore_signal(barrier, inc=1, device_id=peer, device_id_type=MESH)
    pl.semaphore_wait(barrier, 6)

    tok_send = remote(tok_hbm, xp, extra_s.at[0], extra_r.at[0], y_peer)

    @pl.when(first)
    def _():
        tok_send.start()

    for k in range(n_gather):
        for m in (0, 1, 2):
            ag(k, m).start()
    own_w.wait()
    load_tok.wait()

    start = starts_ref[0, y] - y * rows

    def build_mask(query_dim):
        def body(blk):
            shape = (64, rows)
            r = lax.broadcasted_iota(jnp.int32, shape, 0) + blk.start
            s = lax.broadcasted_iota(jnp.int32, shape, 1)
            q_pos, k_pos = (r, s) if query_dim == 0 else (s, r)
            inside = (r >= start) & (r < start + PIECE) & (s >= start) & (s < start + PIECE)
            MK[blk, :] = jnp.where((k_pos <= q_pos) | inside, 0.0, masked)

        by_rows(body)

    build_mask(0)
    dgains[...] = jnp.zeros_like(dgains)

    for s in range(0, 4):
        ag_step(s)

    gains[0:8, 0:width] = jnp.transpose(weight(0, 0, LANES).astype(f32))[0:8, :]

    def norm_in(src, dst):
        def body(blk):
            t = src[blk, :].astype(f32)
            dst[blk, :] = (t * rms(t) * gains[0:1, :]).astype(bf16)

        by_rows(body)

    norm_in(TB, xo)

    @pl.when(second)
    def _():
        tok_send.wait_recv()
        norm_in(xp, xp)

    ag_step(4)
    ag_step(5)

    def rotated(u, place, sign):
        return u * cos_ref[place, :] + sign * (pltpu.roll(u, HALF, 1) * sin_ref[place, :])

    def project(src, dst, at, place, turn):
        def run(yy, off):
            r = dot_nn(src[...], weight(yy, LANES + off, 256))
            for hh in range(2):
                u = r[:, hh * HEAD_DIM : (hh + 1) * HEAD_DIM]
                if turn:
                    u = rotated(u, place, 1.0)
                dst[yy, :, cut(off + hh * HEAD_DIM, HEAD_DIM)] = u.astype(bf16)

        per = hc // 256
        loop(2 * per, lambda i: run(i // per, pl.multiple_of(at + lax.rem(i, per) * 256, 256)))

    own_place = pl.ds(pl.multiple_of(y * rows, rows), rows)
    old_place = pl.ds(0, rows)
    project(xo, KVQ, 0, own_place, True)
    project(xo, KVQ, hc, own_place, False)
    project(xo, KVQ, 2 * hc, own_place, True)

    @pl.when(second)
    def _():
        project(xp, KVp, 0, old_place, True)
        project(xp, KVp, hc, old_place, False)

    ag_step(6)

    per_y = hc // HEAD_DIM
    attn_scale = 1.0 / math.sqrt(HEAD_DIM)
    log2_scale = attn_scale * math.log2(math.e)
    lane = lax.broadcasted_iota(jnp.int32, (1, LANES), 1)

    def head_at(h):
        yy = h // per_y
        off = pl.multiple_of(lax.rem(h, per_y) * HEAD_DIM, HEAD_DIM)
        return yy, cut(off, HEAD_DIM), cut(off + hc, HEAD_DIM), cut(off + 2 * hc, HEAD_DIM)

    def attend(i, both):
        h = i // 2
        blk = pl.ds(pl.multiple_of(lax.rem(i, 2) * (rows // 2), rows // 2), rows // 2)
        yy, k_at, v_at, q_at = head_at(h)
        q = KVQ[yy, blk, q_at]
        s = dot_nt(q, KVQ[yy, :, k_at]) * log2_scale + MK[blk, :]
        top = jnp.max(s, axis=-1, keepdims=True)
        if both:
            s_old = dot_nt(q, KVp[yy, :, k_at]) * log2_scale
            top = jnp.maximum(top, jnp.max(s_old, axis=-1, keepdims=True))
        e = jnp.exp2(s - top)
        total = jnp.sum(e, axis=-1, keepdims=True)
        if both:
            e_old = jnp.exp2(s_old - top)
            total = total + jnp.sum(e_old, axis=-1, keepdims=True)
        inv = 1.0 / total
        o = dot_nn((e * inv).astype(bf16), KVQ[yy, :, v_at])
        if both:
            o = o + dot_nn((e_old * inv).astype(bf16), KVp[yy, :, v_at])
        att[blk, pl.ds(pl.multiple_of(h * HEAD_DIM, HEAD_DIM), HEAD_DIM)] = o.astype(bf16)
        stat = top + jnp.log2(total)
        stat_a[blk, :] = jnp.where(lane == h, stat, stat_a[blk, :])

    def attend_heads(lo, hi):
        @pl.when(first)
        def _():
            loop(2 * (hi - lo), lambda i: attend(i + 2 * lo, False))

        @pl.when(second)
        def _():
            loop(2 * (hi - lo), lambda i: attend(i + 2 * lo, True))

    stat_a[...] = jnp.zeros_like(stat_a)
    attend_heads(0, p.heads)
    ag_step(7)

    def o_proj(zz):
        cols = pl.ds(pl.multiple_of(zz * (width // 4), width // 4), width // 4)
        ba[:, cols] = dot_nt(att[:, 0:hc], weight(0, p.o_at, hc, zz)) + dot_nt(
            att[:, hc : 2 * hc], weight(1, p.o_at, hc, zz)
        )

    loop(4, o_proj)

    def mid_rows(blk):
        b = ba[blk, :]
        m = TB[blk, :].astype(f32) + b * rms(b) * gains[1:2, :]
        mid[blk, :] = m
        nf[blk, :] = (m * rms(m) * gains[2:3, :]).astype(bf16)

    by_rows(mid_rows)
    load_og = pltpu.make_async_copy(og_hbm, TB, loc.at[0])
    load_og.start()
    ag_step(8)

    def gate_up(lo, hi):
        def run(i):
            yy = i // (hi - lo)
            t = lax.rem(i, hi - lo) + lo
            off = pl.multiple_of(t * 256, 256)
            r = dot_nn(nf[...], weight(yy, p.gu_at + off, 256))
            g, u = r[:, 0:LANES], r[:, LANES:256]
            GU[yy, :, pl.ds(off, 256)] = r.astype(bf16)
            HID[yy, :, pl.ds(pl.multiple_of(t * LANES, LANES), LANES)] = (
                g * sigmoid(g) * u
            ).astype(bf16)

        loop(2 * (hi - lo), run)

    ag_step(9)
    gate_up(0, 6)
    ag_step(10)
    ag_step(11)
    ag_step(12)
    gate_up(6, 2 * ff // 256)
    for s in range(13, n_gather + 3):
        ag_step(s)

    def down_proj(zz):
        cols = pl.ds(pl.multiple_of(zz * (width // 4), width // 4), width // 4)
        bff[:, cols] = dot_nt(HID[0], weight(0, p.d_at, ff, zz)) + dot_nt(HID[1], weight(1, p.d_at, ff, zz))

    loop(4, down_proj)
    load_og.wait()

    def out_rows(blk):
        b = bff[blk, :]
        scale = rms(b)
        e = TB[blk, :].astype(f32)
        LO[blk, :] = (mid[blk, :] + b * scale * gains[3:4, :]).astype(bf16)
        BF[blk, :] = norm_grad(b, scale, gains[3:4, :], e).astype(bf16)
        dgains[3:4, :] += jnp.sum(b * scale * e, axis=0, keepdims=True)

    by_rows(out_rows)
    put_out = pltpu.make_async_copy(LO, out_hbm, loc.at[1])
    put_out.start()

    for k in range(n_gather):
        for m in range(8):
            ag(k, m).wait_send()

    n_reduce = len(p.reduce)

    def rs(j, m):
        at, size = p.reduce[j]
        cols, slot, part = pl.ds(at, size), j % 2, pl.ds(0, size)
        sem = (rs_s.at[j, m], rs_r.at[j, m])
        low, high = pl.ds(0, 2), pl.ds(2, 2)
        if m == 0:
            return remote(W.at[:, :, :, 1 - c, :, cols], R1.at[slot, :, :, :, :, part], *sem, core_peer)
        if m == 1:
            return remote(W.at[1 - y, low, :, c, :, cols], R2A.at[slot, :, :, :, part], *sem, y_peer)
        if m == 2:
            return remote(W.at[:, high, 1 - x, c, :, cols], R2B.at[slot, :, :, :, part], *sem, x_peer)
        if m == 3:
            return remote(W.at[y, low, 1 - x, c, :, cols], R3A.at[slot, :, :, part], *sem, x_peer)
        if m == 4:
            return remote(W.at[1 - y, high, x, c, :, cols], R3B.at[slot, :, :, part], *sem, y_peer)
        d = m - 5
        return remote(W.at[y, up(d + 1), x, c, :, cols], R4.at[slot, d, :, part], *sem, z_peers[d])

    rs_sources = [core_peer, y_peer, x_peer, x_peer, y_peer] + z_sources

    def rs_start(j, m):
        if j >= 2:
            pl.semaphore_wait(credit.at[m], 1)
        rs(j, m).start()

    def rs_used(j, m):
        if j + 2 < n_reduce:
            pl.semaphore_signal(credit.at[m], inc=1, device_id=rs_sources[m], device_id_type=MESH)

    def put_sum(j):
        at, size = p.reduce[j]
        return pltpu.make_async_copy(
            ST.at[j % 2, :, pl.ds(0, size)], gr_hbm.at[:, pl.ds(at, size)], loc.at[2 + j % 2]
        )

    def rs_event(j, phase):
        at, size = p.reduce[j]
        cols, slot, part = pl.ds(at, size), j % 2, pl.ds(0, size)
        if phase == 0:
            rs_start(j, 0)
        elif phase == 1:
            rs(j, 0).wait_recv()

            def add(i):
                a, b, d = i // 8, lax.rem(i // 2, 4), lax.rem(i, 2)
                W[a, b, d, c, :, cols] = W[a, b, d, c, :, cols] + R1[slot, a, b, d, :, part]

            loop(16, add)
            rs_used(j, 0)
            rs_start(j, 1)
            rs_start(j, 2)
        elif phase == 2:
            rs(j, 1).wait_recv()

            def add_a(i):
                b, d = i // 2, lax.rem(i, 2)
                W[y, b, d, c, :, cols] = W[y, b, d, c, :, cols] + R2A[slot, b, d, :, part]

            loop(4, add_a)
            rs_used(j, 1)
            rs_start(j, 3)
            rs(j, 2).wait_recv()

            def add_b(i):
                a, b = i // 2, lax.rem(i, 2)
                W[a, b + 2, x, c, :, cols] = W[a, b + 2, x, c, :, cols] + R2B[slot, a, b, :, part]

            loop(4, add_b)
            rs_used(j, 2)
            rs_start(j, 4)
        elif phase == 3:
            rs(j, 3).wait_recv()
            rs(j, 4).wait_recv()
            for b in range(2):
                W[y, b, x, c, :, cols] = W[y, b, x, c, :, cols] + R3A[slot, b, :, part]
                W[y, b + 2, x, c, :, cols] = W[y, b + 2, x, c, :, cols] + R3B[slot, b, :, part]
            rs_used(j, 3)
            rs_used(j, 4)
            for m in (5, 6, 7):
                rs_start(j, m)
        else:
            for m in (5, 6, 7):
                rs(j, m).wait_recv()
            if j >= 2:
                put_sum(j - 2).wait()
            total = W[y, z, x, c, :, cols].astype(f32)
            for d in range(3):
                total = total + R4[slot, d, :, part].astype(f32)
            ST[slot, :, part] = total
            for m in (5, 6, 7):
                rs_used(j, m)
            put_sum(j).start()

    events = [(j, t - j) for t in range(n_reduce + 4) for j in range(n_reduce) if 0 <= t - j <= 4]
    done = [0]

    def pump(ready, until):
        while done[0] < len(events):
            j, phase = events[done[0]]
            if j >= ready or j + phase >= until:
                break
            rs_event(j, phase)
            done[0] += 1

    def back_tile(yy, t, bh):
        off = pl.multiple_of(t * 256, 256)
        g = GU[yy, :, pl.ds(off, LANES)].astype(f32)
        u = GU[yy, :, cut(off + LANES, LANES)].astype(f32)
        s = sigmoid(g)
        GU[yy, :, pl.ds(off, LANES)] = (bh * u * s * (1.0 + g * (1.0 - s))).astype(bf16)
        GU[yy, :, cut(off + LANES, LANES)] = (bh * g * s).astype(bf16)

    pairs = ff // 256

    def back_pair(i):
        yy, t = i // pairs, lax.rem(i, pairs)
        bh = dot_nn(BF[...], weight(yy, p.d_at + pl.multiple_of(t * 256, 256), 256))
        back_tile(yy, 2 * t, bh[:, 0:LANES])
        back_tile(yy, 2 * t + 1, bh[:, LANES:256])

    def back_last(yy):
        bh = dot_nn(BF[...], weight(yy, p.d_at + pairs * 256, LANES))
        back_tile(yy, jnp.int32(2 * pairs), bh)

    loop(2 * pairs, back_pair)
    if ff % 256:
        loop(2, back_last)

    T[...] = jnp.transpose(BF[...])

    def grad_down_pair(i):
        yy, off = i // pairs, pl.multiple_of(lax.rem(i, pairs) * 256, 256)
        put_weight(yy, p.d_at + off, 256, dot_nn(T[...], HID[yy, :, pl.ds(off, 256)]))

    def grad_down_last(yy):
        put_weight(yy, p.d_at + pairs * 256, LANES, dot_nn(T[...], HID[yy, :, pl.ds(pairs * 256, LANES)]))

    loop(2 * pairs, grad_down_pair)
    if ff % 256:
        loop(2, grad_down_last)

    n_d = len(p.d_cuts)
    n_gu = n_d + len(p.gu_cuts)
    pump(n_d, 2)

    def back_normed(zz):
        cols = pl.ds(pl.multiple_of(zz * (width // 4), width // 4), width // 4)
        acc = dot_nt(GU[0, :, 0:ff], weight(0, p.gu_at, ff, zz))
        acc = acc + dot_nt(GU[0, :, ff : 2 * ff], weight(0, p.gu_at + ff, ff, zz))
        acc = acc + dot_nt(GU[1, :, 0:ff], weight(1, p.gu_at, ff, zz))
        bff[:, cols] = acc + dot_nt(GU[1, :, ff : 2 * ff], weight(1, p.gu_at + ff, ff, zz))

    loop(4, back_normed)
    pump(n_d, 4)
    T[...] = jnp.transpose(nf[...])

    def grad_gate_up(lo, hi):
        def run(i):
            yy, off = i // (hi - lo), pl.multiple_of((lax.rem(i, hi - lo) + lo) * 256, 256)
            put_weight(yy, p.gu_at + off, 256, dot_nn(T[...], GU[yy, :, pl.ds(off, 256)]))

        loop(2 * (hi - lo), run)

    grad_gate_up(0, 4)
    pump(n_d + 2, 5)
    grad_gate_up(4, 2 * ff // 256)
    pump(n_gu, 6)

    def mid_back(blk):
        m = mid[blk, :]
        scale = rms(m)
        e = bff[blk, :]
        bm = TB[blk, :].astype(f32) + norm_grad(m, scale, gains[2:3, :], e)
        dgains[2:3, :] += jnp.sum(m * scale * e, axis=0, keepdims=True)
        b = ba[blk, :]
        scale_b = rms(b)
        BF[blk, :] = norm_grad(b, scale_b, gains[1:2, :], bm).astype(bf16)
        dgains[1:2, :] += jnp.sum(b * scale_b * bm, axis=0, keepdims=True)
        mid[blk, :] = bm

    by_rows(mid_back)
    load_again = pltpu.make_async_copy(tok_hbm, TB, loc.at[0])
    load_again.start()
    pump(n_gu, 7)

    per_o = hc // 256

    def back_att(i):
        yy, off = i // per_o, pl.multiple_of(lax.rem(i, per_o) * 256, 256)
        nf[:, cut(yy * hc + off, 256)] = dot_nn(BF[...], weight(yy, p.o_at + off, 256)).astype(bf16)

    loop(2 * per_o, back_att)
    T[...] = jnp.transpose(BF[...])

    def grad_out_tile(i):
        yy, off = i // per_o, pl.multiple_of(lax.rem(i, per_o) * 256, 256)
        put_weight(yy, p.o_at + off, 256, dot_nn(T[...], att[:, cut(yy * hc + off, 256)]))

    loop(2 * per_o, grad_out_tile)
    pump(n_gu + 1, 8)

    stat_b[...] = jnp.zeros_like(stat_b)
    for h in range(p.heads):
        cols = slice(h * HEAD_DIM, (h + 1) * HEAD_DIM)
        inner = jnp.sum(nf[:, cols].astype(f32) * att[:, cols].astype(f32), axis=-1, keepdims=True)
        stat_b[...] = jnp.where(lane == h, inner, stat_b[...])
    log_rows = jnp.transpose(stat_a[...])[0 : p.heads, :]
    inner_rows = jnp.transpose(stat_b[...])[0 : p.heads, :]
    gains[8 : 8 + p.heads, 0:rows] = log_rows
    gains[8 : 8 + p.heads, rows : 2 * rows] = inner_rows
    build_mask(1)

    def attend_grad(h, both):
        yy, k_at, v_at, q_at = head_at(h)
        q = KVQ[yy, :, q_at]
        do = nf[:, pl.ds(pl.multiple_of(h * HEAD_DIM, HEAD_DIM), HEAD_DIM)]
        log_row = gains[pl.ds(8 + h, 1), 0:rows]
        inner_row = gains[pl.ds(8 + h, 1), rows : 2 * rows]

        def side(ref, place, hide):
            k, v = ref[yy, :, k_at], ref[yy, :, v_at]
            s = dot_nt(k, q) * log2_scale
            if hide:
                s = s + MK[...]
            prob = jnp.exp2(s - log_row)
            dv = dot_nn(prob.astype(bf16), do)
            ds = (prob * (dot_nt(v, do) - inner_row) * attn_scale).astype(bf16)
            dk = dot_nn(ds, q)
            dq = dot_tn(ds, k)
            ref[yy, :, v_at] = dv.astype(bf16)
            ref[yy, :, k_at] = rotated(dk, place, -1.0).astype(bf16)
            return dq

        dq = side(KVQ, own_place, True)
        if both:
            dq = dq + side(KVp, old_place, False)
        KVQ[yy, :, q_at] = rotated(dq, own_place, -1.0).astype(bf16)

    def grad_heads(lo, hi):
        @pl.when(first)
        def _():
            loop(hi - lo, lambda h: attend_grad(h + lo, False))

        @pl.when(second)
        def _():
            loop(hi - lo, lambda h: attend_grad(h + lo, True))

    half_heads = p.heads // 2
    grad_heads(0, half_heads)
    pump(n_gu + 1, 10)
    grad_heads(half_heads, p.heads)
    pump(n_gu + 1, 11)
    put_out.wait()

    back_send = remote(LO, KVp.at[0, :, pl.ds(0, width)], extra_s.at[1], extra_r.at[1], y_peer)

    @pl.when(second)
    def _():
        def old_back(zz):
            cols = pl.ds(pl.multiple_of(zz * (width // 4), width // 4), width // 4)
            LO[:, cols] = (
                dot_nt(KVp[0], weight(0, p.k_at, 2 * hc, zz)) + dot_nt(KVp[1], weight(1, p.k_at, 2 * hc, zz))
            ).astype(bf16)

        loop(4, old_back)
        back_send.start()

    def own_back(zz):
        cols = pl.ds(pl.multiple_of(zz * (width // 4), width // 4), width // 4)
        bff[:, cols] = dot_nt(KVQ[0], weight(0, p.k_at, p.kvq, zz)) + dot_nt(KVQ[1], weight(1, p.k_at, p.kvq, zz))

    loop(4, own_back)
    pump(n_gu + 1, 12)
    T[...] = jnp.transpose(xo[...])
    tiles = p.kvq // 256

    def grad_kvq(i):
        yy, off = i // tiles, pl.multiple_of(lax.rem(i, tiles) * 256, 256)
        put_weight(yy, p.k_at + off, 256, dot_nn(T[...], KVQ[yy, :, pl.ds(off, 256)]))

    loop(2 * tiles, grad_kvq)

    @pl.when(second)
    def _():
        T[...] = jnp.transpose(xp[...])
        old_tiles = 2 * hc // 256

        def grad_old(i):
            yy, off = i // old_tiles, pl.multiple_of(lax.rem(i, old_tiles) * 256, 256)
            put_weight(
                yy, p.k_at + off, 256,
                weight(yy, p.k_at + off, 256).astype(f32) + dot_nn(T[...], KVp[yy, :, pl.ds(off, 256)]),
            )

        loop(2 * old_tiles, grad_old)

    pump(n_reduce - 1, 13)
    load_again.wait()

    @pl.when(first)
    def _():
        back_send.wait_recv()

        def join(blk):
            bff[blk, :] += KVp[0, blk, pl.ds(0, width)].astype(f32)

        by_rows(join)

    def in_back(blk):
        t = TB[blk, :].astype(f32)
        scale = rms(t)
        e = bff[blk, :]
        mid[blk, :] = mid[blk, :] + norm_grad(t, scale, gains[0:1, :], e)
        dgains[0:1, :] += jnp.sum(t * scale * e, axis=0, keepdims=True)

    by_rows(in_back)
    put_ig = pltpu.make_async_copy(mid, ig_hbm, loc.at[0])
    put_ig.start()

    gain_cols = jnp.transpose(jnp.concatenate([dgains[...], jnp.zeros((LANES - 8, width), f32)], axis=0))
    put_weight(0, 0, LANES, gain_cols)
    put_weight(1, 0, LANES, gain_cols)
    pump(n_reduce, len(events))
    put_ig.wait()
    for j in (n_reduce - 2, n_reduce - 1):
        put_sum(j).wait()

    for j in range(n_reduce):
        for m in range(8):
            rs(j, m).wait_send()

    @pl.when(first)
    def _():
        tok_send.wait_send()

    @pl.when(second)
    def _():
        back_send.wait_send()


def pack_rows(plan, weights, gain_shards):
    query, key, value, out, gate, up, down = weights
    shard_rows = plan.shard_rows
    columns = jnp.stack(gain_shards, axis=1)
    columns = jnp.pad(columns, ((0, 0), (0, LANES - columns.shape[1])))
    turns = jnp.stack(
        [gate.reshape(shard_rows, -1, LANES), up.reshape(shard_rows, -1, LANES)], axis=2
    ).reshape(shard_rows, -1)
    return jnp.concatenate([columns, key, value, query, out.T, turns, down.T], axis=1)


def unpack_rows(plan, total):
    hc, ff = plan.head_cols, plan.ff_cols

    def piece(at, size):
        return total[:, at : at + size]

    turns = piece(plan.gu_at, 2 * ff).reshape(plan.shard_rows, -1, 2, LANES)
    return (
        piece(plan.q_at, hc),
        piece(plan.k_at, hc),
        piece(plan.v_at, hc),
        piece(plan.o_at, hc).T,
        turns[:, :, 0].reshape(plan.shard_rows, ff),
        turns[:, :, 1].reshape(plan.shard_rows, ff),
        piece(plan.d_at, ff).T,
        total[:, 0],
        total[:, 1],
        total[:, 2],
        total[:, 3],
    )


def fused_on_device(
    tokens,
    query_weight,
    key_weight,
    value_weight,
    out_weight,
    gate_weight,
    up_weight,
    down_weight,
    gain_attn_in,
    gain_attn_out,
    gain_ff_in,
    gain_ff_out,
    piece_starts,
    out_grad,
):
    rows, width = tokens.shape
    plan = Plan(rows, width, query_weight.shape[1], gate_weight.shape[1], query_weight.shape[0])
    shard = pack_rows(
        plan,
        (query_weight, key_weight, value_weight, out_weight, gate_weight, up_weight, down_weight),
        (gain_attn_in, gain_attn_out, gain_ff_in, gain_ff_out),
    )
    cosine, sine = rope_at(jnp.arange(2 * rows, dtype=jnp.int32))
    cosine, sine = cosine[:, 0], sine[:, 0]
    cos_table = jnp.concatenate([cosine, cosine], axis=1)
    sin_table = jnp.concatenate([-sine, sine], axis=1)
    hc, ff, sr = plan.head_cols, plan.ff_cols, plan.shard_rows
    anywhere = pl.BlockSpec(memory_space=pl.ANY)
    in_vmem = pl.BlockSpec(memory_space=pltpu.VMEM)
    n_gather, n_reduce = len(plan.gather), len(plan.reduce)
    scratch = [
        pltpu.VMEM((2, 4, 2, 2, sr, plan.cols), bf16),
        pltpu.VMEM((2, rows, 3 * hc), bf16),
        pltpu.VMEM((2, rows, 2 * hc), bf16),
        pltpu.VMEM((rows, width), bf16),
        pltpu.VMEM((rows, width), bf16),
        pltpu.VMEM((width, rows), bf16),
        pltpu.VMEM((rows, 2 * hc), bf16),
        pltpu.VMEM((rows, width), f32),
        pltpu.VMEM((rows, width), f32),
        pltpu.VMEM((rows, width), f32),
        pltpu.VMEM((rows, width), bf16),
        pltpu.VMEM((2, rows, 2 * ff), bf16),
        pltpu.VMEM((2, rows, ff), bf16),
        pltpu.VMEM((rows, width), bf16),
        pltpu.VMEM((rows, width), bf16),
        pltpu.VMEM((rows, width), bf16),
        pltpu.VMEM((rows, rows), f32),
        pltpu.VMEM((8 + plan.heads, max(width, 2 * rows)), f32),
        pltpu.VMEM((8, width), f32),
        pltpu.VMEM((rows, LANES), f32),
        pltpu.VMEM((rows, LANES), f32),
        pltpu.VMEM((2, 2, 4, 2, sr, 512), bf16),
        pltpu.VMEM((2, 2, 2, sr, 512), bf16),
        pltpu.VMEM((2, 2, 2, sr, 512), bf16),
        pltpu.VMEM((2, 2, sr, 512), bf16),
        pltpu.VMEM((2, 2, sr, 512), bf16),
        pltpu.VMEM((2, 3, sr, 512), bf16),
        pltpu.VMEM((2, sr, 512), f32),
        pltpu.SemaphoreType.DMA((n_gather, 8)),
        pltpu.SemaphoreType.DMA((n_gather, 8)),
        pltpu.SemaphoreType.DMA((n_reduce, 8)),
        pltpu.SemaphoreType.DMA((n_reduce, 8)),
        pltpu.SemaphoreType.DMA((4,)),
        pltpu.SemaphoreType.DMA((2,)),
        pltpu.SemaphoreType.DMA((2,)),
        pltpu.SemaphoreType.REGULAR((8,)),
    ]
    out, input_grad, total = pl.pallas_call(
        functools.partial(fused_layer, plan),
        out_shape=(
            jax.ShapeDtypeStruct((rows, width), bf16),
            jax.ShapeDtypeStruct((rows, width), f32),
            jax.ShapeDtypeStruct((sr, plan.cols), f32),
        ),
        in_specs=[anywhere, anywhere, anywhere, pl.BlockSpec(memory_space=pltpu.SMEM), in_vmem, in_vmem],
        out_specs=(anywhere, anywhere, anywhere),
        scratch_shapes=scratch,
        compiler_params=pltpu.CompilerParams(
            collective_id=0, has_side_effects=True, vmem_limit_bytes=67043328
        ),
        name="fused_layer",
    )(shard, tokens, out_grad, piece_starts, cos_table, sin_table)
    return (out, input_grad) + unpack_rows(plan, total)


def fits_fused(mesh, tokens, query_weight, gate_weight, piece_starts):
    dp, tensor = mesh.shape["dp"], mesh.shape["tensor"]
    sequences, pieces = piece_starts.shape
    return (
        (dp, tensor, pieces, sequences) == (16, 2, 2, dp)
        and tokens.shape[0] % (dp * tensor * 256) == 0
        and tokens.shape[1] == query_weight.shape[1]
        and tokens.shape[1] % (dp * 16) == 0
        and query_weight.shape[1] % (tensor * 256) == 0
        and gate_weight.shape[1] % (tensor * LANES) == 0
    )


def solution(mesh):
    placed = (
        P(("dp", "tensor"), None),
        P("dp", "tensor"),
        P("dp", "tensor"),
        P("dp", "tensor"),
        P("tensor", "dp"),
        P("dp", "tensor"),
        P("dp", "tensor"),
        P("tensor", "dp"),
        P("dp"),
        P("dp"),
        P("dp"),
        P("dp"),
        P("dp", None),
        P(("dp", "tensor"), None),
    )
    def step(*arrays):
        fused = fits_fused(mesh, arrays[0], arrays[1], arrays[5], arrays[12])
        return place(fused_on_device if fused else on_device)(*arrays)

    def place(body):
        return jax.shard_map(
            body,
            mesh=mesh,
            in_specs=placed,
            out_specs=(
                P(("dp", "tensor"), None),
                P(("dp", "tensor"), None),
                P("dp", "tensor"),
                P("dp", "tensor"),
                P("dp", "tensor"),
                P("tensor", "dp"),
                P("dp", "tensor"),
                P("dp", "tensor"),
                P("tensor", "dp"),
                P("dp"),
                P("dp"),
                P("dp"),
                P("dp"),
            ),
            check_vma=False,
        )

    return step
```

```python
import functools
import math

import jax
import jax.numpy as jnp
import numpy as np
from jax import lax
from jax.experimental import pallas as pl
from jax.experimental.pallas import tpu as pltpu
from jax.sharding import PartitionSpec as P

HEAD_DIM = 128
PIECE = 256


norm_eps = 1e-06
rope_base = 50000.0
masked = -1e30


def rms_scale(values):
    return lax.rsqrt(jnp.mean(values * values, axis=-1, keepdims=True) + norm_eps)


def norm_back(values, scale, gain, incoming):
    weighted = gain * incoming
    row_inner = jnp.mean(values * weighted, axis=-1, keepdims=True)
    backward = scale * weighted - values * (scale * scale * scale) * row_inner
    return (backward, jnp.sum(values * scale * incoming, axis=0))


def rope_at(places):
    half_dim = HEAD_DIM // 2
    inverse = rope_base ** (-(jnp.arange(half_dim, dtype=jnp.float32) * 2.0) / HEAD_DIM)
    angles = places.astype(jnp.float32)[:, None, None] * inverse[None, None, :]
    return (jnp.cos(angles), jnp.sin(angles))


def rope_tables(count, length):
    return rope_at(jnp.arange(count, dtype=jnp.int32) % length)


def rotate(values, cosine, sine):
    half_dim = values.shape[-1] // 2
    lower_half = values[..., :half_dim]
    upper_half = values[..., half_dim:]
    return jnp.concatenate(
        [lower_half * cosine - upper_half * sine, upper_half * cosine + lower_half * sine], axis=-1
    )


def unrotate(grads, cosine, sine):
    half_dim = grads.shape[-1] // 2
    lower_half = grads[..., :half_dim]
    upper_half = grads[..., half_dim:]
    return jnp.concatenate(
        [lower_half * cosine + upper_half * sine, upper_half * cosine - lower_half * sine], axis=-1
    )


def piece_ids(starts, length):
    places = jnp.arange(length, dtype=jnp.int32)
    inside = (places[None, :, None] >= starts[:, None, :]) & (
        places[None, :, None] < starts[:, None, :] + PIECE
    )
    labels = jnp.arange(1, starts.shape[1] + 1, dtype=jnp.int32)
    return jnp.sum(jnp.where(inside, labels, 0), axis=2)


def visible(piece_id, offset, count):
    length = piece_id.shape[0]
    query_place = offset + jnp.arange(count, dtype=jnp.int32)
    key_place = jnp.arange(length, dtype=jnp.int32)
    query_ids = piece_id[offset : offset + count]
    return (key_place[None, :] <= query_place[:, None]) | (
        query_ids[:, None] == piece_id[None, :]
    ) & (query_ids[:, None] > 0)


def block_scores(queries, key_vecs, piece_id, offset, count):
    attn_scale = 1.0 / math.sqrt(queries.shape[-1])
    q_block = queries[offset : offset + count]
    scores = (
        jnp.einsum("qhd,khd->hqk", q_block, key_vecs, preferred_element_type=jnp.float32)
        * attn_scale
    )
    return (jnp.where(visible(piece_id, offset, count)[None], scores, masked), q_block)


def attend_one(seq_items):
    queries, key_vecs, values, piece_id = seq_items
    length = queries.shape[0]
    block_rows = min(512, length)
    outputs = []
    log_totals = []
    for offset in range(0, length, block_rows):
        logits, q_block = block_scores(queries, key_vecs, piece_id, offset, block_rows)
        row_max = jnp.max(logits, axis=-1, keepdims=True)
        log_total = row_max + jnp.log(jnp.sum(jnp.exp(logits - row_max), axis=-1, keepdims=True))
        probs = jnp.exp(logits - log_total).astype(jnp.bfloat16)
        mixed = jnp.einsum("hqk,khd->qhd", probs, values, preferred_element_type=jnp.float32)
        outputs.append(mixed.astype(jnp.bfloat16))
        log_totals.append(log_total)
    return (jnp.concatenate(outputs, axis=0), jnp.concatenate(log_totals, axis=1))


def attend_back(seq_items):
    queries, key_vecs, values, piece_id, log_totals, grad_mixed = seq_items
    length = queries.shape[0]
    block_rows = min(512, length)
    attn_scale = 1.0 / math.sqrt(queries.shape[-1])
    grad_keys = jnp.zeros(key_vecs.shape, jnp.float32)
    grad_values = jnp.zeros(values.shape, jnp.float32)
    grad_queries = []
    for offset in range(0, length, block_rows):
        logits, q_block = block_scores(queries, key_vecs, piece_id, offset, block_rows)
        probs = jnp.exp(logits - log_totals[:, offset : offset + block_rows])
        grad_block = grad_mixed[offset : offset + block_rows]
        grad_values = grad_values + jnp.einsum(
            "hqk,qhd->khd",
            probs.astype(jnp.bfloat16),
            grad_block,
            preferred_element_type=jnp.float32,
        )
        grad_probs = jnp.einsum(
            "qhd,khd->hqk", grad_block, values, preferred_element_type=jnp.float32
        )
        row_inner = jnp.sum(probs * grad_probs, axis=-1, keepdims=True)
        grad_scores = (probs * (grad_probs - row_inner) * attn_scale).astype(jnp.bfloat16)
        grad_queries.append(
            jnp.einsum("hqk,khd->qhd", grad_scores, key_vecs, preferred_element_type=jnp.float32)
        )
        grad_keys = grad_keys + jnp.einsum(
            "hqk,qhd->khd", grad_scores, q_block, preferred_element_type=jnp.float32
        )
    return (jnp.concatenate(grad_queries, axis=0), grad_keys, grad_values)


def times_trans(left, right):
    return lax.dot_general(
        left, right, (((1,), (1,)), ((), ())), preferred_element_type=jnp.float32
    )


def trans_times(left, right):
    return lax.dot_general(
        left, right, (((0,), (0,)), ((), ())), preferred_element_type=jnp.float32
    )


def fetch_weights(shards):
    gathered = (
        lax.all_gather(shards[0], "dp", axis=0, tiled=True),
        lax.all_gather(shards[1], "dp", axis=0, tiled=True),
        lax.all_gather(shards[2], "dp", axis=0, tiled=True),
        lax.all_gather(shards[3], "dp", axis=1, tiled=True),
        lax.all_gather(shards[4], "dp", axis=0, tiled=True),
        lax.all_gather(shards[5], "dp", axis=0, tiled=True),
        lax.all_gather(shards[6], "dp", axis=1, tiled=True),
        lax.all_gather(shards[7], "dp", axis=1, tiled=True),
    )
    return gathered


def gather_rows(normed):
    return lax.all_gather(normed, "tensor", axis=0, tiled=True)


def sum_rows(sum_terms):
    return lax.psum_scatter(sum_terms, "tensor", scatter_dimension=0, tiled=True)


def gather_grads(grad_terms):
    return lax.all_gather(grad_terms, "tensor", axis=0, tiled=True)


def sum_grads(grad_terms):
    return lax.psum_scatter(
        grad_terms.astype(jnp.bfloat16), "tensor", scatter_dimension=0, tiled=True
    ).astype(jnp.float32)


def by_sequence(values, seq_count):
    return values.reshape(seq_count, values.shape[0] // seq_count, values.shape[1], values.shape[2])


def attention_part(normed, gathered, cosine, sine, piece_id):
    whole_rows = gather_rows(normed)
    group_rows = whole_rows.shape[0]
    seq_count = piece_id.shape[0]

    def project(weight):
        return jnp.dot(whole_rows, weight, preferred_element_type=jnp.float32).reshape(
            group_rows, -1, HEAD_DIM
        )

    queries = rotate(project(gathered[0]), cosine, sine).astype(jnp.bfloat16)
    key_vecs = rotate(project(gathered[1]), cosine, sine).astype(jnp.bfloat16)
    values = project(gathered[2]).astype(jnp.bfloat16)
    outputs, log_totals = lax.map(
        attend_one,
        (
            by_sequence(queries, seq_count),
            by_sequence(key_vecs, seq_count),
            by_sequence(values, seq_count),
            piece_id,
        ),
    )
    return (whole_rows, queries, key_vecs, values, outputs.reshape(group_rows, -1), log_totals)


def feed_part(normed, gathered):
    whole_rows = gather_rows(normed)
    gate_pre = jnp.dot(whole_rows, gathered[4], preferred_element_type=jnp.float32)
    up_pre = jnp.dot(whole_rows, gathered[5], preferred_element_type=jnp.float32)
    hidden = (jax.nn.silu(gate_pre) * up_pre).astype(jnp.bfloat16)
    return (whole_rows, gate_pre, up_pre, hidden)


def on_device(
    tokens,
    query_weight,
    key_weight,
    value_weight,
    out_weight,
    gate_weight,
    up_weight,
    down_weight,
    gain_attn_in,
    gain_attn_out,
    gain_ff_in,
    gain_ff_out,
    piece_starts,
    out_grad,
):
    shards = (
        query_weight,
        key_weight,
        value_weight,
        out_weight,
        gate_weight,
        up_weight,
        down_weight,
        jnp.stack([gain_attn_in, gain_attn_out, gain_ff_in, gain_ff_out]),
    )
    gathered = fetch_weights(shards)
    gain_rows = gathered[7].astype(jnp.float32)
    tok_rows = tokens.astype(jnp.float32)
    seq_count = piece_starts.shape[0]
    own_rows = tokens.shape[0]
    group_rows = own_rows * lax.axis_size("tensor")
    length = group_rows // seq_count
    piece_id = piece_ids(piece_starts, length)
    incoming = out_grad.astype(jnp.float32)
    scale_in = rms_scale(tok_rows)
    normed_in = (tok_rows * scale_in * gain_rows[0]).astype(jnp.bfloat16)
    cosine, sine = rope_tables(group_rows, length)
    attn_parts = attention_part(normed_in, gathered, cosine, sine, piece_id)
    branch_attn = sum_rows(jnp.dot(attn_parts[4], gathered[3], preferred_element_type=jnp.float32))
    scale_attn = rms_scale(branch_attn)
    mid_rows = tok_rows + branch_attn * scale_attn * gain_rows[1]
    scale_mid = rms_scale(mid_rows)
    normed_ff = (mid_rows * scale_mid * gain_rows[2]).astype(jnp.bfloat16)
    feed_parts = feed_part(normed_ff, gathered)
    branch_ff = sum_rows(jnp.dot(feed_parts[3], gathered[6], preferred_element_type=jnp.float32))
    scale_ff = rms_scale(branch_ff)
    result = (mid_rows + branch_ff * scale_ff * gain_rows[3]).astype(jnp.bfloat16)
    gathered = fetch_weights(shards)
    feed_parts = feed_part(normed_ff, gathered)
    whole_ff, gate_pre, up_pre, hidden = feed_parts
    back_ff, gain_grad_ff_out = norm_back(branch_ff, scale_ff, gain_rows[3], incoming)
    wide_back_ff = gather_grads(back_ff.astype(jnp.bfloat16))
    grad_down = trans_times(hidden, wide_back_ff)
    back_hidden = times_trans(wide_back_ff, gathered[6])
    sigmoid_gate = jax.nn.sigmoid(gate_pre)
    back_gate = (
        back_hidden * up_pre * sigmoid_gate * (1.0 + gate_pre * (1.0 - sigmoid_gate))
    ).astype(jnp.bfloat16)
    back_up = (back_hidden * gate_pre * sigmoid_gate).astype(jnp.bfloat16)
    grad_gate = trans_times(whole_ff, back_gate)
    grad_up = trans_times(whole_ff, back_up)
    back_normed_ff = sum_grads(
        times_trans(back_gate, gathered[4]) + times_trans(back_up, gathered[5])
    )
    back_from_ff, gain_grad_ff_in = norm_back(mid_rows, scale_mid, gain_rows[2], back_normed_ff)
    back_mid = incoming + back_from_ff
    back_attn, gain_grad_attn_out = norm_back(branch_attn, scale_attn, gain_rows[1], back_mid)
    wide_back_attn = gather_grads(back_attn.astype(jnp.bfloat16))
    attn_parts = attention_part(normed_in, gathered, cosine, sine, piece_id)
    whole_in, queries, key_vecs, values, attended, log_totals = attn_parts
    grad_out = trans_times(attended, wide_back_attn)
    back_attended = times_trans(wide_back_attn, gathered[3]).astype(jnp.bfloat16)
    back_queries, back_keys, back_values = lax.map(
        attend_back,
        (
            by_sequence(queries, seq_count),
            by_sequence(key_vecs, seq_count),
            by_sequence(values, seq_count),
            piece_id,
            log_totals,
            by_sequence(back_attended.reshape(group_rows, -1, HEAD_DIM), seq_count),
        ),
    )
    back_queries = (
        unrotate(back_queries.reshape(group_rows, -1, HEAD_DIM), cosine, sine)
        .reshape(group_rows, -1)
        .astype(jnp.bfloat16)
    )
    back_keys = (
        unrotate(back_keys.reshape(group_rows, -1, HEAD_DIM), cosine, sine)
        .reshape(group_rows, -1)
        .astype(jnp.bfloat16)
    )
    back_values = back_values.reshape(group_rows, -1).astype(jnp.bfloat16)
    grad_query = trans_times(whole_in, back_queries)
    grad_key = trans_times(whole_in, back_keys)
    grad_value = trans_times(whole_in, back_values)
    back_normed_in = sum_grads(
        times_trans(back_queries, gathered[0])
        + times_trans(back_keys, gathered[1])
        + times_trans(back_values, gathered[2])
    )
    back_from_in, gain_grad_attn_in = norm_back(tok_rows, scale_in, gain_rows[0], back_normed_in)
    input_grad = back_mid + back_from_in
    weight_terms = (grad_query, grad_key, grad_value, grad_out, grad_gate, grad_up, grad_down)
    gain_grads = lax.psum(
        jnp.stack([gain_grad_attn_in, gain_grad_attn_out, gain_grad_ff_in, gain_grad_ff_out]),
        "tensor",
    )
    grad_sums = (
        lax.psum_scatter(
            weight_terms[0].astype(jnp.bfloat16), "dp", scatter_dimension=0, tiled=True
        ).astype(jnp.float32),
        lax.psum_scatter(
            weight_terms[1].astype(jnp.bfloat16), "dp", scatter_dimension=0, tiled=True
        ).astype(jnp.float32),
        lax.psum_scatter(
            weight_terms[2].astype(jnp.bfloat16), "dp", scatter_dimension=0, tiled=True
        ).astype(jnp.float32),
        lax.psum_scatter(
            weight_terms[3].astype(jnp.bfloat16), "dp", scatter_dimension=1, tiled=True
        ).astype(jnp.float32),
        lax.psum_scatter(
            weight_terms[4].astype(jnp.bfloat16), "dp", scatter_dimension=0, tiled=True
        ).astype(jnp.float32),
        lax.psum_scatter(
            weight_terms[5].astype(jnp.bfloat16), "dp", scatter_dimension=0, tiled=True
        ).astype(jnp.float32),
        lax.psum_scatter(
            weight_terms[6].astype(jnp.bfloat16), "dp", scatter_dimension=1, tiled=True
        ).astype(jnp.float32),
        lax.psum_scatter(
            gain_grads.astype(jnp.bfloat16), "dp", scatter_dimension=1, tiled=True
        ).astype(jnp.float32),
    )
    return (
        result,
        input_grad,
        grad_sums[0],
        grad_sums[1],
        grad_sums[2],
        grad_sums[3],
        grad_sums[4],
        grad_sums[5],
        grad_sums[6],
        grad_sums[7][0],
        grad_sums[7][1],
        grad_sums[7][2],
        grad_sums[7][3],
    )


LANES = 128
HALF = HEAD_DIM // 2
MESH = pl.DeviceIdType.MESH
GATHER_FIRST = (256, 384)
GATHER_DOWN = (384, 256, 512, 256)
REDUCE_DOWN = (512, 512)
REDUCE_LAST = (256, 256)
GATHER_LATE = 2
REDUCE_LATE = 0
LATE_SLOTS = (0, 1, 6, 7, 8)
X_FIRST = (1, 2)
X_FIRST_SUM = (2, 2, 2, 2, 2, 2, 2, 2, 1, 1, 1, 1, 1, 1, 1, 1, 1, 1, 1, 1)
PACE = (1, 2, 3, 4, 5, 6, 7, 8, 9, 10, 11, 12, 13)
TOKEN_PIECES = 8
TOKENS_A_STEP = 2
f32 = jnp.float32
bf16 = jnp.bfloat16


class Plan:
    def __init__(self, rows, width, head_cols, ff_cols, shard_rows):
        self.rows = rows
        self.width = width
        self.head_cols = head_cols
        self.ff_cols = ff_cols
        self.shard_rows = shard_rows
        self.heads = 2 * head_cols // HEAD_DIM
        self.k_at = LANES
        self.v_at = self.k_at + head_cols
        self.q_at = self.v_at + head_cols
        self.o_at = self.q_at + head_cols
        self.gu_at = self.o_at + head_cols
        self.d_at = self.gu_at + 2 * ff_cols
        self.cols = self.d_at + ff_cols
        self.kvq = 3 * head_cols

        def cuts(start, total, sizes=()):
            pieces = []
            while total > 0:
                size = min(sizes[len(pieces)] if len(pieces) < len(sizes) else 512, total)
                pieces.append((start, size))
                start, total = start + size, total - size
            return pieces

        gu_cuts = cuts(self.gu_at, 2 * ff_cols)
        self.gather = (
            cuts(0, self.v_at, GATHER_FIRST)
            + [(self.v_at, head_cols), (self.q_at, head_cols), (self.o_at, head_cols)]
            + gu_cuts
            + cuts(self.d_at, ff_cols, GATHER_DOWN)
        )
        self.d_cuts = cuts(self.d_at, ff_cols, REDUCE_DOWN)
        self.gu_cuts = gu_cuts
        self.reduce = (
            self.d_cuts
            + self.gu_cuts
            + [(self.o_at, head_cols), (self.q_at, head_cols), (self.v_at, head_cols)]
            + cuts(self.k_at, head_cols, REDUCE_LAST)
            + [(0, LANES)]
        )
        self.gather_late = set(range(len(self.gather) - GATHER_LATE, len(self.gather)))
        self.reduce_late = set(range(REDUCE_LATE))

    def held(self, at):
        return next(k for k, (start, size) in enumerate(self.gather) if start + size >= at) + 3

    def split(self, k):
        return X_FIRST[k % len(X_FIRST)]

    def split_sum(self, j):
        return X_FIRST_SUM[j % len(X_FIRST_SUM)]


def sigmoid(v):
    return 0.5 * jnp.tanh(0.5 * v) + 0.5


def dot_nn(left, right):
    return lax.dot_general(left, right, (((1,), (0,)), ((), ())), preferred_element_type=f32)


def dot_nt(left, right):
    return lax.dot_general(left, right, (((1,), (1,)), ((), ())), preferred_element_type=f32)


def dot_tn(left, right):
    return lax.dot_general(left, right, (((0,), (0,)), ((), ())), preferred_element_type=f32)


def fused_layer(
    plan,
    k_hbm, v_hbm, q_hbm, g_hbm, u_hbm, o_hbm, d_hbm, gain_shard, tok_hbm, og_hbm, starts_ref, inverse_ref,
    out_hbm, ig_hbm, gr_hbm,
    W, KVQ, KVp, xo, xp, T, att, ba, mid, bff, nf, GU, HID, BF, TB, LO, MK, gains, dgains, stat_a, stat_b, DQ, cos_ref, sin_ref,
    R1, R2A, R2B, R3A, R3B, R4, RQ1, RQ2, RQ3, ST,
    ag_s, ag_r, rs_s, rs_r, loc, pack_sem, extra_s, extra_r, credit,
):
    p = plan
    dp = lax.axis_index("dp")
    y = lax.axis_index("tensor")
    c = lax.rem(dp, 2)
    x = lax.rem(dp // 2, 2)
    z = dp // 4
    rows, width, hc, ff = p.rows, p.width, p.head_cols, p.ff_cols
    first = y == 0
    second = y == 1

    def dev(zz, xx, cc, yy):
        return (zz * 4 + xx * 2 + cc, yy)

    def up(step):
        return lax.rem(z + step, 4)

    core_peer = dev(z, x, 1 - c, y)
    x_peer = dev(z, 1 - x, c, y)
    y_peer = dev(z, x, c, 1 - y)
    z_peers = [dev(up(d), x, c, y) for d in (1, 2, 3)]
    z_sources = [dev(up(4 - d), x, c, y) for d in (1, 2, 3)]

    def remote(src, dst, send, recv, to):
        return pltpu.make_async_remote_copy(
            src_ref=src, dst_ref=dst, send_sem=send, recv_sem=recv, device_id=to, device_id_type=MESH
        )

    def cut(at, size):
        return pl.ds(at if isinstance(at, int) else pl.multiple_of(at, LANES), size)

    def weight(yy, at, size, zz=None):
        if zz is None:
            return W[yy, :, :, :, :, cut(at, size)].reshape(width, size)
        return W[yy, zz, :, :, :, cut(at, size)].reshape(width // 4, size)

    def put_weight(yy, at, size, value):
        W[yy, :, :, :, :, cut(at, size)] = value.astype(bf16).reshape(4, 2, 2, p.shard_rows, size)

    def rms(v):
        return lax.rsqrt(jnp.mean(v * v, axis=-1, keepdims=True) + norm_eps)

    def norm_grad(v, scale, gain, e):
        weighted = gain * e
        inner = jnp.mean(v * weighted, axis=-1, keepdims=True)
        return scale * weighted - v * (scale * scale * scale) * inner

    def by_rows(body, size=64):
        def step(i, carry):
            body(pl.ds(pl.multiple_of(i * size, size), size))
            return carry

        lax.fori_loop(0, rows // size, step, 0)

    def loop(count, body):
        def step(i, carry):
            body(i)
            return carry

        lax.fori_loop(0, count, step, 0)

    own_w = W.at[y, z, x, c]

    def ag(k, m):
        at, size = p.gather[k]
        cols = pl.ds(at, size)
        sem = (ag_s.at[k, m], ag_r.at[k, m])
        if k in p.gather_late:
            half = size // 2 // LANES * LANES
            cols_a, cols_b = pl.ds(at, half), pl.ds(at + half, size - half)
            if m < 3:
                ref = W.at[:, z, :, c, :, cols]
                return remote(ref, ref, *sem, z_peers[m])
            if m == 3:
                return remote(own_w.at[:, cols_a], W.at[y, z, x, c, :, cols_a], *sem, x_peer)
            if m == 4:
                return remote(own_w.at[:, cols_b], W.at[y, z, x, c, :, cols_b], *sem, y_peer)
            if m == 5:
                ref = W.at[y, z, :, c, :, cols_a]
                return remote(ref, ref, *sem, y_peer)
            if m == 6:
                ref = W.at[:, z, x, c, :, cols_b]
                return remote(ref, ref, *sem, x_peer)
        low, high = pl.ds(0, p.split(k)), pl.ds(p.split(k), 4 - p.split(k))
        if m < 3:
            return remote(own_w.at[:, cols], W.at[y, z, x, c, :, cols], *sem, z_peers[m])
        if m == 3:
            ref = W.at[y, low, x, c, :, cols]
            return remote(ref, ref, *sem, x_peer)
        if m == 4:
            ref = W.at[y, high, x, c, :, cols]
            return remote(ref, ref, *sem, y_peer)
        if m == 5:
            ref = W.at[y, low, :, c, :, cols]
            return remote(ref, ref, *sem, y_peer)
        if m == 6:
            ref = W.at[:, high, x, c, :, cols]
            return remote(ref, ref, *sem, x_peer)
        ref = W.at[:, :, :, c, :, cols]
        return remote(ref, ref, *sem, core_peer)

    n_gather = len(p.gather)
    n_early = n_gather - len(p.gather_late)

    def ag_step(s):
        if 0 <= s < n_early:
            for m in (0, 1, 2):
                ag(s, m).wait_recv()
            ag(s, 3).start()
            ag(s, 4).start()
        if 0 <= s - 1 < n_early:
            ag(s - 1, 3).wait_recv()
            ag(s - 1, 5).start()
            ag(s - 1, 4).wait_recv()
            ag(s - 1, 6).start()
        if 0 <= s - 2 < n_early:
            ag(s - 2, 5).wait_recv()
            ag(s - 2, 6).wait_recv()
            ag(s - 2, 7).start()
        if 0 <= s - 3 < n_early:
            ag(s - 3, 7).wait_recv()
        k = s - 2
        if n_early <= k < n_gather:
            for m in (0, 1, 2):
                ag(k, m).wait_recv()
            ag(k, 7).start()
        if n_early <= k - 1 < n_gather:
            ag(k - 1, 7).wait_recv()

    steps = [0]

    def tok_piece(i):
        blk = pl.ds(i * (rows // TOKEN_PIECES), rows // TOKEN_PIECES)
        return remote(tok_hbm.at[blk, :], xp.at[blk, :], extra_s.at[1 + i], extra_r.at[1 + i], y_peer)

    def tok_send(i):
        @pl.when(first)
        def _():
            tok_piece(i).start()

    def ag_until(at, more=0):
        goal = max(p.held(at), steps[0] + more - 1)
        while steps[0] <= goal:
            ag_step(steps[0])
            for i in range(TOKEN_PIECES):
                if i // TOKENS_A_STEP == steps[0]:
                    tok_send(i)
            steps[0] += 1
            if steps[0] == 1:
                ag_late_turn()
            if steps[0] == 5:
                ag_late_z()

    def ag_late_turn():
        for k in sorted(p.gather_late):
            ag(k, 3).wait_recv()
            ag(k, 5).start()
            ag(k, 4).wait_recv()
            ag(k, 6).start()

    def ag_late_z():
        for k in sorted(p.gather_late):
            ag(k, 5).wait_recv()
            ag(k, 6).wait_recv()
            for m in (0, 1, 2):
                ag(k, m).start()

    load_tok = pltpu.make_async_copy(tok_hbm, TB, loc.at[0])
    load_tok.start()
    packing = []
    for src, at, size in (
        (k_hbm, p.k_at, hc), (v_hbm, p.v_at, hc), (q_hbm, p.q_at, hc), (o_hbm, p.o_at, hc), (d_hbm, p.d_at, ff)
    ):
        packing.append((src, own_w.at[:, pl.ds(at, size)]))
    for t in range(ff // LANES):
        for n, src in enumerate((g_hbm, u_hbm)):
            to = own_w.at[:, pl.ds(p.gu_at + (2 * t + n) * LANES, LANES)]
            packing.append((src.at[:, pl.ds(t * LANES, LANES)], to))
    packing = [pltpu.make_async_copy(src, to, pack_sem.at[i]) for i, (src, to) in enumerate(packing)]
    for copy in packing:
        copy.start()
    barrier = pltpu.get_barrier_semaphore()
    for peer in [core_peer, x_peer, y_peer] + z_peers:
        pl.semaphore_signal(barrier, inc=1, device_id=peer, device_id_type=MESH)
    count = gain_shard.shape[0]
    spread = jnp.concatenate([gain_shard[...], jnp.zeros((LANES - count, p.shard_rows), f32)], axis=0)
    W[y, z, x, c, :, pl.ds(0, LANES)] = jnp.transpose(spread).astype(bf16)
    for copy in packing:
        copy.wait()
    pl.semaphore_wait(barrier, 6)

    for k in sorted(p.gather_late):
        ag(k, 3).start()
        ag(k, 4).start()

    for k in range(n_early):
        for m in (0, 1, 2):
            ag(k, m).start()
    load_tok.wait()

    def tables(i):
        blk = pl.ds(pl.multiple_of(i * 64, 64), 64)
        place = (lax.broadcasted_iota(jnp.int32, (64, LANES), 0) + i * 64).astype(f32)
        angle = place * inverse_ref[...]
        cos_ref[blk, :] = jnp.cos(angle)
        turned = jnp.sin(angle)
        sin_ref[blk, :] = jnp.where(lax.broadcasted_iota(jnp.int32, (64, LANES), 1) < HALF, -turned, turned)

    loop(2 * rows // 64, tables)

    start = starts_ref[0, y] - y * rows

    def build_mask(query_dim):
        def body(blk):
            shape = (64, rows)
            r = lax.broadcasted_iota(jnp.int32, shape, 0) + blk.start
            s = lax.broadcasted_iota(jnp.int32, shape, 1)
            q_pos, k_pos = (r, s) if query_dim == 0 else (s, r)
            inside = (r >= start) & (r < start + PIECE) & (s >= start) & (s < start + PIECE)
            MK[blk, :] = jnp.where((k_pos <= q_pos) | inside, 0.0, masked)

        by_rows(body)

    build_mask(0)
    dgains[...] = jnp.zeros_like(dgains)

    ag_until(LANES)
    gains[0:8, 0:width] = jnp.transpose(weight(0, 0, LANES).astype(f32))[0:8, :]

    def norm_in(src, dst):
        def body(blk):
            t = src[blk, :].astype(f32)
            dst[blk, :] = (t * rms(t) * gains[0:1, :]).astype(bf16)

        by_rows(body)

    norm_in(TB, xo)

    def rotated(u, place, sign):
        return u * cos_ref[place, :] + sign * (pltpu.roll(u, HALF, 1) * sin_ref[place, :])

    def project(src, dst, at, place, turn):
        def run(yy, off):
            r = dot_nn(src[...], weight(yy, LANES + off, 256))
            for hh in range(2):
                u = r[:, hh * HEAD_DIM : (hh + 1) * HEAD_DIM]
                if turn:
                    u = rotated(u, place, 1.0)
                dst[yy, :, cut(off + hh * HEAD_DIM, HEAD_DIM)] = u.astype(bf16)

        per = hc // 256
        loop(2 * per, lambda i: run(i // per, pl.multiple_of(at + lax.rem(i, per) * 256, 256)))

    own_place = pl.ds(pl.multiple_of(y * rows, rows), rows)
    old_place = pl.ds(0, rows)
    ag_until(p.v_at)
    project(xo, KVQ, 0, own_place, True)
    ag_until(p.q_at)
    project(xo, KVQ, hc, own_place, False)

    @pl.when(second)
    def _():
        for i in range(TOKEN_PIECES):
            tok_piece(i).wait_recv()
        norm_in(xp, xp)

    ag_until(p.o_at)
    project(xo, KVQ, 2 * hc, own_place, True)

    @pl.when(second)
    def _():
        project(xp, KVp, 0, old_place, True)

    ag_until(p.gu_at)

    @pl.when(second)
    def _():
        project(xp, KVp, hc, old_place, False)

    ag_until(0, 1)

    per_y = hc // HEAD_DIM
    attn_scale = 1.0 / math.sqrt(HEAD_DIM)
    log2_scale = attn_scale * math.log2(math.e)
    lane = lax.broadcasted_iota(jnp.int32, (1, LANES), 1)

    def head_at(h):
        yy = h // per_y
        off = pl.multiple_of(lax.rem(h, per_y) * HEAD_DIM, HEAD_DIM)
        return yy, cut(off, HEAD_DIM), cut(off + hc, HEAD_DIM), cut(off + 2 * hc, HEAD_DIM)

    def attend(i, both):
        h = i // 2
        blk = pl.ds(pl.multiple_of(lax.rem(i, 2) * (rows // 2), rows // 2), rows // 2)
        yy, k_at, v_at, q_at = head_at(h)
        q = KVQ[yy, blk, q_at]
        s = dot_nt(q, KVQ[yy, :, k_at]) * log2_scale + MK[blk, :]
        top = jnp.max(s, axis=-1, keepdims=True)
        if both:
            s_old = dot_nt(q, KVp[yy, :, k_at]) * log2_scale
            top = jnp.maximum(top, jnp.max(s_old, axis=-1, keepdims=True))
        e = jnp.exp2(s - top)
        total = jnp.sum(e, axis=-1, keepdims=True)
        if both:
            e_old = jnp.exp2(s_old - top)
            total = total + jnp.sum(e_old, axis=-1, keepdims=True)
        inv = 1.0 / total
        o = dot_nn((e * inv).astype(bf16), KVQ[yy, :, v_at])
        if both:
            o = o + dot_nn((e_old * inv).astype(bf16), KVp[yy, :, v_at])
        att[blk, pl.ds(pl.multiple_of(h * HEAD_DIM, HEAD_DIM), HEAD_DIM)] = o.astype(bf16)
        stat = top + jnp.log2(total)
        stat_a[blk, :] = jnp.where(lane == h, stat, stat_a[blk, :])

    def attend_heads(lo, hi):
        @pl.when(first)
        def _():
            loop(2 * (hi - lo), lambda i: attend(i + 2 * lo, False))

        @pl.when(second)
        def _():
            loop(2 * (hi - lo), lambda i: attend(i + 2 * lo, True))

    stat_a[...] = jnp.zeros_like(stat_a)
    for h in range(0, p.heads, 2):
        attend_heads(h, h + 2)
        ag_until(0, 1)


    def o_proj(zz):
        cols = pl.ds(pl.multiple_of(zz * (width // 4), width // 4), width // 4)
        ba[:, cols] = dot_nt(att[:, 0:hc], weight(0, p.o_at, hc, zz)) + dot_nt(
            att[:, hc : 2 * hc], weight(1, p.o_at, hc, zz)
        )

    loop(4, o_proj)

    def mid_rows(blk):
        b = ba[blk, :]
        m = TB[blk, :].astype(f32) + b * rms(b) * gains[1:2, :]
        mid[blk, :] = m
        nf[blk, :] = (m * rms(m) * gains[2:3, :]).astype(bf16)

    by_rows(mid_rows)
    load_og = pltpu.make_async_copy(og_hbm, TB, loc.at[0])
    load_og.start()

    def gate_up(lo, hi):
        def run(i):
            yy = i // (hi - lo)
            t = lax.rem(i, hi - lo) + lo
            off = pl.multiple_of(t * 256, 256)
            r = dot_nn(nf[...], weight(yy, p.gu_at + off, 256))
            g, u = r[:, 0:LANES], r[:, LANES:256]
            GU[yy, :, pl.ds(off, 256)] = r.astype(bf16)
            HID[yy, :, pl.ds(pl.multiple_of(t * LANES, LANES), LANES)] = (
                g * sigmoid(g) * u
            ).astype(bf16)

        loop(2 * (hi - lo), run)

    ag_until(0, 1)
    tiles = 2 * ff // 256
    for lo in range(0, tiles, 4):
        hi = min(lo + 4, tiles)
        ag_until(p.gu_at + hi * 256)
        gate_up(lo, hi)
        ag_until(0, 1)

    def down_proj(lo, hi, more):
        def run(zz):
            cols = pl.ds(pl.multiple_of(zz * (width // 4), width // 4), width // 4)
            acc = dot_nt(HID[0, :, lo:hi], weight(0, p.d_at + lo, hi - lo, zz)) + dot_nt(
                HID[1, :, lo:hi], weight(1, p.d_at + lo, hi - lo, zz)
            )
            bff[:, cols] = bff[:, cols] + acc if more else acc

        loop(4, run)

    early = ff - sum(size for k, (at, size) in enumerate(p.gather) if k in p.gather_late)
    ag_until(p.d_at + early)
    down_proj(0, early, False)
    ag_until(p.cols)
    down_proj(early, ff, True)
    load_og.wait()

    def out_rows(blk):
        b = bff[blk, :]
        scale = rms(b)
        e = TB[blk, :].astype(f32)
        LO[blk, :] = (mid[blk, :] + b * scale * gains[3:4, :]).astype(bf16)
        BF[blk, :] = norm_grad(b, scale, gains[3:4, :], e).astype(bf16)
        dgains[3:4, :] += jnp.sum(b * scale * e, axis=0, keepdims=True)

    by_rows(out_rows)
    put_out = pltpu.make_async_copy(LO, out_hbm, loc.at[1])
    put_out.start()

    for k in range(n_gather):
        for m in range(8):
            ag(k, m).wait_send()

    n_reduce = len(p.reduce)

    def rs_parts(j):
        at, size = p.reduce[j]
        half = size // 2 // LANES * LANES
        return (pl.ds(at, half), pl.ds(0, half)), (pl.ds(at + half, size - half), pl.ds(half, size - half))

    def rs(j, m):
        at, size = p.reduce[j]
        cols, slot, part = pl.ds(at, size), j % 2, pl.ds(0, size)
        sem = (rs_s.at[j, m], rs_r.at[j, m])
        if m == 0:
            return remote(W.at[:, :, :, 1 - c, :, cols], R1.at[slot, :, :, :, :, part], *sem, core_peer)
        d = m - 5
        if j in p.reduce_late:
            (cols_a, part_a), (cols_b, part_b) = rs_parts(j)
            if m == 1:
                return remote(W.at[1 - y, z, :, c, :, cols_a], RQ2.at[j, :, :, part_a], *sem, y_peer)
            if m == 2:
                return remote(W.at[:, z, 1 - x, c, :, cols_b], RQ2.at[j, :, :, part_b], *sem, x_peer)
            if m == 3:
                return remote(W.at[y, z, 1 - x, c, :, cols_a], RQ3.at[j, :, part_a], *sem, x_peer)
            if m == 4:
                return remote(W.at[1 - y, z, x, c, :, cols_b], RQ3.at[j, :, part_b], *sem, y_peer)
            return remote(W.at[:, up(d + 1), :, c, :, cols], RQ1.at[j, d, :, :, :, part], *sem, z_peers[d])
        low, high = pl.ds(0, p.split_sum(j)), pl.ds(p.split_sum(j), 4 - p.split_sum(j))
        if m == 1:
            return remote(W.at[1 - y, low, :, c, :, cols], R2A.at[slot, low, :, :, part], *sem, y_peer)
        if m == 2:
            return remote(W.at[:, high, 1 - x, c, :, cols], R2B.at[slot, :, pl.ds(0, 4 - p.split_sum(j)), :, part], *sem, x_peer)
        if m == 3:
            return remote(W.at[y, low, 1 - x, c, :, cols], R3A.at[slot, low, :, part], *sem, x_peer)
        if m == 4:
            return remote(W.at[1 - y, high, x, c, :, cols], R3B.at[slot, pl.ds(0, 4 - p.split_sum(j)), :, part], *sem, y_peer)
        return remote(W.at[y, up(d + 1), x, c, :, cols], R4.at[slot, d, :, part], *sem, z_peers[d])

    rs_sources = [core_peer, y_peer, x_peer, x_peer, y_peer] + z_sources
    n_late = len(p.reduce_late)

    def rs_first(m):
        return 2 if m == 0 else n_late + 2

    def rs_start(j, m):
        if j >= rs_first(m):
            pl.semaphore_wait(credit.at[m], 1)
        rs(j, m).start()

    def rs_used(j, m):
        if j + 2 < n_reduce and j + 2 >= rs_first(m):
            pl.semaphore_signal(credit.at[m], inc=1, device_id=rs_sources[m], device_id_type=MESH)

    finished = []

    def put_sum(i):
        at, size = p.reduce[finished[i]]
        return pltpu.make_async_copy(
            ST.at[i % 2, :, pl.ds(0, size)], gr_hbm.at[:, pl.ds(at, size)], loc.at[2 + i % 2]
        )

    def finish(j, total):
        i = len(finished)
        finished.append(j)
        if i >= 2:
            put_sum(i - 2).wait()
        ST[i % 2, :, pl.ds(0, p.reduce[j][1])] = total
        put_sum(i).start()

    def rs_core(j):
        at, size = p.reduce[j]
        cols, slot, part = pl.ds(at, size), j % 2, pl.ds(0, size)
        rs(j, 0).wait_recv()

        def add(i):
            a, b, d = i // 8, lax.rem(i // 2, 4), lax.rem(i, 2)
            W[a, b, d, c, :, cols] = W[a, b, d, c, :, cols] + R1[slot, a, b, d, :, part]

        loop(16, add)
        rs_used(j, 0)

    def rs_late_event(j, phase):
        at, size = p.reduce[j]
        cols, part = pl.ds(at, size), pl.ds(0, size)
        (cols_a, part_a), (cols_b, part_b) = rs_parts(j)
        if phase == 0:
            rs_start(j, 0)
        elif phase == 1:
            rs_core(j)
            for m in (5, 6, 7):
                rs_start(j, m)
        elif phase == 2:
            for m in (5, 6, 7):
                rs(j, m).wait_recv()

            def add_q(i):
                a, b = i // 2, lax.rem(i, 2)
                total = W[a, z, b, c, :, cols].astype(f32)
                for d in range(3):
                    total = total + RQ1[j, d, a, b, :, part].astype(f32)
                W[a, z, b, c, :, cols] = total.astype(bf16)

            loop(4, add_q)
            rs_start(j, 1)
            rs_start(j, 2)
        elif phase == 3:
            rs(j, 1).wait_recv()
            rs(j, 2).wait_recv()
            for d in range(2):
                W[y, z, d, c, :, cols_a] = W[y, z, d, c, :, cols_a] + RQ2[j, d, :, part_a]
                W[d, z, x, c, :, cols_b] = W[d, z, x, c, :, cols_b] + RQ2[j, d, :, part_b]
            rs_start(j, 3)
            rs_start(j, 4)
        else:
            rs(j, 3).wait_recv()
            rs(j, 4).wait_recv()
            finish(j, W[y, z, x, c, :, cols].astype(f32) + RQ3[j, :, part].astype(f32))

    def rs_event(j, phase):
        if j in p.reduce_late:
            rs_late_event(j, phase)
            return
        at, size = p.reduce[j]
        cols, slot, part = pl.ds(at, size), j % 2, pl.ds(0, size)
        n_low = p.split_sum(j)
        n_high = 4 - n_low
        if phase == 0:
            rs_start(j, 0)
        elif phase == 1:
            rs_core(j)
            rs_start(j, 1)
            rs_start(j, 2)
        elif phase == 2:
            rs(j, 1).wait_recv()

            def add_a(i):
                b, d = i // 2, lax.rem(i, 2)
                W[y, b, d, c, :, cols] = W[y, b, d, c, :, cols] + R2A[slot, b, d, :, part]

            loop(2 * n_low, add_a)
            rs_used(j, 1)
            rs_start(j, 3)
            rs(j, 2).wait_recv()

            def add_b(i):
                a, b = i // n_high, lax.rem(i, n_high)
                W[a, b + n_low, x, c, :, cols] = W[a, b + n_low, x, c, :, cols] + R2B[slot, a, b, :, part]

            loop(2 * n_high, add_b)
            rs_used(j, 2)
            rs_start(j, 4)
        elif phase == 3:
            rs(j, 3).wait_recv()
            for b in range(n_low):
                W[y, b, x, c, :, cols] = W[y, b, x, c, :, cols] + R3A[slot, b, :, part]
            rs_used(j, 3)
            rs(j, 4).wait_recv()
            for b in range(n_high):
                W[y, b + n_low, x, c, :, cols] = W[y, b + n_low, x, c, :, cols] + R3B[slot, b, :, part]
            rs_used(j, 4)
            for m in (5, 6, 7):
                rs_start(j, m)
        else:
            for m in (5, 6, 7):
                rs(j, m).wait_recv()
            total = W[y, z, x, c, :, cols].astype(f32)
            for d in range(3):
                total = total + R4[slot, d, :, part].astype(f32)
            for m in (5, 6, 7):
                rs_used(j, m)
            finish(j, total)

    def slot_of(j, phase):
        return j + (LATE_SLOTS[phase] if j in p.reduce_late else phase)

    events = sorted(
        ((j, phase) for j in range(n_reduce) for phase in range(5)), key=lambda e: (slot_of(*e), -e[0], e[1])
    )
    done = [0]

    def pump(ready, until):
        while done[0] < len(events):
            j, phase = events[done[0]]
            if j >= ready or slot_of(j, phase) >= until:
                break
            rs_event(j, phase)
            done[0] += 1

    def back_tile(yy, t, bh):
        off = pl.multiple_of(t * 256, 256)
        g = GU[yy, :, pl.ds(off, LANES)].astype(f32)
        u = GU[yy, :, cut(off + LANES, LANES)].astype(f32)
        s = sigmoid(g)
        GU[yy, :, pl.ds(off, LANES)] = (bh * u * s * (1.0 + g * (1.0 - s))).astype(bf16)
        GU[yy, :, cut(off + LANES, LANES)] = (bh * g * s).astype(bf16)

    pairs = ff // 256

    def back_hidden(lo, hi):
        def run(i):
            yy, t = i // (hi - lo), lax.rem(i, hi - lo) + lo
            bh = dot_nn(BF[...], weight(yy, p.d_at + pl.multiple_of(t * 256, 256), 256))
            back_tile(yy, 2 * t, bh[:, 0:LANES])
            back_tile(yy, 2 * t + 1, bh[:, LANES:256])

        loop(2 * (hi - lo), run)

    def grad_down(lo, hi):
        def run(i):
            yy, off = i // (hi - lo), pl.multiple_of((lax.rem(i, hi - lo) + lo) * 256, 256)
            put_weight(yy, p.d_at + off, 256, dot_nn(T[...], HID[yy, :, pl.ds(off, 256)]))

        loop(2 * (hi - lo), run)

    def back_hidden_last(yy):
        bh = dot_nn(BF[...], weight(yy, p.d_at + pairs * 256, LANES))
        back_tile(yy, jnp.int32(2 * pairs), bh)

    def grad_down_last(yy):
        put_weight(yy, p.d_at + pairs * 256, LANES, dot_nn(T[...], HID[yy, :, pl.ds(pairs * 256, LANES)]))

    n_d = len(p.d_cuts)
    n_gu = n_d + len(p.gu_cuts)
    first_pairs = p.d_cuts[0][1] // 256
    T[...] = jnp.transpose(BF[...])
    back_hidden(0, first_pairs)
    grad_down(0, first_pairs)
    pump(1, PACE[0])
    back_hidden(first_pairs, pairs)
    if ff % 256:
        loop(2, back_hidden_last)
    grad_down(first_pairs, pairs)
    if ff % 256:
        loop(2, grad_down_last)
    pump(n_d, PACE[1])

    def back_normed(zz):
        cols = pl.ds(pl.multiple_of(zz * (width // 4), width // 4), width // 4)
        acc = dot_nt(GU[0, :, 0:ff], weight(0, p.gu_at, ff, zz))
        acc = acc + dot_nt(GU[0, :, ff : 2 * ff], weight(0, p.gu_at + ff, ff, zz))
        acc = acc + dot_nt(GU[1, :, 0:ff], weight(1, p.gu_at, ff, zz))
        bff[:, cols] = acc + dot_nt(GU[1, :, ff : 2 * ff], weight(1, p.gu_at + ff, ff, zz))

    loop(2, back_normed)
    pump(n_d, PACE[1] + 1)
    loop(2, lambda i: back_normed(i + 2))
    pump(n_d, PACE[2])
    T[...] = jnp.transpose(nf[...])

    def grad_gate_up(lo, hi):
        def run(i):
            yy, off = i // (hi - lo), pl.multiple_of((lax.rem(i, hi - lo) + lo) * 256, 256)
            put_weight(yy, p.gu_at + off, 256, dot_nn(T[...], GU[yy, :, pl.ds(off, 256)]))

        loop(2 * (hi - lo), run)

    grad_gate_up(0, 4)
    pump(n_d + 2, PACE[3])
    grad_gate_up(4, 2 * ff // 256)
    pump(n_gu, PACE[4])

    def mid_back(blk):
        m = mid[blk, :]
        scale = rms(m)
        e = bff[blk, :]
        bm = TB[blk, :].astype(f32) + norm_grad(m, scale, gains[2:3, :], e)
        dgains[2:3, :] += jnp.sum(m * scale * e, axis=0, keepdims=True)
        b = ba[blk, :]
        scale_b = rms(b)
        BF[blk, :] = norm_grad(b, scale_b, gains[1:2, :], bm).astype(bf16)
        dgains[1:2, :] += jnp.sum(b * scale_b * bm, axis=0, keepdims=True)
        mid[blk, :] = bm

    by_rows(mid_back)
    load_again = pltpu.make_async_copy(tok_hbm, TB, loc.at[0])
    load_again.start()
    pump(n_gu, PACE[5])

    per_o = hc // 256

    def back_att(i):
        yy, off = i // per_o, pl.multiple_of(lax.rem(i, per_o) * 256, 256)
        nf[:, cut(yy * hc + off, 256)] = dot_nn(BF[...], weight(yy, p.o_at + off, 256)).astype(bf16)

    loop(2 * per_o, back_att)
    T[...] = jnp.transpose(BF[...])

    def grad_out_tile(i):
        yy, off = i // per_o, pl.multiple_of(lax.rem(i, per_o) * 256, 256)
        put_weight(yy, p.o_at + off, 256, dot_nn(T[...], att[:, cut(yy * hc + off, 256)]))

    loop(2 * per_o, grad_out_tile)
    pump(n_gu + 1, PACE[6])

    stat_b[...] = jnp.zeros_like(stat_b)
    for h in range(p.heads):
        cols = slice(h * HEAD_DIM, (h + 1) * HEAD_DIM)
        inner = jnp.sum(nf[:, cols].astype(f32) * att[:, cols].astype(f32), axis=-1, keepdims=True)
        stat_b[...] = jnp.where(lane == h, inner, stat_b[...])
    log_rows = jnp.transpose(stat_a[...])[0 : p.heads, :]
    inner_rows = jnp.transpose(stat_b[...])[0 : p.heads, :]
    gains[8 : 8 + p.heads, 0:rows] = log_rows
    gains[8 : 8 + p.heads, rows : 2 * rows] = inner_rows
    build_mask(1)

    def attend_grad(h):
        yy, k_at, v_at, q_at = head_at(h)
        q = KVQ[yy, :, q_at]
        do = nf[:, pl.ds(pl.multiple_of(h * HEAD_DIM, HEAD_DIM), HEAD_DIM)]
        log_row = gains[pl.ds(8 + h, 1), 0:rows]
        inner_row = gains[pl.ds(8 + h, 1), rows : 2 * rows]

        def side(ref, place, hide):
            k, v = ref[yy, :, k_at], ref[yy, :, v_at]
            s = dot_nt(k, q) * log2_scale
            if hide:
                s = s + MK[...]
            prob = jnp.exp2(s - log_row)
            dv = dot_nn(prob.astype(bf16), do)
            ds = (prob * (dot_nt(v, do) - inner_row) * attn_scale).astype(bf16)
            dk = dot_nn(ds, q)
            dq = dot_tn(ds, k)
            ref[yy, :, v_at] = dv.astype(bf16)
            ref[yy, :, k_at] = rotated(dk, place, -1.0).astype(bf16)
            return dq

        DQ[...] = side(KVQ, own_place, True)

        @pl.when(second)
        def _():
            DQ[...] += side(KVp, old_place, False)

        KVQ[yy, :, q_at] = rotated(DQ[...], own_place, -1.0).astype(bf16)

    def grad_heads(lo, hi):
        loop(hi - lo, lambda h: attend_grad(h + lo))

    for i in range(4):
        grad_heads(i * p.heads // 4, (i + 1) * p.heads // 4)
        pump(n_gu + 1, PACE[7 + i])

    put_out.wait()

    back_send = remote(LO, KVp.at[0, :, pl.ds(0, width)], extra_s.at[0], extra_r.at[0], y_peer)

    @pl.when(second)
    def _():
        def old_back(zz):
            cols = pl.ds(pl.multiple_of(zz * (width // 4), width // 4), width // 4)
            LO[:, cols] = (
                dot_nt(KVp[0], weight(0, p.k_at, 2 * hc, zz)) + dot_nt(KVp[1], weight(1, p.k_at, 2 * hc, zz))
            ).astype(bf16)

        loop(4, old_back)
        back_send.start()

    def own_back(zz):
        cols = pl.ds(pl.multiple_of(zz * (width // 4), width // 4), width // 4)
        bff[:, cols] = dot_nt(KVQ[0], weight(0, p.k_at, p.kvq, zz)) + dot_nt(KVQ[1], weight(1, p.k_at, p.kvq, zz))

    loop(4, own_back)
    pump(n_gu + 1, PACE[11])
    T[...] = jnp.transpose(xo[...])
    tiles = p.kvq // 256

    def grad_kvq(i):
        yy, off = i // tiles, pl.multiple_of(lax.rem(i, tiles) * 256, 256)
        put_weight(yy, p.k_at + off, 256, dot_nn(T[...], KVQ[yy, :, pl.ds(off, 256)]))

    loop(2 * tiles, grad_kvq)

    @pl.when(second)
    def _():
        T[...] = jnp.transpose(xp[...])
        old_tiles = 2 * hc // 256

        def grad_old(i):
            yy, off = i // old_tiles, pl.multiple_of(lax.rem(i, old_tiles) * 256, 256)
            put_weight(
                yy, p.k_at + off, 256,
                weight(yy, p.k_at + off, 256).astype(f32) + dot_nn(T[...], KVp[yy, :, pl.ds(off, 256)]),
            )

        loop(2 * old_tiles, grad_old)

    pump(n_reduce - 1, PACE[12])
    load_again.wait()

    @pl.when(first)
    def _():
        back_send.wait_recv()

        def join(blk):
            bff[blk, :] += KVp[0, blk, pl.ds(0, width)].astype(f32)

        by_rows(join)

    def in_back(blk):
        t = TB[blk, :].astype(f32)
        scale = rms(t)
        e = bff[blk, :]
        mid[blk, :] = mid[blk, :] + norm_grad(t, scale, gains[0:1, :], e)
        dgains[0:1, :] += jnp.sum(t * scale * e, axis=0, keepdims=True)

    by_rows(in_back)
    put_ig = pltpu.make_async_copy(mid, ig_hbm, loc.at[0])
    put_ig.start()

    gain_cols = jnp.transpose(jnp.concatenate([dgains[...], jnp.zeros((LANES - 8, width), f32)], axis=0))
    put_weight(0, 0, LANES, gain_cols)
    put_weight(1, 0, LANES, gain_cols)
    pump(n_reduce, len(events) * 2)
    put_ig.wait()
    for i in (n_reduce - 2, n_reduce - 1):
        put_sum(i).wait()

    for j in range(n_reduce):
        for m in range(8):
            rs(j, m).wait_send()

    @pl.when(first)
    def _():
        for i in range(TOKEN_PIECES):
            tok_piece(i).wait_send()

    @pl.when(second)
    def _():
        back_send.wait_send()


def finish_layer(plan, out_hbm, ig_hbm, total, out_to, ig_to, gq, gk, gv, go, gg, gu, gd, g0, g1, g2, g3, o_buf, i_buf, sems):
    hc, ff = plan.head_cols, plan.ff_cols
    loads = (
        pltpu.make_async_copy(out_hbm, o_buf, sems.at[0]),
        pltpu.make_async_copy(ig_hbm, i_buf, sems.at[1]),
    )
    stores = (
        pltpu.make_async_copy(o_buf, out_to, sems.at[2]),
        pltpu.make_async_copy(i_buf, ig_to, sems.at[3]),
    )
    for copy in loads:
        copy.start()
    gq[...] = total[:, plan.q_at : plan.q_at + hc]
    gk[...] = total[:, plan.k_at : plan.k_at + hc]
    gv[...] = total[:, plan.v_at : plan.v_at + hc]
    go[...] = total[:, plan.o_at : plan.o_at + hc]
    for load, store in zip(loads, stores):
        load.wait()
        store.start()
    gd[...] = total[:, plan.d_at : plan.d_at + ff]
    for t in range(ff // LANES):
        at = plan.gu_at + 2 * t * LANES
        gg[:, t * LANES : (t + 1) * LANES] = total[:, at : at + LANES]
        gu[:, t * LANES : (t + 1) * LANES] = total[:, at + LANES : at + 2 * LANES]
    gains = jnp.transpose(total[:, 0:LANES])
    for i, ref in enumerate((g0, g1, g2, g3)):
        ref[...] = gains[i : i + 1, :]
    for store in stores:
        store.wait()


def fused_on_device(
    tokens,
    query_weight,
    key_weight,
    value_weight,
    out_weight,
    gate_weight,
    up_weight,
    down_weight,
    gain_attn_in,
    gain_attn_out,
    gain_ff_in,
    gain_ff_out,
    piece_starts,
    out_grad,
):
    rows, width = tokens.shape
    plan = Plan(rows, width, query_weight.shape[1], gate_weight.shape[1], query_weight.shape[0])
    gain_shard = jnp.stack([gain_attn_in, gain_attn_out, gain_ff_in, gain_ff_out]).astype(f32)
    half = rope_base ** (-(np.arange(HALF, dtype=np.float32) * 2.0) / HEAD_DIM)
    inverse = jnp.asarray(np.concatenate([half, half])[None].astype(np.float32))
    hc, ff, sr = plan.head_cols, plan.ff_cols, plan.shard_rows
    anywhere = pl.BlockSpec(memory_space=pl.ANY)
    in_vmem = pl.BlockSpec(memory_space=pltpu.VMEM)
    n_gather, n_reduce = len(plan.gather), len(plan.reduce)
    scratch = [
        pltpu.VMEM((2, 4, 2, 2, sr, plan.cols), bf16),
        pltpu.VMEM((2, rows, 3 * hc), bf16),
        pltpu.VMEM((2, rows, 2 * hc), bf16),
        pltpu.VMEM((rows, width), bf16),
        pltpu.VMEM((rows, width), bf16),
        pltpu.VMEM((width, rows), bf16),
        pltpu.VMEM((rows, 2 * hc), bf16),
        pltpu.VMEM((rows, width), f32),
        pltpu.VMEM((rows, width), f32),
        pltpu.VMEM((rows, width), f32),
        pltpu.VMEM((rows, width), bf16),
        pltpu.VMEM((2, rows, 2 * ff), bf16),
        pltpu.VMEM((2, rows, ff), bf16),
        pltpu.VMEM((rows, width), bf16),
        pltpu.VMEM((rows, width), bf16),
        pltpu.VMEM((rows, width), bf16),
        pltpu.VMEM((rows, rows), f32),
        pltpu.VMEM((8 + plan.heads, max(width, 2 * rows)), f32),
        pltpu.VMEM((8, width), f32),
        pltpu.VMEM((rows, LANES), f32),
        pltpu.VMEM((rows, LANES), f32),
        pltpu.VMEM((rows, HEAD_DIM), f32),
        pltpu.VMEM((2 * rows, LANES), f32),
        pltpu.VMEM((2 * rows, LANES), f32),
        pltpu.VMEM((2, 2, 4, 2, sr, 512), bf16),
        pltpu.VMEM((2, 2, 2, sr, 512), bf16),
        pltpu.VMEM((2, 2, 3, sr, 512), bf16),
        pltpu.VMEM((2, 2, sr, 512), bf16),
        pltpu.VMEM((2, 3, sr, 512), bf16),
        pltpu.VMEM((2, 3, sr, 512), bf16),
        pltpu.VMEM((max(1, REDUCE_LATE), 3, 2, 2, sr, 512), bf16),
        pltpu.VMEM((max(1, REDUCE_LATE), 2, sr, 512), bf16),
        pltpu.VMEM((max(1, REDUCE_LATE), sr, 512), bf16),
        pltpu.VMEM((2, sr, 512), f32),
        pltpu.SemaphoreType.DMA((n_gather, 8)),
        pltpu.SemaphoreType.DMA((n_gather, 8)),
        pltpu.SemaphoreType.DMA((n_reduce, 8)),
        pltpu.SemaphoreType.DMA((n_reduce, 8)),
        pltpu.SemaphoreType.DMA((4,)),
        pltpu.SemaphoreType.DMA((5 + 2 * (ff // LANES),)),
        pltpu.SemaphoreType.DMA((1 + TOKEN_PIECES,)),
        pltpu.SemaphoreType.DMA((1 + TOKEN_PIECES,)),
        pltpu.SemaphoreType.REGULAR((8,)),
    ]
    out, input_grad, total = pl.pallas_call(
        functools.partial(fused_layer, plan),
        out_shape=(
            jax.ShapeDtypeStruct((rows, width), bf16),
            jax.ShapeDtypeStruct((rows, width), f32),
            jax.ShapeDtypeStruct((sr, plan.cols), f32),
        ),
        in_specs=[anywhere] * 7 + [in_vmem] + [anywhere] * 2 + [pl.BlockSpec(memory_space=pltpu.SMEM), in_vmem],
        out_specs=(anywhere, anywhere, anywhere),
        scratch_shapes=scratch,
        compiler_params=pltpu.CompilerParams(
            collective_id=0, has_side_effects=True, vmem_limit_bytes=67043328
        ),
        name="fused_layer",
    )(
        key_weight, value_weight, query_weight, gate_weight, up_weight, out_weight.T, down_weight.T,
        gain_shard, tokens, out_grad, piece_starts, inverse,
    )

    def grad(*shape):
        return jax.ShapeDtypeStruct(shape, f32)

    outs = pl.pallas_call(
        functools.partial(finish_layer, plan),
        out_shape=(
            jax.ShapeDtypeStruct((rows, width), bf16),
            grad(rows, width),
            grad(sr, hc),
            grad(sr, hc),
            grad(sr, hc),
            grad(sr, hc),
            grad(sr, ff),
            grad(sr, ff),
            grad(sr, ff),
        )
        + (grad(1, sr),) * 4,
        in_specs=[anywhere, anywhere, in_vmem],
        out_specs=(anywhere, anywhere) + (in_vmem,) * 11,
        scratch_shapes=[
            pltpu.VMEM((rows, width), bf16),
            pltpu.VMEM((rows, width), f32),
            pltpu.SemaphoreType.DMA((4,)),
        ],
        name="finish_layer",
    )(out, input_grad, total)
    outs = list(outs)
    outs[5], outs[8] = outs[5].T, outs[8].T
    return tuple(outs[:9]) + tuple(o[0] for o in outs[9:])


def fits_fused(mesh, tokens, query_weight, gate_weight, piece_starts):
    dp, tensor = mesh.shape["dp"], mesh.shape["tensor"]
    sequences, pieces = piece_starts.shape
    return (
        (dp, tensor, pieces, sequences) == (16, 2, 2, dp)
        and tokens.shape[0] % (dp * tensor * 256) == 0
        and tokens.shape[1] == query_weight.shape[1]
        and tokens.shape[1] % (dp * 16) == 0
        and query_weight.shape[1] % (tensor * 256) == 0
        and gate_weight.shape[1] % (tensor * LANES) == 0
    )


def solution(mesh):
    placed = (
        P(("dp", "tensor"), None),
        P("dp", "tensor"),
        P("dp", "tensor"),
        P("dp", "tensor"),
        P("tensor", "dp"),
        P("dp", "tensor"),
        P("dp", "tensor"),
        P("tensor", "dp"),
        P("dp"),
        P("dp"),
        P("dp"),
        P("dp"),
        P("dp", None),
        P(("dp", "tensor"), None),
    )
    def step(*arrays):
        fused = fits_fused(mesh, arrays[0], arrays[1], arrays[5], arrays[12])
        return place(fused_on_device if fused else on_device)(*arrays)

    def place(body):
        return jax.shard_map(
            body,
            mesh=mesh,
            in_specs=placed,
            out_specs=(
                P(("dp", "tensor"), None),
                P(("dp", "tensor"), None),
                P("dp", "tensor"),
                P("dp", "tensor"),
                P("dp", "tensor"),
                P("tensor", "dp"),
                P("dp", "tensor"),
                P("dp", "tensor"),
                P("tensor", "dp"),
                P("dp"),
                P("dp"),
                P("dp"),
                P("dp"),
            ),
            check_vma=False,
        )

    return step
```

```python
import functools
import math

import jax
import jax.numpy as jnp
import numpy as np
from jax import lax
from jax.experimental import pallas as pl
from jax.experimental.pallas import tpu as pltpu
from jax.sharding import PartitionSpec as P

HEAD_DIM = 128
PIECE = 256


norm_eps = 1e-06
rope_base = 50000.0
masked = -1e30


def rms_scale(values):
    return lax.rsqrt(jnp.mean(values * values, axis=-1, keepdims=True) + norm_eps)


def norm_back(values, scale, gain, incoming):
    weighted = gain * incoming
    row_inner = jnp.mean(values * weighted, axis=-1, keepdims=True)
    backward = scale * weighted - values * (scale * scale * scale) * row_inner
    return (backward, jnp.sum(values * scale * incoming, axis=0))


def rope_at(places):
    half_dim = HEAD_DIM // 2
    inverse = rope_base ** (-(jnp.arange(half_dim, dtype=jnp.float32) * 2.0) / HEAD_DIM)
    angles = places.astype(jnp.float32)[:, None, None] * inverse[None, None, :]
    return (jnp.cos(angles), jnp.sin(angles))


def rope_tables(count, length):
    return rope_at(jnp.arange(count, dtype=jnp.int32) % length)


def rotate(values, cosine, sine):
    half_dim = values.shape[-1] // 2
    lower_half = values[..., :half_dim]
    upper_half = values[..., half_dim:]
    return jnp.concatenate(
        [lower_half * cosine - upper_half * sine, upper_half * cosine + lower_half * sine], axis=-1
    )


def unrotate(grads, cosine, sine):
    half_dim = grads.shape[-1] // 2
    lower_half = grads[..., :half_dim]
    upper_half = grads[..., half_dim:]
    return jnp.concatenate(
        [lower_half * cosine + upper_half * sine, upper_half * cosine - lower_half * sine], axis=-1
    )


def piece_ids(starts, length):
    places = jnp.arange(length, dtype=jnp.int32)
    inside = (places[None, :, None] >= starts[:, None, :]) & (
        places[None, :, None] < starts[:, None, :] + PIECE
    )
    labels = jnp.arange(1, starts.shape[1] + 1, dtype=jnp.int32)
    return jnp.sum(jnp.where(inside, labels, 0), axis=2)


def visible(piece_id, offset, count):
    length = piece_id.shape[0]
    query_place = offset + jnp.arange(count, dtype=jnp.int32)
    key_place = jnp.arange(length, dtype=jnp.int32)
    query_ids = piece_id[offset : offset + count]
    return (key_place[None, :] <= query_place[:, None]) | (
        query_ids[:, None] == piece_id[None, :]
    ) & (query_ids[:, None] > 0)


def block_scores(queries, key_vecs, piece_id, offset, count):
    attn_scale = 1.0 / math.sqrt(queries.shape[-1])
    q_block = queries[offset : offset + count]
    scores = (
        jnp.einsum("qhd,khd->hqk", q_block, key_vecs, preferred_element_type=jnp.float32)
        * attn_scale
    )
    return (jnp.where(visible(piece_id, offset, count)[None], scores, masked), q_block)


def attend_one(seq_items):
    queries, key_vecs, values, piece_id = seq_items
    length = queries.shape[0]
    block_rows = min(512, length)
    outputs = []
    log_totals = []
    for offset in range(0, length, block_rows):
        logits, q_block = block_scores(queries, key_vecs, piece_id, offset, block_rows)
        row_max = jnp.max(logits, axis=-1, keepdims=True)
        log_total = row_max + jnp.log(jnp.sum(jnp.exp(logits - row_max), axis=-1, keepdims=True))
        probs = jnp.exp(logits - log_total).astype(jnp.bfloat16)
        mixed = jnp.einsum("hqk,khd->qhd", probs, values, preferred_element_type=jnp.float32)
        outputs.append(mixed.astype(jnp.bfloat16))
        log_totals.append(log_total)
    return (jnp.concatenate(outputs, axis=0), jnp.concatenate(log_totals, axis=1))


def attend_back(seq_items):
    queries, key_vecs, values, piece_id, log_totals, grad_mixed = seq_items
    length = queries.shape[0]
    block_rows = min(512, length)
    attn_scale = 1.0 / math.sqrt(queries.shape[-1])
    grad_keys = jnp.zeros(key_vecs.shape, jnp.float32)
    grad_values = jnp.zeros(values.shape, jnp.float32)
    grad_queries = []
    for offset in range(0, length, block_rows):
        logits, q_block = block_scores(queries, key_vecs, piece_id, offset, block_rows)
        probs = jnp.exp(logits - log_totals[:, offset : offset + block_rows])
        grad_block = grad_mixed[offset : offset + block_rows]
        grad_values = grad_values + jnp.einsum(
            "hqk,qhd->khd",
            probs.astype(jnp.bfloat16),
            grad_block,
            preferred_element_type=jnp.float32,
        )
        grad_probs = jnp.einsum(
            "qhd,khd->hqk", grad_block, values, preferred_element_type=jnp.float32
        )
        row_inner = jnp.sum(probs * grad_probs, axis=-1, keepdims=True)
        grad_scores = (probs * (grad_probs - row_inner) * attn_scale).astype(jnp.bfloat16)
        grad_queries.append(
            jnp.einsum("hqk,khd->qhd", grad_scores, key_vecs, preferred_element_type=jnp.float32)
        )
        grad_keys = grad_keys + jnp.einsum(
            "hqk,qhd->khd", grad_scores, q_block, preferred_element_type=jnp.float32
        )
    return (jnp.concatenate(grad_queries, axis=0), grad_keys, grad_values)


def times_trans(left, right):
    return lax.dot_general(
        left, right, (((1,), (1,)), ((), ())), preferred_element_type=jnp.float32
    )


def trans_times(left, right):
    return lax.dot_general(
        left, right, (((0,), (0,)), ((), ())), preferred_element_type=jnp.float32
    )


def fetch_weights(shards):
    gathered = (
        lax.all_gather(shards[0], "dp", axis=0, tiled=True),
        lax.all_gather(shards[1], "dp", axis=0, tiled=True),
        lax.all_gather(shards[2], "dp", axis=0, tiled=True),
        lax.all_gather(shards[3], "dp", axis=1, tiled=True),
        lax.all_gather(shards[4], "dp", axis=0, tiled=True),
        lax.all_gather(shards[5], "dp", axis=0, tiled=True),
        lax.all_gather(shards[6], "dp", axis=1, tiled=True),
        lax.all_gather(shards[7], "dp", axis=1, tiled=True),
    )
    return gathered


def gather_rows(normed):
    return lax.all_gather(normed, "tensor", axis=0, tiled=True)


def sum_rows(sum_terms):
    return lax.psum_scatter(sum_terms, "tensor", scatter_dimension=0, tiled=True)


def gather_grads(grad_terms):
    return lax.all_gather(grad_terms, "tensor", axis=0, tiled=True)


def sum_grads(grad_terms):
    return lax.psum_scatter(
        grad_terms.astype(jnp.bfloat16), "tensor", scatter_dimension=0, tiled=True
    ).astype(jnp.float32)


def by_sequence(values, seq_count):
    return values.reshape(seq_count, values.shape[0] // seq_count, values.shape[1], values.shape[2])


def attention_part(normed, gathered, cosine, sine, piece_id):
    whole_rows = gather_rows(normed)
    group_rows = whole_rows.shape[0]
    seq_count = piece_id.shape[0]

    def project(weight):
        return jnp.dot(whole_rows, weight, preferred_element_type=jnp.float32).reshape(
            group_rows, -1, HEAD_DIM
        )

    queries = rotate(project(gathered[0]), cosine, sine).astype(jnp.bfloat16)
    key_vecs = rotate(project(gathered[1]), cosine, sine).astype(jnp.bfloat16)
    values = project(gathered[2]).astype(jnp.bfloat16)
    outputs, log_totals = lax.map(
        attend_one,
        (
            by_sequence(queries, seq_count),
            by_sequence(key_vecs, seq_count),
            by_sequence(values, seq_count),
            piece_id,
        ),
    )
    return (whole_rows, queries, key_vecs, values, outputs.reshape(group_rows, -1), log_totals)


def feed_part(normed, gathered):
    whole_rows = gather_rows(normed)
    gate_pre = jnp.dot(whole_rows, gathered[4], preferred_element_type=jnp.float32)
    up_pre = jnp.dot(whole_rows, gathered[5], preferred_element_type=jnp.float32)
    hidden = (jax.nn.silu(gate_pre) * up_pre).astype(jnp.bfloat16)
    return (whole_rows, gate_pre, up_pre, hidden)


def on_device(
    tokens,
    query_weight,
    key_weight,
    value_weight,
    out_weight,
    gate_weight,
    up_weight,
    down_weight,
    gain_attn_in,
    gain_attn_out,
    gain_ff_in,
    gain_ff_out,
    piece_starts,
    out_grad,
):
    shards = (
        query_weight,
        key_weight,
        value_weight,
        out_weight,
        gate_weight,
        up_weight,
        down_weight,
        jnp.stack([gain_attn_in, gain_attn_out, gain_ff_in, gain_ff_out]),
    )
    gathered = fetch_weights(shards)
    gain_rows = gathered[7].astype(jnp.float32)
    tok_rows = tokens.astype(jnp.float32)
    seq_count = piece_starts.shape[0]
    own_rows = tokens.shape[0]
    group_rows = own_rows * lax.axis_size("tensor")
    length = group_rows // seq_count
    piece_id = piece_ids(piece_starts, length)
    incoming = out_grad.astype(jnp.float32)
    scale_in = rms_scale(tok_rows)
    normed_in = (tok_rows * scale_in * gain_rows[0]).astype(jnp.bfloat16)
    cosine, sine = rope_tables(group_rows, length)
    attn_parts = attention_part(normed_in, gathered, cosine, sine, piece_id)
    branch_attn = sum_rows(jnp.dot(attn_parts[4], gathered[3], preferred_element_type=jnp.float32))
    scale_attn = rms_scale(branch_attn)
    mid_rows = tok_rows + branch_attn * scale_attn * gain_rows[1]
    scale_mid = rms_scale(mid_rows)
    normed_ff = (mid_rows * scale_mid * gain_rows[2]).astype(jnp.bfloat16)
    feed_parts = feed_part(normed_ff, gathered)
    branch_ff = sum_rows(jnp.dot(feed_parts[3], gathered[6], preferred_element_type=jnp.float32))
    scale_ff = rms_scale(branch_ff)
    result = (mid_rows + branch_ff * scale_ff * gain_rows[3]).astype(jnp.bfloat16)
    gathered = fetch_weights(shards)
    feed_parts = feed_part(normed_ff, gathered)
    whole_ff, gate_pre, up_pre, hidden = feed_parts
    back_ff, gain_grad_ff_out = norm_back(branch_ff, scale_ff, gain_rows[3], incoming)
    wide_back_ff = gather_grads(back_ff.astype(jnp.bfloat16))
    grad_down = trans_times(hidden, wide_back_ff)
    back_hidden = times_trans(wide_back_ff, gathered[6])
    sigmoid_gate = jax.nn.sigmoid(gate_pre)
    back_gate = (
        back_hidden * up_pre * sigmoid_gate * (1.0 + gate_pre * (1.0 - sigmoid_gate))
    ).astype(jnp.bfloat16)
    back_up = (back_hidden * gate_pre * sigmoid_gate).astype(jnp.bfloat16)
    grad_gate = trans_times(whole_ff, back_gate)
    grad_up = trans_times(whole_ff, back_up)
    back_normed_ff = sum_grads(
        times_trans(back_gate, gathered[4]) + times_trans(back_up, gathered[5])
    )
    back_from_ff, gain_grad_ff_in = norm_back(mid_rows, scale_mid, gain_rows[2], back_normed_ff)
    back_mid = incoming + back_from_ff
    back_attn, gain_grad_attn_out = norm_back(branch_attn, scale_attn, gain_rows[1], back_mid)
    wide_back_attn = gather_grads(back_attn.astype(jnp.bfloat16))
    attn_parts = attention_part(normed_in, gathered, cosine, sine, piece_id)
    whole_in, queries, key_vecs, values, attended, log_totals = attn_parts
    grad_out = trans_times(attended, wide_back_attn)
    back_attended = times_trans(wide_back_attn, gathered[3]).astype(jnp.bfloat16)
    back_queries, back_keys, back_values = lax.map(
        attend_back,
        (
            by_sequence(queries, seq_count),
            by_sequence(key_vecs, seq_count),
            by_sequence(values, seq_count),
            piece_id,
            log_totals,
            by_sequence(back_attended.reshape(group_rows, -1, HEAD_DIM), seq_count),
        ),
    )
    back_queries = (
        unrotate(back_queries.reshape(group_rows, -1, HEAD_DIM), cosine, sine)
        .reshape(group_rows, -1)
        .astype(jnp.bfloat16)
    )
    back_keys = (
        unrotate(back_keys.reshape(group_rows, -1, HEAD_DIM), cosine, sine)
        .reshape(group_rows, -1)
        .astype(jnp.bfloat16)
    )
    back_values = back_values.reshape(group_rows, -1).astype(jnp.bfloat16)
    grad_query = trans_times(whole_in, back_queries)
    grad_key = trans_times(whole_in, back_keys)
    grad_value = trans_times(whole_in, back_values)
    back_normed_in = sum_grads(
        times_trans(back_queries, gathered[0])
        + times_trans(back_keys, gathered[1])
        + times_trans(back_values, gathered[2])
    )
    back_from_in, gain_grad_attn_in = norm_back(tok_rows, scale_in, gain_rows[0], back_normed_in)
    input_grad = back_mid + back_from_in
    weight_terms = (grad_query, grad_key, grad_value, grad_out, grad_gate, grad_up, grad_down)
    gain_grads = lax.psum(
        jnp.stack([gain_grad_attn_in, gain_grad_attn_out, gain_grad_ff_in, gain_grad_ff_out]),
        "tensor",
    )
    grad_sums = (
        lax.psum_scatter(
            weight_terms[0].astype(jnp.bfloat16), "dp", scatter_dimension=0, tiled=True
        ).astype(jnp.float32),
        lax.psum_scatter(
            weight_terms[1].astype(jnp.bfloat16), "dp", scatter_dimension=0, tiled=True
        ).astype(jnp.float32),
        lax.psum_scatter(
            weight_terms[2].astype(jnp.bfloat16), "dp", scatter_dimension=0, tiled=True
        ).astype(jnp.float32),
        lax.psum_scatter(
            weight_terms[3].astype(jnp.bfloat16), "dp", scatter_dimension=1, tiled=True
        ).astype(jnp.float32),
        lax.psum_scatter(
            weight_terms[4].astype(jnp.bfloat16), "dp", scatter_dimension=0, tiled=True
        ).astype(jnp.float32),
        lax.psum_scatter(
            weight_terms[5].astype(jnp.bfloat16), "dp", scatter_dimension=0, tiled=True
        ).astype(jnp.float32),
        lax.psum_scatter(
            weight_terms[6].astype(jnp.bfloat16), "dp", scatter_dimension=1, tiled=True
        ).astype(jnp.float32),
        lax.psum_scatter(
            gain_grads.astype(jnp.bfloat16), "dp", scatter_dimension=1, tiled=True
        ).astype(jnp.float32),
    )
    return (
        result,
        input_grad,
        grad_sums[0],
        grad_sums[1],
        grad_sums[2],
        grad_sums[3],
        grad_sums[4],
        grad_sums[5],
        grad_sums[6],
        grad_sums[7][0],
        grad_sums[7][1],
        grad_sums[7][2],
        grad_sums[7][3],
    )


LANES = 128
HALF = HEAD_DIM // 2
MESH = pl.DeviceIdType.MESH
GATHER_FIRST = (256, 384)
GATHER_DOWN = (512, 384, 256, 256)
REDUCE_DOWN = (512, 512)
REDUCE_LAST = (256, 256)
GATHER_LATE = 2
LATE_STEP = 0
REDUCE_LATE = 0
LATE_SLOTS = (0, 1, 6, 7, 8)
X_FIRST = (1, 2)
X_FIRST_SUM = (2, 2, 2, 2, 2, 2, 2, 2, 1, 1, 1, 1, 1, 1, 1, 1, 1, 1, 1, 1)
PACE = (1, 2, 3, 4, 5, 6, 7, 8, 9, 10, 11, 12, 13)
TOKEN_PIECES = 8
TOKENS_EARLY = 4
TOKENS_A_STEP = 1
f32 = jnp.float32
bf16 = jnp.bfloat16


class Plan:
    def __init__(self, rows, width, head_cols, ff_cols, shard_rows):
        self.rows = rows
        self.width = width
        self.head_cols = head_cols
        self.ff_cols = ff_cols
        self.shard_rows = shard_rows
        self.heads = 2 * head_cols // HEAD_DIM
        self.k_at = LANES
        self.v_at = self.k_at + head_cols
        self.q_at = self.v_at + head_cols
        self.o_at = self.q_at + head_cols
        self.gu_at = self.o_at + head_cols
        self.d_at = self.gu_at + 2 * ff_cols
        self.cols = self.d_at + ff_cols
        self.kvq = 3 * head_cols

        def cuts(start, total, sizes=()):
            pieces = []
            while total > 0:
                size = min(sizes[len(pieces)] if len(pieces) < len(sizes) else 512, total)
                pieces.append((start, size))
                start, total = start + size, total - size
            return pieces

        gu_cuts = cuts(self.gu_at, 2 * ff_cols)
        self.gather = (
            cuts(0, self.v_at, GATHER_FIRST)
            + [(self.v_at, head_cols), (self.q_at, head_cols), (self.o_at, head_cols)]
            + gu_cuts
            + cuts(self.d_at, ff_cols, GATHER_DOWN)
        )
        self.d_cuts = cuts(self.d_at, ff_cols, REDUCE_DOWN)
        self.gu_cuts = gu_cuts
        self.reduce = (
            self.d_cuts
            + self.gu_cuts
            + [(self.o_at, head_cols), (self.q_at, head_cols), (self.v_at, head_cols)]
            + cuts(self.k_at, head_cols, REDUCE_LAST)
            + [(0, LANES)]
        )
        down = len(self.gather) - len(cuts(self.d_at, ff_cols, GATHER_DOWN))
        self.gather_late = list(range(down, down + GATHER_LATE))
        self.gather_early = [k for k in range(len(self.gather)) if k not in self.gather_late]
        self.reduce_late = set(range(REDUCE_LATE))

    def held(self, at):
        early = [i + 3 for i, k in enumerate(self.gather_early) if self.gather[k][0] < at]
        late = [len(self.gather_early) + LATE_STEP + 1 for k in self.gather_late if self.gather[k][0] < at]
        return max(early + late + [0])

    def split(self, k):
        return X_FIRST[k % len(X_FIRST)]

    def split_sum(self, j):
        return X_FIRST_SUM[j % len(X_FIRST_SUM)]


def sigmoid(v):
    return 0.5 * jnp.tanh(0.5 * v) + 0.5


def dot_nn(left, right):
    return lax.dot_general(left, right, (((1,), (0,)), ((), ())), preferred_element_type=f32)


def dot_nt(left, right):
    return lax.dot_general(left, right, (((1,), (1,)), ((), ())), preferred_element_type=f32)


def dot_tn(left, right):
    return lax.dot_general(left, right, (((0,), (0,)), ((), ())), preferred_element_type=f32)


def fused_layer(
    plan,
    k_hbm, v_hbm, q_hbm, g_hbm, u_hbm, o_hbm, d_hbm, gain_shard, tok_hbm, og_hbm, starts_ref, inverse_ref,
    out_hbm, ig_hbm, gr_hbm,
    W, KVQ, KVp, xo, xp, T, att, ba, mid, bff, nf, GU, HID, BF, TB, LO, MK, gains, dgains, stat_a, stat_b, DQ, cos_ref, sin_ref,
    R1, R2A, R2B, R3A, R3B, R4, RQ1, RQ2, RQ3, ST,
    ag_s, ag_r, rs_s, rs_r, loc, pack_sem, extra_s, extra_r, credit,
):
    p = plan
    dp = lax.axis_index("dp")
    y = lax.axis_index("tensor")
    c = lax.rem(dp, 2)
    x = lax.rem(dp // 2, 2)
    z = dp // 4
    rows, width, hc, ff = p.rows, p.width, p.head_cols, p.ff_cols
    first = y == 0
    second = y == 1

    def dev(zz, xx, cc, yy):
        return (zz * 4 + xx * 2 + cc, yy)

    def up(step):
        return lax.rem(z + step, 4)

    core_peer = dev(z, x, 1 - c, y)
    x_peer = dev(z, 1 - x, c, y)
    y_peer = dev(z, x, c, 1 - y)
    z_peers = [dev(up(d), x, c, y) for d in (1, 2, 3)]
    z_sources = [dev(up(4 - d), x, c, y) for d in (1, 2, 3)]

    def remote(src, dst, send, recv, to):
        return pltpu.make_async_remote_copy(
            src_ref=src, dst_ref=dst, send_sem=send, recv_sem=recv, device_id=to, device_id_type=MESH
        )

    def cut(at, size):
        return pl.ds(at if isinstance(at, int) else pl.multiple_of(at, LANES), size)

    def weight(yy, at, size, zz=None):
        if zz is None:
            return W[yy, :, :, :, :, cut(at, size)].reshape(width, size)
        return W[yy, zz, :, :, :, cut(at, size)].reshape(width // 4, size)

    def put_weight(yy, at, size, value):
        W[yy, :, :, :, :, cut(at, size)] = value.astype(bf16).reshape(4, 2, 2, p.shard_rows, size)

    def rms(v):
        return lax.rsqrt(jnp.mean(v * v, axis=-1, keepdims=True) + norm_eps)

    def norm_grad(v, scale, gain, e):
        weighted = gain * e
        inner = jnp.mean(v * weighted, axis=-1, keepdims=True)
        return scale * weighted - v * (scale * scale * scale) * inner

    def by_rows(body, size=64):
        def step(i, carry):
            body(pl.ds(pl.multiple_of(i * size, size), size))
            return carry

        lax.fori_loop(0, rows // size, step, 0)

    def loop(count, body):
        def step(i, carry):
            body(i)
            return carry

        lax.fori_loop(0, count, step, 0)

    own_w = W.at[y, z, x, c]

    def ag(k, m):
        at, size = p.gather[k]
        cols = pl.ds(at, size)
        sem = (ag_s.at[k, m], ag_r.at[k, m])
        if k in p.gather_late:
            half = size // 2 // LANES * LANES
            cols_a, cols_b = pl.ds(at, half), pl.ds(at + half, size - half)
            if m < 3:
                ref = W.at[:, z, :, c, :, cols]
                return remote(ref, ref, *sem, z_peers[m])
            if m == 3:
                return remote(own_w.at[:, cols_a], W.at[y, z, x, c, :, cols_a], *sem, x_peer)
            if m == 4:
                return remote(own_w.at[:, cols_b], W.at[y, z, x, c, :, cols_b], *sem, y_peer)
            if m == 5:
                ref = W.at[y, z, :, c, :, cols_a]
                return remote(ref, ref, *sem, y_peer)
            if m == 6:
                ref = W.at[:, z, x, c, :, cols_b]
                return remote(ref, ref, *sem, x_peer)
        low, high = pl.ds(0, p.split(k)), pl.ds(p.split(k), 4 - p.split(k))
        if m < 3:
            return remote(own_w.at[:, cols], W.at[y, z, x, c, :, cols], *sem, z_peers[m])
        if m == 3:
            ref = W.at[y, low, x, c, :, cols]
            return remote(ref, ref, *sem, x_peer)
        if m == 4:
            ref = W.at[y, high, x, c, :, cols]
            return remote(ref, ref, *sem, y_peer)
        if m == 5:
            ref = W.at[y, low, :, c, :, cols]
            return remote(ref, ref, *sem, y_peer)
        if m == 6:
            ref = W.at[:, high, x, c, :, cols]
            return remote(ref, ref, *sem, x_peer)
        ref = W.at[:, :, :, c, :, cols]
        return remote(ref, ref, *sem, core_peer)

    n_gather = len(p.gather)
    n_early = len(p.gather_early)

    def ag_step(s):
        def early(i):
            return p.gather_early[i] if 0 <= i < n_early else None

        k = early(s)
        if k is not None:
            for m in (0, 1, 2):
                ag(k, m).wait_recv()
            ag(k, 3).start()
            ag(k, 4).start()
        k = early(s - 1)
        if k is not None:
            ag(k, 3).wait_recv()
            ag(k, 5).start()
            ag(k, 4).wait_recv()
            ag(k, 6).start()
        k = early(s - 2)
        if k is not None:
            ag(k, 5).wait_recv()
            ag(k, 6).wait_recv()
            ag(k, 7).start()
        k = early(s - 3)
        if k is not None:
            ag(k, 7).wait_recv()
        if s == n_early + LATE_STEP:
            for k in p.gather_late:
                for m in (0, 1, 2):
                    ag(k, m).wait_recv()
                ag(k, 7).start()
        if s == n_early + LATE_STEP + 1:
            for k in p.gather_late:
                ag(k, 7).wait_recv()

    steps = [0]

    def tok_piece(i):
        blk = pl.ds(i * (rows // TOKEN_PIECES), rows // TOKEN_PIECES)
        return remote(tok_hbm.at[blk, :], xp.at[blk, :], extra_s.at[1 + i], extra_r.at[1 + i], y_peer)

    def tok_send(i):
        @pl.when(first)
        def _():
            tok_piece(i).start()

    def ag_until(at, more=0):
        goal = max(p.held(at), steps[0] + more - 1)
        while steps[0] <= goal:
            ag_step(steps[0])
            for i in range(TOKENS_EARLY, TOKEN_PIECES):
                if (i - TOKENS_EARLY) // TOKENS_A_STEP == steps[0]:
                    tok_send(i)
            steps[0] += 1
            if steps[0] == 1:
                ag_late_turn()
            if steps[0] == 5:
                ag_late_z()

    def ag_late_turn():
        for k in p.gather_late:
            ag(k, 3).wait_recv()
            ag(k, 5).start()
            ag(k, 4).wait_recv()
            ag(k, 6).start()

    def ag_late_z():
        for k in p.gather_late:
            ag(k, 5).wait_recv()
            ag(k, 6).wait_recv()
            for m in (0, 1, 2):
                ag(k, m).start()

    load_tok = pltpu.make_async_copy(tok_hbm, TB, loc.at[0])
    load_tok.start()
    packing = []
    for src, at, size in (
        (k_hbm, p.k_at, hc), (v_hbm, p.v_at, hc), (q_hbm, p.q_at, hc), (o_hbm, p.o_at, hc), (d_hbm, p.d_at, ff)
    ):
        packing.append((src, own_w.at[:, pl.ds(at, size)]))
    for t in range(ff // LANES):
        for n, src in enumerate((g_hbm, u_hbm)):
            to = own_w.at[:, pl.ds(p.gu_at + (2 * t + n) * LANES, LANES)]
            packing.append((src.at[:, pl.ds(t * LANES, LANES)], to))
    packing = [pltpu.make_async_copy(src, to, pack_sem.at[i]) for i, (src, to) in enumerate(packing)]
    for copy in packing:
        copy.start()
    barrier = pltpu.get_barrier_semaphore()
    for peer in [core_peer, x_peer, y_peer] + z_peers:
        pl.semaphore_signal(barrier, inc=1, device_id=peer, device_id_type=MESH)
    count = gain_shard.shape[0]
    spread = jnp.concatenate([gain_shard[...], jnp.zeros((LANES - count, p.shard_rows), f32)], axis=0)
    W[y, z, x, c, :, pl.ds(0, LANES)] = jnp.transpose(spread).astype(bf16)
    for copy in packing:
        copy.wait()
    pl.semaphore_wait(barrier, 6)

    for k in p.gather_late:
        ag(k, 3).start()
        ag(k, 4).start()

    for k in p.gather_early:
        for m in (0, 1, 2):
            ag(k, m).start()
    for i in range(TOKENS_EARLY):
        tok_send(i)
    load_tok.wait()

    def tables(i):
        blk = pl.ds(pl.multiple_of(i * 64, 64), 64)
        place = (lax.broadcasted_iota(jnp.int32, (64, LANES), 0) + i * 64).astype(f32)
        angle = place * inverse_ref[...]
        cos_ref[blk, :] = jnp.cos(angle)
        turned = jnp.sin(angle)
        sin_ref[blk, :] = jnp.where(lax.broadcasted_iota(jnp.int32, (64, LANES), 1) < HALF, -turned, turned)

    loop(2 * rows // 64, tables)

    start = starts_ref[0, y] - y * rows

    def build_mask(query_dim):
        def body(blk):
            shape = (64, rows)
            r = lax.broadcasted_iota(jnp.int32, shape, 0) + blk.start
            s = lax.broadcasted_iota(jnp.int32, shape, 1)
            q_pos, k_pos = (r, s) if query_dim == 0 else (s, r)
            inside = (r >= start) & (r < start + PIECE) & (s >= start) & (s < start + PIECE)
            MK[blk, :] = jnp.where((k_pos <= q_pos) | inside, 0.0, masked)

        by_rows(body)

    build_mask(0)
    dgains[...] = jnp.zeros_like(dgains)

    ag_until(LANES)
    gains[0:8, 0:width] = jnp.transpose(weight(0, 0, LANES).astype(f32))[0:8, :]

    def norm_in(src, dst):
        def body(blk):
            t = src[blk, :].astype(f32)
            dst[blk, :] = (t * rms(t) * gains[0:1, :]).astype(bf16)

        by_rows(body)

    norm_in(TB, xo)

    def rotated(u, place, sign):
        return u * cos_ref[place, :] + sign * (pltpu.roll(u, HALF, 1) * sin_ref[place, :])

    def project(src, dst, at, place, turn):
        def run(yy, off):
            r = dot_nn(src[...], weight(yy, LANES + off, 256))
            for hh in range(2):
                u = r[:, hh * HEAD_DIM : (hh + 1) * HEAD_DIM]
                if turn:
                    u = rotated(u, place, 1.0)
                dst[yy, :, cut(off + hh * HEAD_DIM, HEAD_DIM)] = u.astype(bf16)

        per = hc // 256
        loop(2 * per, lambda i: run(i // per, pl.multiple_of(at + lax.rem(i, per) * 256, 256)))

    own_place = pl.ds(pl.multiple_of(y * rows, rows), rows)
    old_place = pl.ds(0, rows)
    ag_until(p.v_at)
    project(xo, KVQ, 0, own_place, True)
    ag_until(p.q_at)
    project(xo, KVQ, hc, own_place, False)

    @pl.when(second)
    def _():
        for i in range(TOKEN_PIECES):
            tok_piece(i).wait_recv()
        norm_in(xp, xp)

    ag_until(p.o_at)
    project(xo, KVQ, 2 * hc, own_place, True)

    @pl.when(second)
    def _():
        project(xp, KVp, 0, old_place, True)

    ag_until(p.gu_at)

    @pl.when(second)
    def _():
        project(xp, KVp, hc, old_place, False)

    ag_until(0, 1)

    per_y = hc // HEAD_DIM
    attn_scale = 1.0 / math.sqrt(HEAD_DIM)
    log2_scale = attn_scale * math.log2(math.e)
    lane = lax.broadcasted_iota(jnp.int32, (1, LANES), 1)

    def head_at(h):
        yy = h // per_y
        off = pl.multiple_of(lax.rem(h, per_y) * HEAD_DIM, HEAD_DIM)
        return yy, cut(off, HEAD_DIM), cut(off + hc, HEAD_DIM), cut(off + 2 * hc, HEAD_DIM)

    def attend(i, both):
        h = i // 2
        blk = pl.ds(pl.multiple_of(lax.rem(i, 2) * (rows // 2), rows // 2), rows // 2)
        yy, k_at, v_at, q_at = head_at(h)
        q = KVQ[yy, blk, q_at]
        s = dot_nt(q, KVQ[yy, :, k_at]) * log2_scale + MK[blk, :]
        top = jnp.max(s, axis=-1, keepdims=True)
        if both:
            s_old = dot_nt(q, KVp[yy, :, k_at]) * log2_scale
            top = jnp.maximum(top, jnp.max(s_old, axis=-1, keepdims=True))
        e = jnp.exp2(s - top)
        total = jnp.sum(e, axis=-1, keepdims=True)
        if both:
            e_old = jnp.exp2(s_old - top)
            total = total + jnp.sum(e_old, axis=-1, keepdims=True)
        inv = 1.0 / total
        o = dot_nn((e * inv).astype(bf16), KVQ[yy, :, v_at])
        if both:
            o = o + dot_nn((e_old * inv).astype(bf16), KVp[yy, :, v_at])
        att[blk, pl.ds(pl.multiple_of(h * HEAD_DIM, HEAD_DIM), HEAD_DIM)] = o.astype(bf16)
        stat = top + jnp.log2(total)
        stat_a[blk, :] = jnp.where(lane == h, stat, stat_a[blk, :])

    def attend_heads(lo, hi):
        @pl.when(first)
        def _():
            loop(2 * (hi - lo), lambda i: attend(i + 2 * lo, False))

        @pl.when(second)
        def _():
            loop(2 * (hi - lo), lambda i: attend(i + 2 * lo, True))

    stat_a[...] = jnp.zeros_like(stat_a)
    for h in range(0, p.heads, 2):
        attend_heads(h, h + 2)
        ag_until(0, 1)


    def o_proj(zz):
        cols = pl.ds(pl.multiple_of(zz * (width // 4), width // 4), width // 4)
        ba[:, cols] = dot_nt(att[:, 0:hc], weight(0, p.o_at, hc, zz)) + dot_nt(
            att[:, hc : 2 * hc], weight(1, p.o_at, hc, zz)
        )

    loop(4, o_proj)

    def mid_rows(blk):
        b = ba[blk, :]
        m = TB[blk, :].astype(f32) + b * rms(b) * gains[1:2, :]
        mid[blk, :] = m
        nf[blk, :] = (m * rms(m) * gains[2:3, :]).astype(bf16)

    by_rows(mid_rows)
    load_og = pltpu.make_async_copy(og_hbm, TB, loc.at[0])
    load_og.start()

    def gate_up(lo, hi):
        def run(i):
            yy = i // (hi - lo)
            t = lax.rem(i, hi - lo) + lo
            off = pl.multiple_of(t * 256, 256)
            r = dot_nn(nf[...], weight(yy, p.gu_at + off, 256))
            g, u = r[:, 0:LANES], r[:, LANES:256]
            GU[yy, :, pl.ds(off, 256)] = r.astype(bf16)
            HID[yy, :, pl.ds(pl.multiple_of(t * LANES, LANES), LANES)] = (
                g * sigmoid(g) * u
            ).astype(bf16)

        loop(2 * (hi - lo), run)

    ag_until(0, 1)
    tiles = 2 * ff // 256
    for lo in range(0, tiles, 2):
        hi = min(lo + 2, tiles)
        ag_until(p.gu_at + hi * 256)
        gate_up(lo, hi)

    def down_proj(lo, hi, more):
        def run(zz):
            cols = pl.ds(pl.multiple_of(zz * (width // 4), width // 4), width // 4)
            acc = dot_nt(HID[0, :, lo:hi], weight(0, p.d_at + lo, hi - lo, zz)) + dot_nt(
                HID[1, :, lo:hi], weight(1, p.d_at + lo, hi - lo, zz)
            )
            bff[:, cols] = bff[:, cols] + acc if more else acc

        loop(4, run)

    ready = 0
    for n, (at, size) in enumerate(p.gather[p.gather_late[0] :]):
        if n >= GATHER_LATE - 1:
            ag_until(at + size)
            down_proj(ready, at + size - p.d_at, ready > 0)
            ready = at + size - p.d_at

    load_og.wait()

    def out_rows(blk):
        b = bff[blk, :]
        scale = rms(b)
        e = TB[blk, :].astype(f32)
        LO[blk, :] = (mid[blk, :] + b * scale * gains[3:4, :]).astype(bf16)
        BF[blk, :] = norm_grad(b, scale, gains[3:4, :], e).astype(bf16)
        dgains[3:4, :] += jnp.sum(b * scale * e, axis=0, keepdims=True)

    by_rows(out_rows)
    put_out = pltpu.make_async_copy(LO, out_hbm, loc.at[1])
    put_out.start()

    for k in range(n_gather):
        for m in range(8):
            ag(k, m).wait_send()

    n_reduce = len(p.reduce)

    def rs_parts(j):
        at, size = p.reduce[j]
        half = size // 2 // LANES * LANES
        return (pl.ds(at, half), pl.ds(0, half)), (pl.ds(at + half, size - half), pl.ds(half, size - half))

    def rs(j, m):
        at, size = p.reduce[j]
        cols, slot, part = pl.ds(at, size), j % 2, pl.ds(0, size)
        sem = (rs_s.at[j, m], rs_r.at[j, m])
        if m == 0:
            return remote(W.at[:, :, :, 1 - c, :, cols], R1.at[slot, :, :, :, :, part], *sem, core_peer)
        d = m - 5
        if j in p.reduce_late:
            (cols_a, part_a), (cols_b, part_b) = rs_parts(j)
            if m == 1:
                return remote(W.at[1 - y, z, :, c, :, cols_a], RQ2.at[j, :, :, part_a], *sem, y_peer)
            if m == 2:
                return remote(W.at[:, z, 1 - x, c, :, cols_b], RQ2.at[j, :, :, part_b], *sem, x_peer)
            if m == 3:
                return remote(W.at[y, z, 1 - x, c, :, cols_a], RQ3.at[j, :, part_a], *sem, x_peer)
            if m == 4:
                return remote(W.at[1 - y, z, x, c, :, cols_b], RQ3.at[j, :, part_b], *sem, y_peer)
            return remote(W.at[:, up(d + 1), :, c, :, cols], RQ1.at[j, d, :, :, :, part], *sem, z_peers[d])
        low, high = pl.ds(0, p.split_sum(j)), pl.ds(p.split_sum(j), 4 - p.split_sum(j))
        if m == 1:
            return remote(W.at[1 - y, low, :, c, :, cols], R2A.at[slot, low, :, :, part], *sem, y_peer)
        if m == 2:
            return remote(W.at[:, high, 1 - x, c, :, cols], R2B.at[slot, :, pl.ds(0, 4 - p.split_sum(j)), :, part], *sem, x_peer)
        if m == 3:
            return remote(W.at[y, low, 1 - x, c, :, cols], R3A.at[slot, low, :, part], *sem, x_peer)
        if m == 4:
            return remote(W.at[1 - y, high, x, c, :, cols], R3B.at[slot, pl.ds(0, 4 - p.split_sum(j)), :, part], *sem, y_peer)
        return remote(W.at[y, up(d + 1), x, c, :, cols], R4.at[slot, d, :, part], *sem, z_peers[d])

    rs_sources = [core_peer, y_peer, x_peer, x_peer, y_peer] + z_sources
    n_late = len(p.reduce_late)

    def rs_first(m):
        return 2 if m == 0 else n_late + 2

    def rs_start(j, m):
        if j >= rs_first(m):
            pl.semaphore_wait(credit.at[m], 1)
        rs(j, m).start()

    def rs_used(j, m):
        if j + 2 < n_reduce and j + 2 >= rs_first(m):
            pl.semaphore_signal(credit.at[m], inc=1, device_id=rs_sources[m], device_id_type=MESH)

    finished = []

    def put_sum(i):
        at, size = p.reduce[finished[i]]
        return pltpu.make_async_copy(
            ST.at[i % 2, :, pl.ds(0, size)], gr_hbm.at[:, pl.ds(at, size)], loc.at[2 + i % 2]
        )

    def finish(j, total):
        i = len(finished)
        finished.append(j)
        if i >= 2:
            put_sum(i - 2).wait()
        ST[i % 2, :, pl.ds(0, p.reduce[j][1])] = total
        put_sum(i).start()

    def rs_core(j):
        at, size = p.reduce[j]
        cols, slot, part = pl.ds(at, size), j % 2, pl.ds(0, size)
        rs(j, 0).wait_recv()

        def add(i):
            a, b, d = i // 8, lax.rem(i // 2, 4), lax.rem(i, 2)
            W[a, b, d, c, :, cols] = W[a, b, d, c, :, cols] + R1[slot, a, b, d, :, part]

        loop(16, add)
        rs_used(j, 0)

    def rs_late_event(j, phase):
        at, size = p.reduce[j]
        cols, part = pl.ds(at, size), pl.ds(0, size)
        (cols_a, part_a), (cols_b, part_b) = rs_parts(j)
        if phase == 0:
            rs_start(j, 0)
        elif phase == 1:
            rs_core(j)
            for m in (5, 6, 7):
                rs_start(j, m)
        elif phase == 2:
            for m in (5, 6, 7):
                rs(j, m).wait_recv()

            def add_q(i):
                a, b = i // 2, lax.rem(i, 2)
                total = W[a, z, b, c, :, cols].astype(f32)
                for d in range(3):
                    total = total + RQ1[j, d, a, b, :, part].astype(f32)
                W[a, z, b, c, :, cols] = total.astype(bf16)

            loop(4, add_q)
            rs_start(j, 1)
            rs_start(j, 2)
        elif phase == 3:
            rs(j, 1).wait_recv()
            rs(j, 2).wait_recv()
            for d in range(2):
                W[y, z, d, c, :, cols_a] = W[y, z, d, c, :, cols_a] + RQ2[j, d, :, part_a]
                W[d, z, x, c, :, cols_b] = W[d, z, x, c, :, cols_b] + RQ2[j, d, :, part_b]
            rs_start(j, 3)
            rs_start(j, 4)
        else:
            rs(j, 3).wait_recv()
            rs(j, 4).wait_recv()
            finish(j, W[y, z, x, c, :, cols].astype(f32) + RQ3[j, :, part].astype(f32))

    def rs_event(j, phase):
        if j in p.reduce_late:
            rs_late_event(j, phase)
            return
        at, size = p.reduce[j]
        cols, slot, part = pl.ds(at, size), j % 2, pl.ds(0, size)
        n_low = p.split_sum(j)
        n_high = 4 - n_low
        if phase == 0:
            rs_start(j, 0)
        elif phase == 1:
            rs_core(j)
            rs_start(j, 1)
            rs_start(j, 2)
        elif phase == 2:
            rs(j, 1).wait_recv()

            def add_a(i):
                b, d = i // 2, lax.rem(i, 2)
                W[y, b, d, c, :, cols] = W[y, b, d, c, :, cols] + R2A[slot, b, d, :, part]

            loop(2 * n_low, add_a)
            rs_used(j, 1)
            rs_start(j, 3)
            rs(j, 2).wait_recv()

            def add_b(i):
                a, b = i // n_high, lax.rem(i, n_high)
                W[a, b + n_low, x, c, :, cols] = W[a, b + n_low, x, c, :, cols] + R2B[slot, a, b, :, part]

            loop(2 * n_high, add_b)
            rs_used(j, 2)
            rs_start(j, 4)
        elif phase == 3:
            rs(j, 3).wait_recv()
            for b in range(n_low):
                W[y, b, x, c, :, cols] = W[y, b, x, c, :, cols] + R3A[slot, b, :, part]
            rs_used(j, 3)
            rs(j, 4).wait_recv()
            for b in range(n_high):
                W[y, b + n_low, x, c, :, cols] = W[y, b + n_low, x, c, :, cols] + R3B[slot, b, :, part]
            rs_used(j, 4)
            for m in (5, 6, 7):
                rs_start(j, m)
        else:
            for m in (5, 6, 7):
                rs(j, m).wait_recv()
            total = W[y, z, x, c, :, cols].astype(f32)
            for d in range(3):
                total = total + R4[slot, d, :, part].astype(f32)
            for m in (5, 6, 7):
                rs_used(j, m)
            finish(j, total)

    def slot_of(j, phase):
        return j + (LATE_SLOTS[phase] if j in p.reduce_late else phase)

    events = sorted(
        ((j, phase) for j in range(n_reduce) for phase in range(5)), key=lambda e: (slot_of(*e), -e[0], e[1])
    )
    done = [0]

    def pump(ready, until):
        while done[0] < len(events):
            j, phase = events[done[0]]
            if j >= ready or slot_of(j, phase) >= until:
                break
            rs_event(j, phase)
            done[0] += 1

    def back_tile(yy, t, bh):
        off = pl.multiple_of(t * 256, 256)
        g = GU[yy, :, pl.ds(off, LANES)].astype(f32)
        u = GU[yy, :, cut(off + LANES, LANES)].astype(f32)
        s = sigmoid(g)
        GU[yy, :, pl.ds(off, LANES)] = (bh * u * s * (1.0 + g * (1.0 - s))).astype(bf16)
        GU[yy, :, cut(off + LANES, LANES)] = (bh * g * s).astype(bf16)

    pairs = ff // 256

    def back_hidden(lo, hi):
        def run(i):
            yy, t = i // (hi - lo), lax.rem(i, hi - lo) + lo
            bh = dot_nn(BF[...], weight(yy, p.d_at + pl.multiple_of(t * 256, 256), 256))
            back_tile(yy, 2 * t, bh[:, 0:LANES])
            back_tile(yy, 2 * t + 1, bh[:, LANES:256])

        loop(2 * (hi - lo), run)

    def grad_down(lo, hi):
        def run(i):
            yy, off = i // (hi - lo), pl.multiple_of((lax.rem(i, hi - lo) + lo) * 256, 256)
            put_weight(yy, p.d_at + off, 256, dot_nn(T[...], HID[yy, :, pl.ds(off, 256)]))

        loop(2 * (hi - lo), run)

    def back_hidden_last(yy):
        bh = dot_nn(BF[...], weight(yy, p.d_at + pairs * 256, LANES))
        back_tile(yy, jnp.int32(2 * pairs), bh)

    def grad_down_last(yy):
        put_weight(yy, p.d_at + pairs * 256, LANES, dot_nn(T[...], HID[yy, :, pl.ds(pairs * 256, LANES)]))

    n_d = len(p.d_cuts)
    n_gu = n_d + len(p.gu_cuts)
    first_pairs = p.d_cuts[0][1] // 256
    T[...] = jnp.transpose(BF[...])
    back_hidden(0, first_pairs)
    grad_down(0, first_pairs)
    pump(1, PACE[0])
    back_hidden(first_pairs, pairs)
    if ff % 256:
        loop(2, back_hidden_last)
    grad_down(first_pairs, pairs)
    if ff % 256:
        loop(2, grad_down_last)
    pump(n_d, PACE[1])

    def back_normed(zz):
        cols = pl.ds(pl.multiple_of(zz * (width // 4), width // 4), width // 4)
        acc = dot_nt(GU[0, :, 0:ff], weight(0, p.gu_at, ff, zz))
        acc = acc + dot_nt(GU[0, :, ff : 2 * ff], weight(0, p.gu_at + ff, ff, zz))
        acc = acc + dot_nt(GU[1, :, 0:ff], weight(1, p.gu_at, ff, zz))
        bff[:, cols] = acc + dot_nt(GU[1, :, ff : 2 * ff], weight(1, p.gu_at + ff, ff, zz))

    loop(2, back_normed)
    pump(n_d, PACE[1] + 1)
    loop(2, lambda i: back_normed(i + 2))
    pump(n_d, PACE[2])
    T[...] = jnp.transpose(nf[...])

    def grad_gate_up(lo, hi):
        def run(i):
            yy, off = i // (hi - lo), pl.multiple_of((lax.rem(i, hi - lo) + lo) * 256, 256)
            put_weight(yy, p.gu_at + off, 256, dot_nn(T[...], GU[yy, :, pl.ds(off, 256)]))

        loop(2 * (hi - lo), run)

    grad_gate_up(0, 4)
    pump(n_d + 2, PACE[3])
    grad_gate_up(4, 2 * ff // 256)
    pump(n_gu, PACE[4])

    def mid_back(blk):
        m = mid[blk, :]
        scale = rms(m)
        e = bff[blk, :]
        bm = TB[blk, :].astype(f32) + norm_grad(m, scale, gains[2:3, :], e)
        dgains[2:3, :] += jnp.sum(m * scale * e, axis=0, keepdims=True)
        b = ba[blk, :]
        scale_b = rms(b)
        BF[blk, :] = norm_grad(b, scale_b, gains[1:2, :], bm).astype(bf16)
        dgains[1:2, :] += jnp.sum(b * scale_b * bm, axis=0, keepdims=True)
        mid[blk, :] = bm

    by_rows(mid_back)
    load_again = pltpu.make_async_copy(tok_hbm, TB, loc.at[0])
    load_again.start()
    pump(n_gu, PACE[5])

    per_o = hc // 256

    def back_att(i):
        yy, off = i // per_o, pl.multiple_of(lax.rem(i, per_o) * 256, 256)
        nf[:, cut(yy * hc + off, 256)] = dot_nn(BF[...], weight(yy, p.o_at + off, 256)).astype(bf16)

    loop(2 * per_o, back_att)
    T[...] = jnp.transpose(BF[...])

    def grad_out_tile(i):
        yy, off = i // per_o, pl.multiple_of(lax.rem(i, per_o) * 256, 256)
        put_weight(yy, p.o_at + off, 256, dot_nn(T[...], att[:, cut(yy * hc + off, 256)]))

    loop(2 * per_o, grad_out_tile)
    pump(n_gu + 1, PACE[6])

    stat_b[...] = jnp.zeros_like(stat_b)
    for h in range(p.heads):
        cols = slice(h * HEAD_DIM, (h + 1) * HEAD_DIM)
        inner = jnp.sum(nf[:, cols].astype(f32) * att[:, cols].astype(f32), axis=-1, keepdims=True)
        stat_b[...] = jnp.where(lane == h, inner, stat_b[...])
    log_rows = jnp.transpose(stat_a[...])[0 : p.heads, :]
    inner_rows = jnp.transpose(stat_b[...])[0 : p.heads, :]
    gains[8 : 8 + p.heads, 0:rows] = log_rows
    gains[8 : 8 + p.heads, rows : 2 * rows] = inner_rows
    build_mask(1)

    def attend_grad(h):
        yy, k_at, v_at, q_at = head_at(h)
        q = KVQ[yy, :, q_at]
        do = nf[:, pl.ds(pl.multiple_of(h * HEAD_DIM, HEAD_DIM), HEAD_DIM)]
        log_row = gains[pl.ds(8 + h, 1), 0:rows]
        inner_row = gains[pl.ds(8 + h, 1), rows : 2 * rows]

        def side(ref, place, hide):
            k, v = ref[yy, :, k_at], ref[yy, :, v_at]
            s = dot_nt(k, q) * log2_scale
            if hide:
                s = s + MK[...]
            prob = jnp.exp2(s - log_row)
            dv = dot_nn(prob.astype(bf16), do)
            ds = (prob * (dot_nt(v, do) - inner_row) * attn_scale).astype(bf16)
            dk = dot_nn(ds, q)
            dq = dot_tn(ds, k)
            ref[yy, :, v_at] = dv.astype(bf16)
            ref[yy, :, k_at] = rotated(dk, place, -1.0).astype(bf16)
            return dq

        DQ[...] = side(KVQ, own_place, True)

        @pl.when(second)
        def _():
            DQ[...] += side(KVp, old_place, False)

        KVQ[yy, :, q_at] = rotated(DQ[...], own_place, -1.0).astype(bf16)

    def grad_heads(lo, hi):
        loop(hi - lo, lambda h: attend_grad(h + lo))

    for i in range(4):
        grad_heads(i * p.heads // 4, (i + 1) * p.heads // 4)
        pump(n_gu + 1, PACE[7 + i])

    put_out.wait()

    back_send = remote(LO, KVp.at[0, :, pl.ds(0, width)], extra_s.at[0], extra_r.at[0], y_peer)

    @pl.when(second)
    def _():
        def old_back(zz):
            cols = pl.ds(pl.multiple_of(zz * (width // 4), width // 4), width // 4)
            LO[:, cols] = (
                dot_nt(KVp[0], weight(0, p.k_at, 2 * hc, zz)) + dot_nt(KVp[1], weight(1, p.k_at, 2 * hc, zz))
            ).astype(bf16)

        loop(4, old_back)
        back_send.start()

    def own_back(zz):
        cols = pl.ds(pl.multiple_of(zz * (width // 4), width // 4), width // 4)
        bff[:, cols] = dot_nt(KVQ[0], weight(0, p.k_at, p.kvq, zz)) + dot_nt(KVQ[1], weight(1, p.k_at, p.kvq, zz))

    loop(4, own_back)
    pump(n_gu + 1, PACE[11])
    T[...] = jnp.transpose(xo[...])
    tiles = p.kvq // 256

    def grad_kvq(i):
        yy, off = i // tiles, pl.multiple_of(lax.rem(i, tiles) * 256, 256)
        put_weight(yy, p.k_at + off, 256, dot_nn(T[...], KVQ[yy, :, pl.ds(off, 256)]))

    loop(2 * tiles, grad_kvq)

    @pl.when(second)
    def _():
        T[...] = jnp.transpose(xp[...])
        old_tiles = 2 * hc // 256

        def grad_old(i):
            yy, off = i // old_tiles, pl.multiple_of(lax.rem(i, old_tiles) * 256, 256)
            put_weight(
                yy, p.k_at + off, 256,
                weight(yy, p.k_at + off, 256).astype(f32) + dot_nn(T[...], KVp[yy, :, pl.ds(off, 256)]),
            )

        loop(2 * old_tiles, grad_old)

    pump(n_reduce - 1, PACE[12])
    load_again.wait()

    @pl.when(first)
    def _():
        back_send.wait_recv()

        def join(blk):
            bff[blk, :] += KVp[0, blk, pl.ds(0, width)].astype(f32)

        by_rows(join)

    def in_back(blk):
        t = TB[blk, :].astype(f32)
        scale = rms(t)
        e = bff[blk, :]
        mid[blk, :] = mid[blk, :] + norm_grad(t, scale, gains[0:1, :], e)
        dgains[0:1, :] += jnp.sum(t * scale * e, axis=0, keepdims=True)

    by_rows(in_back)
    put_ig = pltpu.make_async_copy(mid, ig_hbm, loc.at[0])
    put_ig.start()

    gain_cols = jnp.transpose(jnp.concatenate([dgains[...], jnp.zeros((LANES - 8, width), f32)], axis=0))
    put_weight(0, 0, LANES, gain_cols)
    put_weight(1, 0, LANES, gain_cols)
    pump(n_reduce, len(events) * 2)
    put_ig.wait()
    for i in (n_reduce - 2, n_reduce - 1):
        put_sum(i).wait()

    for j in range(n_reduce):
        for m in range(8):
            rs(j, m).wait_send()

    @pl.when(first)
    def _():
        for i in range(TOKEN_PIECES):
            tok_piece(i).wait_send()

    @pl.when(second)
    def _():
        back_send.wait_send()


def finish_layer(plan, out_hbm, ig_hbm, total_hbm, out_to, ig_to, gq, gk, gv, go, gg, gu, gd, g0, g1, g2, g3, bufs, sems):
    o_buf, i_buf, total = bufs
    load_sem, store_sem = sems
    hc, ff = plan.head_cols, plan.ff_cols
    cuts = ((0, plan.gu_at), (plan.gu_at, 2 * ff), (plan.d_at, ff))
    loads = [pltpu.make_async_copy(out_hbm, o_buf, load_sem.at[0]), pltpu.make_async_copy(ig_hbm, i_buf, load_sem.at[1])]
    for i, (at, size) in enumerate(cuts):
        cols = pl.ds(at, size)
        loads.append(pltpu.make_async_copy(total_hbm.at[:, cols], total.at[:, cols], load_sem.at[2 + i]))
    moves = [[(o_buf, out_to)], [(i_buf, ig_to)]]
    moves.append(
        [
            (total.at[:, pl.ds(at, hc)], to)
            for at, to in ((plan.k_at, gk), (plan.v_at, gv), (plan.q_at, gq), (plan.o_at, go))
        ]
    )
    moves.append(
        [
            (total.at[:, pl.ds(plan.gu_at + (2 * t + n) * LANES, LANES)], to.at[:, pl.ds(t * LANES, LANES)])
            for t in range(ff // LANES)
            for n, to in enumerate((gg, gu))
        ]
    )
    moves.append([(total.at[:, pl.ds(plan.d_at, ff)], gd)])
    stores = []
    for load in loads:
        load.start()
    for load, group in zip(loads, moves):
        load.wait()
        for src, to in group:
            stores.append(pltpu.make_async_copy(src, to, store_sem.at[len(stores)]))
            stores[-1].start()
    gains = jnp.transpose(total[:, 0:LANES])
    for i, ref in enumerate((g0, g1, g2, g3)):
        ref[...] = gains[i : i + 1, :]
    for store in stores:
        store.wait()


def fused_on_device(
    tokens,
    query_weight,
    key_weight,
    value_weight,
    out_weight,
    gate_weight,
    up_weight,
    down_weight,
    gain_attn_in,
    gain_attn_out,
    gain_ff_in,
    gain_ff_out,
    piece_starts,
    out_grad,
):
    rows, width = tokens.shape
    plan = Plan(rows, width, query_weight.shape[1], gate_weight.shape[1], query_weight.shape[0])
    gain_shard = jnp.stack([gain_attn_in, gain_attn_out, gain_ff_in, gain_ff_out]).astype(f32)
    half = rope_base ** (-(np.arange(HALF, dtype=np.float32) * 2.0) / HEAD_DIM)
    inverse = jnp.asarray(np.concatenate([half, half])[None].astype(np.float32))
    hc, ff, sr = plan.head_cols, plan.ff_cols, plan.shard_rows
    anywhere = pl.BlockSpec(memory_space=pl.ANY)
    in_vmem = pl.BlockSpec(memory_space=pltpu.VMEM)
    n_gather, n_reduce = len(plan.gather), len(plan.reduce)
    scratch = [
        pltpu.VMEM((2, 4, 2, 2, sr, plan.cols), bf16),
        pltpu.VMEM((2, rows, 3 * hc), bf16),
        pltpu.VMEM((2, rows, 2 * hc), bf16),
        pltpu.VMEM((rows, width), bf16),
        pltpu.VMEM((rows, width), bf16),
        pltpu.VMEM((width, rows), bf16),
        pltpu.VMEM((rows, 2 * hc), bf16),
        pltpu.VMEM((rows, width), f32),
        pltpu.VMEM((rows, width), f32),
        pltpu.VMEM((rows, width), f32),
        pltpu.VMEM((rows, width), bf16),
        pltpu.VMEM((2, rows, 2 * ff), bf16),
        pltpu.VMEM((2, rows, ff), bf16),
        pltpu.VMEM((rows, width), bf16),
        pltpu.VMEM((rows, width), bf16),
        pltpu.VMEM((rows, width), bf16),
        pltpu.VMEM((rows, rows), f32),
        pltpu.VMEM((8 + plan.heads, max(width, 2 * rows)), f32),
        pltpu.VMEM((8, width), f32),
        pltpu.VMEM((rows, LANES), f32),
        pltpu.VMEM((rows, LANES), f32),
        pltpu.VMEM((rows, HEAD_DIM), f32),
        pltpu.VMEM((2 * rows, LANES), f32),
        pltpu.VMEM((2 * rows, LANES), f32),
        pltpu.VMEM((2, 2, 4, 2, sr, 512), bf16),
        pltpu.VMEM((2, 2, 2, sr, 512), bf16),
        pltpu.VMEM((2, 2, 3, sr, 512), bf16),
        pltpu.VMEM((2, 2, sr, 512), bf16),
        pltpu.VMEM((2, 3, sr, 512), bf16),
        pltpu.VMEM((2, 3, sr, 512), bf16),
        pltpu.VMEM((max(1, REDUCE_LATE), 3, 2, 2, sr, 512), bf16),
        pltpu.VMEM((max(1, REDUCE_LATE), 2, sr, 512), bf16),
        pltpu.VMEM((max(1, REDUCE_LATE), sr, 512), bf16),
        pltpu.VMEM((2, sr, 512), f32),
        pltpu.SemaphoreType.DMA((n_gather, 8)),
        pltpu.SemaphoreType.DMA((n_gather, 8)),
        pltpu.SemaphoreType.DMA((n_reduce, 8)),
        pltpu.SemaphoreType.DMA((n_reduce, 8)),
        pltpu.SemaphoreType.DMA((4,)),
        pltpu.SemaphoreType.DMA((5 + 2 * (ff // LANES),)),
        pltpu.SemaphoreType.DMA((1 + TOKEN_PIECES,)),
        pltpu.SemaphoreType.DMA((1 + TOKEN_PIECES,)),
        pltpu.SemaphoreType.REGULAR((8,)),
    ]
    out, input_grad, total = pl.pallas_call(
        functools.partial(fused_layer, plan),
        out_shape=(
            jax.ShapeDtypeStruct((rows, width), bf16),
            jax.ShapeDtypeStruct((rows, width), f32),
            jax.ShapeDtypeStruct((sr, plan.cols), f32),
        ),
        in_specs=[anywhere] * 7 + [in_vmem] + [anywhere] * 2 + [pl.BlockSpec(memory_space=pltpu.SMEM), in_vmem],
        out_specs=(anywhere, anywhere, anywhere),
        scratch_shapes=scratch,
        compiler_params=pltpu.CompilerParams(
            collective_id=0, has_side_effects=True, vmem_limit_bytes=67043328
        ),
        name="fused_layer",
    )(
        key_weight, value_weight, query_weight, gate_weight, up_weight, out_weight.T, down_weight.T,
        gain_shard, tokens, out_grad, piece_starts, inverse,
    )

    def grad(*shape):
        return jax.ShapeDtypeStruct(shape, f32)

    outs = pl.pallas_call(
        functools.partial(finish_layer, plan),
        out_shape=(
            jax.ShapeDtypeStruct((rows, width), bf16),
            grad(rows, width),
            grad(sr, hc),
            grad(sr, hc),
            grad(sr, hc),
            grad(sr, hc),
            grad(sr, ff),
            grad(sr, ff),
            grad(sr, ff),
        )
        + (grad(1, sr),) * 4,
        in_specs=[anywhere] * 3,
        out_specs=(anywhere,) * 9 + (in_vmem,) * 4,
        scratch_shapes=[
            (
                pltpu.VMEM((rows, width), bf16),
                pltpu.VMEM((rows, width), f32),
                pltpu.VMEM((sr, plan.cols), f32),
            ),
            (pltpu.SemaphoreType.DMA((5,)), pltpu.SemaphoreType.DMA((7 + 2 * (ff // LANES),))),
        ],
        name="finish_layer",
    )(out, input_grad, total)
    outs = list(outs)
    outs[5], outs[8] = outs[5].T, outs[8].T
    return tuple(outs[:9]) + tuple(o[0] for o in outs[9:])


def fits_fused(mesh, tokens, query_weight, gate_weight, piece_starts):
    dp, tensor = mesh.shape["dp"], mesh.shape["tensor"]
    sequences, pieces = piece_starts.shape
    return (
        (dp, tensor, pieces, sequences) == (16, 2, 2, dp)
        and tokens.shape[0] % (dp * tensor * 256) == 0
        and tokens.shape[1] == query_weight.shape[1]
        and tokens.shape[1] % (dp * 16) == 0
        and query_weight.shape[1] % (tensor * 256) == 0
        and gate_weight.shape[1] % (tensor * LANES) == 0
    )


def solution(mesh):
    placed = (
        P(("dp", "tensor"), None),
        P("dp", "tensor"),
        P("dp", "tensor"),
        P("dp", "tensor"),
        P("tensor", "dp"),
        P("dp", "tensor"),
        P("dp", "tensor"),
        P("tensor", "dp"),
        P("dp"),
        P("dp"),
        P("dp"),
        P("dp"),
        P("dp", None),
        P(("dp", "tensor"), None),
    )
    def step(*arrays):
        fused = fits_fused(mesh, arrays[0], arrays[1], arrays[5], arrays[12])
        return place(fused_on_device if fused else on_device)(*arrays)

    def place(body):
        return jax.shard_map(
            body,
            mesh=mesh,
            in_specs=placed,
            out_specs=(
                P(("dp", "tensor"), None),
                P(("dp", "tensor"), None),
                P("dp", "tensor"),
                P("dp", "tensor"),
                P("dp", "tensor"),
                P("tensor", "dp"),
                P("dp", "tensor"),
                P("dp", "tensor"),
                P("tensor", "dp"),
                P("dp"),
                P("dp"),
                P("dp"),
                P("dp"),
            ),
            check_vma=False,
        )

    return step
```

```python
import functools
import math

import jax
import jax.numpy as jnp
import numpy as np
from jax import lax
from jax.experimental import pallas as pl
from jax.experimental.pallas import tpu as pltpu
from jax.sharding import PartitionSpec as P

HEAD_DIM = 128
PIECE = 256


norm_eps = 1e-06
rope_base = 50000.0
masked = -1e30


def rms_scale(values):
    return lax.rsqrt(jnp.mean(values * values, axis=-1, keepdims=True) + norm_eps)


def norm_back(values, scale, gain, incoming):
    weighted = gain * incoming
    row_inner = jnp.mean(values * weighted, axis=-1, keepdims=True)
    backward = scale * weighted - values * (scale * scale * scale) * row_inner
    return (backward, jnp.sum(values * scale * incoming, axis=0))


def rope_at(places):
    half_dim = HEAD_DIM // 2
    inverse = rope_base ** (-(jnp.arange(half_dim, dtype=jnp.float32) * 2.0) / HEAD_DIM)
    angles = places.astype(jnp.float32)[:, None, None] * inverse[None, None, :]
    return (jnp.cos(angles), jnp.sin(angles))


def rope_tables(count, length):
    return rope_at(jnp.arange(count, dtype=jnp.int32) % length)


def rotate(values, cosine, sine):
    half_dim = values.shape[-1] // 2
    lower_half = values[..., :half_dim]
    upper_half = values[..., half_dim:]
    return jnp.concatenate(
        [lower_half * cosine - upper_half * sine, upper_half * cosine + lower_half * sine], axis=-1
    )


def unrotate(grads, cosine, sine):
    half_dim = grads.shape[-1] // 2
    lower_half = grads[..., :half_dim]
    upper_half = grads[..., half_dim:]
    return jnp.concatenate(
        [lower_half * cosine + upper_half * sine, upper_half * cosine - lower_half * sine], axis=-1
    )


def piece_ids(starts, length):
    places = jnp.arange(length, dtype=jnp.int32)
    inside = (places[None, :, None] >= starts[:, None, :]) & (
        places[None, :, None] < starts[:, None, :] + PIECE
    )
    labels = jnp.arange(1, starts.shape[1] + 1, dtype=jnp.int32)
    return jnp.sum(jnp.where(inside, labels, 0), axis=2)


def visible(piece_id, offset, count):
    length = piece_id.shape[0]
    query_place = offset + jnp.arange(count, dtype=jnp.int32)
    key_place = jnp.arange(length, dtype=jnp.int32)
    query_ids = piece_id[offset : offset + count]
    return (key_place[None, :] <= query_place[:, None]) | (
        query_ids[:, None] == piece_id[None, :]
    ) & (query_ids[:, None] > 0)


def block_scores(queries, key_vecs, piece_id, offset, count):
    attn_scale = 1.0 / math.sqrt(queries.shape[-1])
    q_block = queries[offset : offset + count]
    scores = (
        jnp.einsum("qhd,khd->hqk", q_block, key_vecs, preferred_element_type=jnp.float32)
        * attn_scale
    )
    return (jnp.where(visible(piece_id, offset, count)[None], scores, masked), q_block)


def attend_one(seq_items):
    queries, key_vecs, values, piece_id = seq_items
    length = queries.shape[0]
    block_rows = min(512, length)
    outputs = []
    log_totals = []
    for offset in range(0, length, block_rows):
        logits, q_block = block_scores(queries, key_vecs, piece_id, offset, block_rows)
        row_max = jnp.max(logits, axis=-1, keepdims=True)
        log_total = row_max + jnp.log(jnp.sum(jnp.exp(logits - row_max), axis=-1, keepdims=True))
        probs = jnp.exp(logits - log_total).astype(jnp.bfloat16)
        mixed = jnp.einsum("hqk,khd->qhd", probs, values, preferred_element_type=jnp.float32)
        outputs.append(mixed.astype(jnp.bfloat16))
        log_totals.append(log_total)
    return (jnp.concatenate(outputs, axis=0), jnp.concatenate(log_totals, axis=1))


def attend_back(seq_items):
    queries, key_vecs, values, piece_id, log_totals, grad_mixed = seq_items
    length = queries.shape[0]
    block_rows = min(512, length)
    attn_scale = 1.0 / math.sqrt(queries.shape[-1])
    grad_keys = jnp.zeros(key_vecs.shape, jnp.float32)
    grad_values = jnp.zeros(values.shape, jnp.float32)
    grad_queries = []
    for offset in range(0, length, block_rows):
        logits, q_block = block_scores(queries, key_vecs, piece_id, offset, block_rows)
        probs = jnp.exp(logits - log_totals[:, offset : offset + block_rows])
        grad_block = grad_mixed[offset : offset + block_rows]
        grad_values = grad_values + jnp.einsum(
            "hqk,qhd->khd",
            probs.astype(jnp.bfloat16),
            grad_block,
            preferred_element_type=jnp.float32,
        )
        grad_probs = jnp.einsum(
            "qhd,khd->hqk", grad_block, values, preferred_element_type=jnp.float32
        )
        row_inner = jnp.sum(probs * grad_probs, axis=-1, keepdims=True)
        grad_scores = (probs * (grad_probs - row_inner) * attn_scale).astype(jnp.bfloat16)
        grad_queries.append(
            jnp.einsum("hqk,khd->qhd", grad_scores, key_vecs, preferred_element_type=jnp.float32)
        )
        grad_keys = grad_keys + jnp.einsum(
            "hqk,qhd->khd", grad_scores, q_block, preferred_element_type=jnp.float32
        )
    return (jnp.concatenate(grad_queries, axis=0), grad_keys, grad_values)


def times_trans(left, right):
    return lax.dot_general(
        left, right, (((1,), (1,)), ((), ())), preferred_element_type=jnp.float32
    )


def trans_times(left, right):
    return lax.dot_general(
        left, right, (((0,), (0,)), ((), ())), preferred_element_type=jnp.float32
    )


def fetch_weights(shards):
    gathered = (
        lax.all_gather(shards[0], "dp", axis=0, tiled=True),
        lax.all_gather(shards[1], "dp", axis=0, tiled=True),
        lax.all_gather(shards[2], "dp", axis=0, tiled=True),
        lax.all_gather(shards[3], "dp", axis=1, tiled=True),
        lax.all_gather(shards[4], "dp", axis=0, tiled=True),
        lax.all_gather(shards[5], "dp", axis=0, tiled=True),
        lax.all_gather(shards[6], "dp", axis=1, tiled=True),
        lax.all_gather(shards[7], "dp", axis=1, tiled=True),
    )
    return gathered


def gather_rows(normed):
    return lax.all_gather(normed, "tensor", axis=0, tiled=True)


def sum_rows(sum_terms):
    return lax.psum_scatter(sum_terms, "tensor", scatter_dimension=0, tiled=True)


def gather_grads(grad_terms):
    return lax.all_gather(grad_terms, "tensor", axis=0, tiled=True)


def sum_grads(grad_terms):
    return lax.psum_scatter(
        grad_terms.astype(jnp.bfloat16), "tensor", scatter_dimension=0, tiled=True
    ).astype(jnp.float32)


def by_sequence(values, seq_count):
    return values.reshape(seq_count, values.shape[0] // seq_count, values.shape[1], values.shape[2])


def attention_part(normed, gathered, cosine, sine, piece_id):
    whole_rows = gather_rows(normed)
    group_rows = whole_rows.shape[0]
    seq_count = piece_id.shape[0]

    def project(weight):
        return jnp.dot(whole_rows, weight, preferred_element_type=jnp.float32).reshape(
            group_rows, -1, HEAD_DIM
        )

    queries = rotate(project(gathered[0]), cosine, sine).astype(jnp.bfloat16)
    key_vecs = rotate(project(gathered[1]), cosine, sine).astype(jnp.bfloat16)
    values = project(gathered[2]).astype(jnp.bfloat16)
    outputs, log_totals = lax.map(
        attend_one,
        (
            by_sequence(queries, seq_count),
            by_sequence(key_vecs, seq_count),
            by_sequence(values, seq_count),
            piece_id,
        ),
    )
    return (whole_rows, queries, key_vecs, values, outputs.reshape(group_rows, -1), log_totals)


def feed_part(normed, gathered):
    whole_rows = gather_rows(normed)
    gate_pre = jnp.dot(whole_rows, gathered[4], preferred_element_type=jnp.float32)
    up_pre = jnp.dot(whole_rows, gathered[5], preferred_element_type=jnp.float32)
    hidden = (jax.nn.silu(gate_pre) * up_pre).astype(jnp.bfloat16)
    return (whole_rows, gate_pre, up_pre, hidden)


def on_device(
    tokens,
    query_weight,
    key_weight,
    value_weight,
    out_weight,
    gate_weight,
    up_weight,
    down_weight,
    gain_attn_in,
    gain_attn_out,
    gain_ff_in,
    gain_ff_out,
    piece_starts,
    out_grad,
):
    shards = (
        query_weight,
        key_weight,
        value_weight,
        out_weight,
        gate_weight,
        up_weight,
        down_weight,
        jnp.stack([gain_attn_in, gain_attn_out, gain_ff_in, gain_ff_out]),
    )
    gathered = fetch_weights(shards)
    gain_rows = gathered[7].astype(jnp.float32)
    tok_rows = tokens.astype(jnp.float32)
    seq_count = piece_starts.shape[0]
    own_rows = tokens.shape[0]
    group_rows = own_rows * lax.axis_size("tensor")
    length = group_rows // seq_count
    piece_id = piece_ids(piece_starts, length)
    incoming = out_grad.astype(jnp.float32)
    scale_in = rms_scale(tok_rows)
    normed_in = (tok_rows * scale_in * gain_rows[0]).astype(jnp.bfloat16)
    cosine, sine = rope_tables(group_rows, length)
    attn_parts = attention_part(normed_in, gathered, cosine, sine, piece_id)
    branch_attn = sum_rows(jnp.dot(attn_parts[4], gathered[3], preferred_element_type=jnp.float32))
    scale_attn = rms_scale(branch_attn)
    mid_rows = tok_rows + branch_attn * scale_attn * gain_rows[1]
    scale_mid = rms_scale(mid_rows)
    normed_ff = (mid_rows * scale_mid * gain_rows[2]).astype(jnp.bfloat16)
    feed_parts = feed_part(normed_ff, gathered)
    branch_ff = sum_rows(jnp.dot(feed_parts[3], gathered[6], preferred_element_type=jnp.float32))
    scale_ff = rms_scale(branch_ff)
    result = (mid_rows + branch_ff * scale_ff * gain_rows[3]).astype(jnp.bfloat16)
    gathered = fetch_weights(shards)
    feed_parts = feed_part(normed_ff, gathered)
    whole_ff, gate_pre, up_pre, hidden = feed_parts
    back_ff, gain_grad_ff_out = norm_back(branch_ff, scale_ff, gain_rows[3], incoming)
    wide_back_ff = gather_grads(back_ff.astype(jnp.bfloat16))
    grad_down = trans_times(hidden, wide_back_ff)
    back_hidden = times_trans(wide_back_ff, gathered[6])
    sigmoid_gate = jax.nn.sigmoid(gate_pre)
    back_gate = (
        back_hidden * up_pre * sigmoid_gate * (1.0 + gate_pre * (1.0 - sigmoid_gate))
    ).astype(jnp.bfloat16)
    back_up = (back_hidden * gate_pre * sigmoid_gate).astype(jnp.bfloat16)
    grad_gate = trans_times(whole_ff, back_gate)
    grad_up = trans_times(whole_ff, back_up)
    back_normed_ff = sum_grads(
        times_trans(back_gate, gathered[4]) + times_trans(back_up, gathered[5])
    )
    back_from_ff, gain_grad_ff_in = norm_back(mid_rows, scale_mid, gain_rows[2], back_normed_ff)
    back_mid = incoming + back_from_ff
    back_attn, gain_grad_attn_out = norm_back(branch_attn, scale_attn, gain_rows[1], back_mid)
    wide_back_attn = gather_grads(back_attn.astype(jnp.bfloat16))
    attn_parts = attention_part(normed_in, gathered, cosine, sine, piece_id)
    whole_in, queries, key_vecs, values, attended, log_totals = attn_parts
    grad_out = trans_times(attended, wide_back_attn)
    back_attended = times_trans(wide_back_attn, gathered[3]).astype(jnp.bfloat16)
    back_queries, back_keys, back_values = lax.map(
        attend_back,
        (
            by_sequence(queries, seq_count),
            by_sequence(key_vecs, seq_count),
            by_sequence(values, seq_count),
            piece_id,
            log_totals,
            by_sequence(back_attended.reshape(group_rows, -1, HEAD_DIM), seq_count),
        ),
    )
    back_queries = (
        unrotate(back_queries.reshape(group_rows, -1, HEAD_DIM), cosine, sine)
        .reshape(group_rows, -1)
        .astype(jnp.bfloat16)
    )
    back_keys = (
        unrotate(back_keys.reshape(group_rows, -1, HEAD_DIM), cosine, sine)
        .reshape(group_rows, -1)
        .astype(jnp.bfloat16)
    )
    back_values = back_values.reshape(group_rows, -1).astype(jnp.bfloat16)
    grad_query = trans_times(whole_in, back_queries)
    grad_key = trans_times(whole_in, back_keys)
    grad_value = trans_times(whole_in, back_values)
    back_normed_in = sum_grads(
        times_trans(back_queries, gathered[0])
        + times_trans(back_keys, gathered[1])
        + times_trans(back_values, gathered[2])
    )
    back_from_in, gain_grad_attn_in = norm_back(tok_rows, scale_in, gain_rows[0], back_normed_in)
    input_grad = back_mid + back_from_in
    weight_terms = (grad_query, grad_key, grad_value, grad_out, grad_gate, grad_up, grad_down)
    gain_grads = lax.psum(
        jnp.stack([gain_grad_attn_in, gain_grad_attn_out, gain_grad_ff_in, gain_grad_ff_out]),
        "tensor",
    )
    grad_sums = (
        lax.psum_scatter(
            weight_terms[0].astype(jnp.bfloat16), "dp", scatter_dimension=0, tiled=True
        ).astype(jnp.float32),
        lax.psum_scatter(
            weight_terms[1].astype(jnp.bfloat16), "dp", scatter_dimension=0, tiled=True
        ).astype(jnp.float32),
        lax.psum_scatter(
            weight_terms[2].astype(jnp.bfloat16), "dp", scatter_dimension=0, tiled=True
        ).astype(jnp.float32),
        lax.psum_scatter(
            weight_terms[3].astype(jnp.bfloat16), "dp", scatter_dimension=1, tiled=True
        ).astype(jnp.float32),
        lax.psum_scatter(
            weight_terms[4].astype(jnp.bfloat16), "dp", scatter_dimension=0, tiled=True
        ).astype(jnp.float32),
        lax.psum_scatter(
            weight_terms[5].astype(jnp.bfloat16), "dp", scatter_dimension=0, tiled=True
        ).astype(jnp.float32),
        lax.psum_scatter(
            weight_terms[6].astype(jnp.bfloat16), "dp", scatter_dimension=1, tiled=True
        ).astype(jnp.float32),
        lax.psum_scatter(
            gain_grads.astype(jnp.bfloat16), "dp", scatter_dimension=1, tiled=True
        ).astype(jnp.float32),
    )
    return (
        result,
        input_grad,
        grad_sums[0],
        grad_sums[1],
        grad_sums[2],
        grad_sums[3],
        grad_sums[4],
        grad_sums[5],
        grad_sums[6],
        grad_sums[7][0],
        grad_sums[7][1],
        grad_sums[7][2],
        grad_sums[7][3],
    )


LANES = 128
HALF = HEAD_DIM // 2
MESH = pl.DeviceIdType.MESH
GATHER_FIRST = (256, 384)
GATHER_DOWN = (512, 384, 256, 256)
REDUCE_DOWN = (512, 512)
REDUCE_LAST = (256, 256)
GATHER_LATE = 2
LATE_STEP = 0
REDUCE_LATE = 0
LATE_SLOTS = (0, 1, 6, 7, 8)
X_FIRST = (1, 2)
X_FIRST_SUM = (2, 2, 2, 2, 2, 2, 2, 2, 1, 1, 1, 1, 1, 1, 1, 1, 1, 1, 1, 1)
PACE = (1, 2, 3, 4, 5, 6, 7, 8, 9, 10, 11, 11, 12)
TOKEN_PIECES = 8
TOKENS_EARLY = 4
TOKENS_A_STEP = 1
f32 = jnp.float32
bf16 = jnp.bfloat16


class Plan:
    def __init__(self, rows, width, head_cols, ff_cols, shard_rows):
        self.rows = rows
        self.width = width
        self.head_cols = head_cols
        self.ff_cols = ff_cols
        self.shard_rows = shard_rows
        self.heads = 2 * head_cols // HEAD_DIM
        self.k_at = LANES
        self.v_at = self.k_at + head_cols
        self.q_at = self.v_at + head_cols
        self.o_at = self.q_at + head_cols
        self.gu_at = self.o_at + head_cols
        self.d_at = self.gu_at + 2 * ff_cols
        self.cols = self.d_at + ff_cols
        self.kvq = 3 * head_cols

        def cuts(start, total, sizes=()):
            pieces = []
            while total > 0:
                size = min(sizes[len(pieces)] if len(pieces) < len(sizes) else 512, total)
                pieces.append((start, size))
                start, total = start + size, total - size
            return pieces

        gu_cuts = cuts(self.gu_at, 2 * ff_cols)
        self.gather = (
            cuts(0, self.v_at, GATHER_FIRST)
            + [(self.v_at, head_cols), (self.q_at, head_cols), (self.o_at, head_cols)]
            + gu_cuts
            + cuts(self.d_at, ff_cols, GATHER_DOWN)
        )
        self.d_cuts = cuts(self.d_at, ff_cols, REDUCE_DOWN)
        self.gu_cuts = gu_cuts
        self.reduce = (
            self.d_cuts
            + self.gu_cuts
            + [(self.o_at, head_cols), (self.q_at, head_cols), (self.v_at, head_cols)]
            + cuts(self.k_at, head_cols, REDUCE_LAST)
            + [(0, LANES)]
        )
        down = len(self.gather) - len(cuts(self.d_at, ff_cols, GATHER_DOWN))
        self.gather_late = list(range(down, down + GATHER_LATE))
        self.gather_early = [k for k in range(len(self.gather)) if k not in self.gather_late]
        self.reduce_late = set(range(REDUCE_LATE))

    def held(self, at):
        early = [i + 3 for i, k in enumerate(self.gather_early) if self.gather[k][0] < at]
        late = [len(self.gather_early) + LATE_STEP + 1 for k in self.gather_late if self.gather[k][0] < at]
        return max(early + late + [0])

    def split(self, k):
        return X_FIRST[k % len(X_FIRST)]

    def split_sum(self, j):
        return X_FIRST_SUM[j % len(X_FIRST_SUM)]


def sigmoid(v):
    return 0.5 * jnp.tanh(0.5 * v) + 0.5


def dot_nn(left, right):
    return lax.dot_general(left, right, (((1,), (0,)), ((), ())), preferred_element_type=f32)


def dot_nt(left, right):
    return lax.dot_general(left, right, (((1,), (1,)), ((), ())), preferred_element_type=f32)


def dot_tn(left, right):
    return lax.dot_general(left, right, (((0,), (0,)), ((), ())), preferred_element_type=f32)


def fused_layer(
    plan,
    k_hbm, v_hbm, q_hbm, g_hbm, u_hbm, o_hbm, d_hbm, gain_shard, tok_hbm, og_hbm, starts_ref, inverse_ref,
    out_hbm, ig_hbm, gr_hbm,
    W, KVQ, KVp, xo, xp, T, att, ba, mid, bff, nf, GU, HID, BF, TB, LO, MK, gains, dgains, stat_a, stat_b, DQ, cos_ref, sin_ref,
    R1, R2A, R2B, R3A, R3B, R4, RQ1, RQ2, RQ3, ST,
    ag_s, ag_r, rs_s, rs_r, loc, pack_sem, extra_s, extra_r, credit,
):
    p = plan
    dp = lax.axis_index("dp")
    y = lax.axis_index("tensor")
    c = lax.rem(dp, 2)
    x = lax.rem(dp // 2, 2)
    z = dp // 4
    rows, width, hc, ff = p.rows, p.width, p.head_cols, p.ff_cols
    first = y == 0
    second = y == 1

    def dev(zz, xx, cc, yy):
        return (zz * 4 + xx * 2 + cc, yy)

    def up(step):
        return lax.rem(z + step, 4)

    core_peer = dev(z, x, 1 - c, y)
    x_peer = dev(z, 1 - x, c, y)
    y_peer = dev(z, x, c, 1 - y)
    z_peers = [dev(up(d), x, c, y) for d in (1, 2, 3)]
    z_sources = [dev(up(4 - d), x, c, y) for d in (1, 2, 3)]

    def remote(src, dst, send, recv, to):
        return pltpu.make_async_remote_copy(
            src_ref=src, dst_ref=dst, send_sem=send, recv_sem=recv, device_id=to, device_id_type=MESH
        )

    def cut(at, size):
        return pl.ds(at if isinstance(at, int) else pl.multiple_of(at, LANES), size)

    def weight(yy, at, size, zz=None):
        if zz is None:
            return W[yy, :, :, :, :, cut(at, size)].reshape(width, size)
        return W[yy, zz, :, :, :, cut(at, size)].reshape(width // 4, size)

    def put_weight(yy, at, size, value):
        W[yy, :, :, :, :, cut(at, size)] = value.astype(bf16).reshape(4, 2, 2, p.shard_rows, size)

    def rms(v):
        return lax.rsqrt(jnp.mean(v * v, axis=-1, keepdims=True) + norm_eps)

    def norm_grad(v, scale, gain, e):
        weighted = gain * e
        inner = jnp.mean(v * weighted, axis=-1, keepdims=True)
        return scale * weighted - v * (scale * scale * scale) * inner

    def by_rows(body, size=64):
        def step(i, carry):
            body(pl.ds(pl.multiple_of(i * size, size), size))
            return carry

        lax.fori_loop(0, rows // size, step, 0)

    def loop(count, body):
        def step(i, carry):
            body(i)
            return carry

        lax.fori_loop(0, count, step, 0)

    own_w = W.at[y, z, x, c]

    def ag(k, m):
        at, size = p.gather[k]
        cols = pl.ds(at, size)
        sem = (ag_s.at[k, m], ag_r.at[k, m])
        if k in p.gather_late:
            half = size // 2 // LANES * LANES
            cols_a, cols_b = pl.ds(at, half), pl.ds(at + half, size - half)
            if m < 3:
                ref = W.at[:, z, :, c, :, cols]
                return remote(ref, ref, *sem, z_peers[m])
            if m == 3:
                return remote(own_w.at[:, cols_a], W.at[y, z, x, c, :, cols_a], *sem, x_peer)
            if m == 4:
                return remote(own_w.at[:, cols_b], W.at[y, z, x, c, :, cols_b], *sem, y_peer)
            if m == 5:
                ref = W.at[y, z, :, c, :, cols_a]
                return remote(ref, ref, *sem, y_peer)
            if m == 6:
                ref = W.at[:, z, x, c, :, cols_b]
                return remote(ref, ref, *sem, x_peer)
        low, high = pl.ds(0, p.split(k)), pl.ds(p.split(k), 4 - p.split(k))
        if m < 3:
            return remote(own_w.at[:, cols], W.at[y, z, x, c, :, cols], *sem, z_peers[m])
        if m == 3:
            ref = W.at[y, low, x, c, :, cols]
            return remote(ref, ref, *sem, x_peer)
        if m == 4:
            ref = W.at[y, high, x, c, :, cols]
            return remote(ref, ref, *sem, y_peer)
        if m == 5:
            ref = W.at[y, low, :, c, :, cols]
            return remote(ref, ref, *sem, y_peer)
        if m == 6:
            ref = W.at[:, high, x, c, :, cols]
            return remote(ref, ref, *sem, x_peer)
        ref = W.at[:, :, :, c, :, cols]
        return remote(ref, ref, *sem, core_peer)

    n_gather = len(p.gather)
    n_early = len(p.gather_early)

    def ag_step(s):
        def early(i):
            return p.gather_early[i] if 0 <= i < n_early else None

        k = early(s)
        if k is not None:
            for m in (0, 1, 2):
                ag(k, m).wait_recv()
            ag(k, 3).start()
            ag(k, 4).start()
        k = early(s - 1)
        if k is not None:
            ag(k, 3).wait_recv()
            ag(k, 5).start()
            ag(k, 4).wait_recv()
            ag(k, 6).start()
        k = early(s - 2)
        if k is not None:
            ag(k, 5).wait_recv()
            ag(k, 6).wait_recv()
            ag(k, 7).start()
        k = early(s - 3)
        if k is not None:
            ag(k, 7).wait_recv()
        if s == n_early + LATE_STEP:
            for k in p.gather_late:
                for m in (0, 1, 2):
                    ag(k, m).wait_recv()
                ag(k, 7).start()
        if s == n_early + LATE_STEP + 1:
            for k in p.gather_late:
                ag(k, 7).wait_recv()

    steps = [0]

    def tok_piece(i):
        blk = pl.ds(i * (rows // TOKEN_PIECES), rows // TOKEN_PIECES)
        return remote(tok_hbm.at[blk, :], xp.at[blk, :], extra_s.at[1 + i], extra_r.at[1 + i], y_peer)

    def tok_send(i):
        @pl.when(first)
        def _():
            tok_piece(i).start()

    def ag_until(at, more=0):
        goal = max(p.held(at), steps[0] + more - 1)
        while steps[0] <= goal:
            ag_step(steps[0])
            for i in range(TOKENS_EARLY, TOKEN_PIECES):
                if (i - TOKENS_EARLY) // TOKENS_A_STEP == steps[0]:
                    tok_send(i)
            steps[0] += 1
            if steps[0] == 1:
                ag_late_turn()
            if steps[0] == 5:
                ag_late_z()

    def ag_late_turn():
        for k in p.gather_late:
            ag(k, 3).wait_recv()
            ag(k, 5).start()
            ag(k, 4).wait_recv()
            ag(k, 6).start()

    def ag_late_z():
        for k in p.gather_late:
            ag(k, 5).wait_recv()
            ag(k, 6).wait_recv()
            for m in (0, 1, 2):
                ag(k, m).start()

    load_tok = pltpu.make_async_copy(tok_hbm, TB, loc.at[0])
    load_tok.start()
    packing = []
    for src, at, size in (
        (k_hbm, p.k_at, hc), (v_hbm, p.v_at, hc), (q_hbm, p.q_at, hc), (o_hbm, p.o_at, hc), (d_hbm, p.d_at, ff)
    ):
        packing.append((src, own_w.at[:, pl.ds(at, size)]))
    for t in range(ff // LANES):
        for n, src in enumerate((g_hbm, u_hbm)):
            to = own_w.at[:, pl.ds(p.gu_at + (2 * t + n) * LANES, LANES)]
            packing.append((src.at[:, pl.ds(t * LANES, LANES)], to))
    packing = [pltpu.make_async_copy(src, to, pack_sem.at[i]) for i, (src, to) in enumerate(packing)]
    for copy in packing:
        copy.start()
    barrier = pltpu.get_barrier_semaphore()
    for peer in [core_peer, x_peer, y_peer] + z_peers:
        pl.semaphore_signal(barrier, inc=1, device_id=peer, device_id_type=MESH)
    count = gain_shard.shape[0]
    spread = jnp.concatenate([gain_shard[...], jnp.zeros((LANES - count, p.shard_rows), f32)], axis=0)
    W[y, z, x, c, :, pl.ds(0, LANES)] = jnp.transpose(spread).astype(bf16)
    for copy in packing:
        copy.wait()
    pl.semaphore_wait(barrier, 6)

    for k in p.gather_late:
        ag(k, 3).start()
        ag(k, 4).start()

    for k in p.gather_early:
        for m in (0, 1, 2):
            ag(k, m).start()
    for i in range(TOKENS_EARLY):
        tok_send(i)
    load_tok.wait()

    def tables(i):
        blk = pl.ds(pl.multiple_of(i * 64, 64), 64)
        place = (lax.broadcasted_iota(jnp.int32, (64, LANES), 0) + i * 64).astype(f32)
        angle = place * inverse_ref[...]
        cos_ref[blk, :] = jnp.cos(angle)
        turned = jnp.sin(angle)
        sin_ref[blk, :] = jnp.where(lax.broadcasted_iota(jnp.int32, (64, LANES), 1) < HALF, -turned, turned)

    loop(2 * rows // 64, tables)

    start = starts_ref[0, y] - y * rows

    def build_mask(query_dim):
        def body(blk):
            shape = (64, rows)
            r = lax.broadcasted_iota(jnp.int32, shape, 0) + blk.start
            s = lax.broadcasted_iota(jnp.int32, shape, 1)
            q_pos, k_pos = (r, s) if query_dim == 0 else (s, r)
            inside = (r >= start) & (r < start + PIECE) & (s >= start) & (s < start + PIECE)
            MK[blk, :] = jnp.where((k_pos <= q_pos) | inside, 0.0, masked)

        by_rows(body)

    build_mask(0)
    dgains[...] = jnp.zeros_like(dgains)

    ag_until(LANES)
    gains[0:8, 0:width] = jnp.transpose(weight(0, 0, LANES).astype(f32))[0:8, :]

    def norm_in(src, dst):
        def body(blk):
            t = src[blk, :].astype(f32)
            dst[blk, :] = (t * rms(t) * gains[0:1, :]).astype(bf16)

        by_rows(body)

    norm_in(TB, xo)

    def rotated(u, place, sign):
        return u * cos_ref[place, :] + sign * (pltpu.roll(u, HALF, 1) * sin_ref[place, :])

    def project(src, dst, at, place, turn):
        def run(yy, off):
            r = dot_nn(src[...], weight(yy, LANES + off, 256))
            for hh in range(2):
                u = r[:, hh * HEAD_DIM : (hh + 1) * HEAD_DIM]
                if turn:
                    u = rotated(u, place, 1.0)
                dst[yy, :, cut(off + hh * HEAD_DIM, HEAD_DIM)] = u.astype(bf16)

        per = hc // 256
        loop(2 * per, lambda i: run(i // per, pl.multiple_of(at + lax.rem(i, per) * 256, 256)))

    own_place = pl.ds(pl.multiple_of(y * rows, rows), rows)
    old_place = pl.ds(0, rows)
    ag_until(p.v_at)
    project(xo, KVQ, 0, own_place, True)
    ag_until(p.q_at)
    project(xo, KVQ, hc, own_place, False)

    @pl.when(second)
    def _():
        for i in range(TOKEN_PIECES):
            tok_piece(i).wait_recv()
        norm_in(xp, xp)

    ag_until(p.o_at)
    project(xo, KVQ, 2 * hc, own_place, True)

    @pl.when(second)
    def _():
        project(xp, KVp, 0, old_place, True)

    ag_until(p.gu_at)

    @pl.when(second)
    def _():
        project(xp, KVp, hc, old_place, False)

    ag_until(0, 1)

    per_y = hc // HEAD_DIM
    attn_scale = 1.0 / math.sqrt(HEAD_DIM)
    log2_scale = attn_scale * math.log2(math.e)
    lane = lax.broadcasted_iota(jnp.int32, (1, LANES), 1)

    def head_at(h):
        yy = h // per_y
        off = pl.multiple_of(lax.rem(h, per_y) * HEAD_DIM, HEAD_DIM)
        return yy, cut(off, HEAD_DIM), cut(off + hc, HEAD_DIM), cut(off + 2 * hc, HEAD_DIM)

    def attend(i, both):
        h = i // 2
        blk = pl.ds(pl.multiple_of(lax.rem(i, 2) * (rows // 2), rows // 2), rows // 2)
        yy, k_at, v_at, q_at = head_at(h)
        q = KVQ[yy, blk, q_at]
        s = dot_nt(q, KVQ[yy, :, k_at]) * log2_scale + MK[blk, :]
        top = jnp.max(s, axis=-1, keepdims=True)
        if both:
            s_old = dot_nt(q, KVp[yy, :, k_at]) * log2_scale
            top = jnp.maximum(top, jnp.max(s_old, axis=-1, keepdims=True))
        e = jnp.exp2(s - top)
        total = jnp.sum(e, axis=-1, keepdims=True)
        if both:
            e_old = jnp.exp2(s_old - top)
            total = total + jnp.sum(e_old, axis=-1, keepdims=True)
        inv = 1.0 / total
        o = dot_nn((e * inv).astype(bf16), KVQ[yy, :, v_at])
        if both:
            o = o + dot_nn((e_old * inv).astype(bf16), KVp[yy, :, v_at])
        att[blk, pl.ds(pl.multiple_of(h * HEAD_DIM, HEAD_DIM), HEAD_DIM)] = o.astype(bf16)
        stat = top + jnp.log2(total)
        stat_a[blk, :] = jnp.where(lane == h, stat, stat_a[blk, :])

    def attend_heads(lo, hi):
        @pl.when(first)
        def _():
            loop(2 * (hi - lo), lambda i: attend(i + 2 * lo, False))

        @pl.when(second)
        def _():
            loop(2 * (hi - lo), lambda i: attend(i + 2 * lo, True))

    stat_a[...] = jnp.zeros_like(stat_a)
    for h in range(0, p.heads, 2):
        attend_heads(h, h + 2)
        ag_until(0, 1)


    def o_proj(zz):
        cols = pl.ds(pl.multiple_of(zz * (width // 4), width // 4), width // 4)
        ba[:, cols] = dot_nt(att[:, 0:hc], weight(0, p.o_at, hc, zz)) + dot_nt(
            att[:, hc : 2 * hc], weight(1, p.o_at, hc, zz)
        )

    loop(4, o_proj)

    def mid_rows(blk):
        b = ba[blk, :]
        m = TB[blk, :].astype(f32) + b * rms(b) * gains[1:2, :]
        mid[blk, :] = m
        nf[blk, :] = (m * rms(m) * gains[2:3, :]).astype(bf16)

    by_rows(mid_rows)
    load_og = pltpu.make_async_copy(og_hbm, TB, loc.at[0])
    load_og.start()

    def gate_up(lo, hi):
        def run(i):
            yy = i // (hi - lo)
            t = lax.rem(i, hi - lo) + lo
            off = pl.multiple_of(t * 256, 256)
            r = dot_nn(nf[...], weight(yy, p.gu_at + off, 256))
            g, u = r[:, 0:LANES], r[:, LANES:256]
            GU[yy, :, pl.ds(off, 256)] = r.astype(bf16)
            HID[yy, :, pl.ds(pl.multiple_of(t * LANES, LANES), LANES)] = (
                g * sigmoid(g) * u
            ).astype(bf16)

        loop(2 * (hi - lo), run)

    ag_until(0, 1)
    tiles = 2 * ff // 256
    for lo in range(0, tiles, 2):
        hi = min(lo + 2, tiles)
        ag_until(p.gu_at + hi * 256)
        gate_up(lo, hi)

    def down_proj(lo, hi, more):
        def run(zz):
            cols = pl.ds(pl.multiple_of(zz * (width // 4), width // 4), width // 4)
            acc = dot_nt(HID[0, :, lo:hi], weight(0, p.d_at + lo, hi - lo, zz)) + dot_nt(
                HID[1, :, lo:hi], weight(1, p.d_at + lo, hi - lo, zz)
            )
            bff[:, cols] = bff[:, cols] + acc if more else acc

        loop(4, run)

    ready = 0
    for n, (at, size) in enumerate(p.gather[p.gather_late[0] :]):
        if n >= GATHER_LATE - 1:
            ag_until(at + size)
            down_proj(ready, at + size - p.d_at, ready > 0)
            ready = at + size - p.d_at

    load_og.wait()

    def out_rows(blk):
        b = bff[blk, :]
        scale = rms(b)
        e = TB[blk, :].astype(f32)
        LO[blk, :] = (mid[blk, :] + b * scale * gains[3:4, :]).astype(bf16)
        BF[blk, :] = norm_grad(b, scale, gains[3:4, :], e).astype(bf16)
        dgains[3:4, :] += jnp.sum(b * scale * e, axis=0, keepdims=True)

    by_rows(out_rows)
    put_out = pltpu.make_async_copy(LO, out_hbm, loc.at[1])
    put_out.start()

    for k in range(n_gather):
        for m in range(8):
            ag(k, m).wait_send()

    n_reduce = len(p.reduce)

    def rs_parts(j):
        at, size = p.reduce[j]
        half = size // 2 // LANES * LANES
        return (pl.ds(at, half), pl.ds(0, half)), (pl.ds(at + half, size - half), pl.ds(half, size - half))

    def rs(j, m):
        at, size = p.reduce[j]
        cols, slot, part = pl.ds(at, size), j % 2, pl.ds(0, size)
        sem = (rs_s.at[j, m], rs_r.at[j, m])
        if m == 0:
            return remote(W.at[:, :, :, 1 - c, :, cols], R1.at[slot, :, :, :, :, part], *sem, core_peer)
        d = m - 5
        if j in p.reduce_late:
            (cols_a, part_a), (cols_b, part_b) = rs_parts(j)
            if m == 1:
                return remote(W.at[1 - y, z, :, c, :, cols_a], RQ2.at[j, :, :, part_a], *sem, y_peer)
            if m == 2:
                return remote(W.at[:, z, 1 - x, c, :, cols_b], RQ2.at[j, :, :, part_b], *sem, x_peer)
            if m == 3:
                return remote(W.at[y, z, 1 - x, c, :, cols_a], RQ3.at[j, :, part_a], *sem, x_peer)
            if m == 4:
                return remote(W.at[1 - y, z, x, c, :, cols_b], RQ3.at[j, :, part_b], *sem, y_peer)
            return remote(W.at[:, up(d + 1), :, c, :, cols], RQ1.at[j, d, :, :, :, part], *sem, z_peers[d])
        low, high = pl.ds(0, p.split_sum(j)), pl.ds(p.split_sum(j), 4 - p.split_sum(j))
        if m == 1:
            return remote(W.at[1 - y, low, :, c, :, cols], R2A.at[slot, low, :, :, part], *sem, y_peer)
        if m == 2:
            return remote(W.at[:, high, 1 - x, c, :, cols], R2B.at[slot, :, pl.ds(0, 4 - p.split_sum(j)), :, part], *sem, x_peer)
        if m == 3:
            return remote(W.at[y, low, 1 - x, c, :, cols], R3A.at[slot, low, :, part], *sem, x_peer)
        if m == 4:
            return remote(W.at[1 - y, high, x, c, :, cols], R3B.at[slot, pl.ds(0, 4 - p.split_sum(j)), :, part], *sem, y_peer)
        return remote(W.at[y, up(d + 1), x, c, :, cols], R4.at[slot, d, :, part], *sem, z_peers[d])

    rs_sources = [core_peer, y_peer, x_peer, x_peer, y_peer] + z_sources
    n_late = len(p.reduce_late)

    def rs_first(m):
        return 2 if m == 0 else n_late + 2

    def rs_start(j, m):
        if j >= rs_first(m):
            pl.semaphore_wait(credit.at[m], 1)
        rs(j, m).start()

    def rs_used(j, m):
        if j + 2 < n_reduce and j + 2 >= rs_first(m):
            pl.semaphore_signal(credit.at[m], inc=1, device_id=rs_sources[m], device_id_type=MESH)

    finished = []

    def put_sum(i):
        at, size = p.reduce[finished[i]]
        return pltpu.make_async_copy(
            ST.at[i % 2, :, pl.ds(0, size)], gr_hbm.at[:, pl.ds(at, size)], loc.at[2 + i % 2]
        )

    def finish(j, total):
        i = len(finished)
        finished.append(j)
        if i >= 2:
            put_sum(i - 2).wait()
        ST[i % 2, :, pl.ds(0, p.reduce[j][1])] = total
        put_sum(i).start()

    def rs_core(j):
        at, size = p.reduce[j]
        cols, slot, part = pl.ds(at, size), j % 2, pl.ds(0, size)
        rs(j, 0).wait_recv()

        def add(i):
            a, b, d = i // 8, lax.rem(i // 2, 4), lax.rem(i, 2)
            W[a, b, d, c, :, cols] = W[a, b, d, c, :, cols] + R1[slot, a, b, d, :, part]

        loop(16, add)
        rs_used(j, 0)

    def rs_late_event(j, phase):
        at, size = p.reduce[j]
        cols, part = pl.ds(at, size), pl.ds(0, size)
        (cols_a, part_a), (cols_b, part_b) = rs_parts(j)
        if phase == 0:
            rs_start(j, 0)
        elif phase == 1:
            rs_core(j)
            for m in (5, 6, 7):
                rs_start(j, m)
        elif phase == 2:
            for m in (5, 6, 7):
                rs(j, m).wait_recv()

            def add_q(i):
                a, b = i // 2, lax.rem(i, 2)
                total = W[a, z, b, c, :, cols].astype(f32)
                for d in range(3):
                    total = total + RQ1[j, d, a, b, :, part].astype(f32)
                W[a, z, b, c, :, cols] = total.astype(bf16)

            loop(4, add_q)
            rs_start(j, 1)
            rs_start(j, 2)
        elif phase == 3:
            rs(j, 1).wait_recv()
            rs(j, 2).wait_recv()
            for d in range(2):
                W[y, z, d, c, :, cols_a] = W[y, z, d, c, :, cols_a] + RQ2[j, d, :, part_a]
                W[d, z, x, c, :, cols_b] = W[d, z, x, c, :, cols_b] + RQ2[j, d, :, part_b]
            rs_start(j, 3)
            rs_start(j, 4)
        else:
            rs(j, 3).wait_recv()
            rs(j, 4).wait_recv()
            finish(j, W[y, z, x, c, :, cols].astype(f32) + RQ3[j, :, part].astype(f32))

    def rs_event(j, phase):
        if j in p.reduce_late:
            rs_late_event(j, phase)
            return
        at, size = p.reduce[j]
        cols, slot, part = pl.ds(at, size), j % 2, pl.ds(0, size)
        n_low = p.split_sum(j)
        n_high = 4 - n_low
        if phase == 0:
            rs_start(j, 0)
        elif phase == 1:
            rs_core(j)
            rs_start(j, 1)
            rs_start(j, 2)
        elif phase == 2:
            rs(j, 1).wait_recv()

            def add_a(i):
                b, d = i // 2, lax.rem(i, 2)
                W[y, b, d, c, :, cols] = W[y, b, d, c, :, cols] + R2A[slot, b, d, :, part]

            loop(2 * n_low, add_a)
            rs_used(j, 1)
            rs_start(j, 3)
            rs(j, 2).wait_recv()

            def add_b(i):
                a, b = i // n_high, lax.rem(i, n_high)
                W[a, b + n_low, x, c, :, cols] = W[a, b + n_low, x, c, :, cols] + R2B[slot, a, b, :, part]

            loop(2 * n_high, add_b)
            rs_used(j, 2)
            rs_start(j, 4)
        elif phase == 3:
            rs(j, 3).wait_recv()
            for b in range(n_low):
                W[y, b, x, c, :, cols] = W[y, b, x, c, :, cols] + R3A[slot, b, :, part]
            rs_used(j, 3)
            rs(j, 4).wait_recv()
            for b in range(n_high):
                W[y, b + n_low, x, c, :, cols] = W[y, b + n_low, x, c, :, cols] + R3B[slot, b, :, part]
            rs_used(j, 4)
            for m in (5, 6, 7):
                rs_start(j, m)
        else:
            for m in (5, 6, 7):
                rs(j, m).wait_recv()
            total = W[y, z, x, c, :, cols].astype(f32)
            for d in range(3):
                total = total + R4[slot, d, :, part].astype(f32)
            for m in (5, 6, 7):
                rs_used(j, m)
            finish(j, total)

    def slot_of(j, phase):
        return j + (LATE_SLOTS[phase] if j in p.reduce_late else phase)

    events = sorted(
        ((j, phase) for j in range(n_reduce) for phase in range(5)), key=lambda e: (slot_of(*e), -e[0], e[1])
    )
    pending = list(events)

    def pump(ready, until):
        blocked = set()
        for j, phase in list(pending):
            if slot_of(j, phase) >= until:
                break
            if j >= ready or j in blocked:
                blocked.add(j)
            else:
                rs_event(j, phase)
                pending.remove((j, phase))

    def back_tile(yy, t, bh):
        off = pl.multiple_of(t * 256, 256)
        g = GU[yy, :, pl.ds(off, LANES)].astype(f32)
        u = GU[yy, :, cut(off + LANES, LANES)].astype(f32)
        s = sigmoid(g)
        GU[yy, :, pl.ds(off, LANES)] = (bh * u * s * (1.0 + g * (1.0 - s))).astype(bf16)
        GU[yy, :, cut(off + LANES, LANES)] = (bh * g * s).astype(bf16)

    pairs = ff // 256

    def back_hidden(lo, hi):
        def run(i):
            yy, t = i // (hi - lo), lax.rem(i, hi - lo) + lo
            bh = dot_nn(BF[...], weight(yy, p.d_at + pl.multiple_of(t * 256, 256), 256))
            back_tile(yy, 2 * t, bh[:, 0:LANES])
            back_tile(yy, 2 * t + 1, bh[:, LANES:256])

        loop(2 * (hi - lo), run)

    def grad_down(lo, hi):
        def run(i):
            yy, off = i // (hi - lo), pl.multiple_of((lax.rem(i, hi - lo) + lo) * 256, 256)
            put_weight(yy, p.d_at + off, 256, dot_nn(T[...], HID[yy, :, pl.ds(off, 256)]))

        loop(2 * (hi - lo), run)

    def back_hidden_last(yy):
        bh = dot_nn(BF[...], weight(yy, p.d_at + pairs * 256, LANES))
        back_tile(yy, jnp.int32(2 * pairs), bh)

    def grad_down_last(yy):
        put_weight(yy, p.d_at + pairs * 256, LANES, dot_nn(T[...], HID[yy, :, pl.ds(pairs * 256, LANES)]))

    n_d = len(p.d_cuts)
    n_gu = n_d + len(p.gu_cuts)
    first_pairs = p.d_cuts[0][1] // 256
    T[...] = jnp.transpose(BF[...])
    back_hidden(0, first_pairs)
    grad_down(0, first_pairs)
    pump(1, PACE[0])
    back_hidden(first_pairs, pairs)
    if ff % 256:
        loop(2, back_hidden_last)
    grad_down(first_pairs, pairs)
    if ff % 256:
        loop(2, grad_down_last)
    pump(n_d, PACE[1])

    def back_normed(zz):
        cols = pl.ds(pl.multiple_of(zz * (width // 4), width // 4), width // 4)
        acc = dot_nt(GU[0, :, 0:ff], weight(0, p.gu_at, ff, zz))
        acc = acc + dot_nt(GU[0, :, ff : 2 * ff], weight(0, p.gu_at + ff, ff, zz))
        acc = acc + dot_nt(GU[1, :, 0:ff], weight(1, p.gu_at, ff, zz))
        bff[:, cols] = acc + dot_nt(GU[1, :, ff : 2 * ff], weight(1, p.gu_at + ff, ff, zz))

    loop(2, back_normed)
    pump(n_d, PACE[1] + 1)
    loop(2, lambda i: back_normed(i + 2))
    pump(n_d, PACE[2])
    T[...] = jnp.transpose(nf[...])

    def grad_gate_up(lo, hi):
        def run(i):
            yy, off = i // (hi - lo), pl.multiple_of((lax.rem(i, hi - lo) + lo) * 256, 256)
            put_weight(yy, p.gu_at + off, 256, dot_nn(T[...], GU[yy, :, pl.ds(off, 256)]))

        loop(2 * (hi - lo), run)

    grad_gate_up(0, 4)
    pump(n_d + 2, PACE[3])
    grad_gate_up(4, 2 * ff // 256)
    pump(n_gu, PACE[4])

    def mid_back(blk):
        m = mid[blk, :]
        scale = rms(m)
        e = bff[blk, :]
        bm = TB[blk, :].astype(f32) + norm_grad(m, scale, gains[2:3, :], e)
        dgains[2:3, :] += jnp.sum(m * scale * e, axis=0, keepdims=True)
        b = ba[blk, :]
        scale_b = rms(b)
        BF[blk, :] = norm_grad(b, scale_b, gains[1:2, :], bm).astype(bf16)
        dgains[1:2, :] += jnp.sum(b * scale_b * bm, axis=0, keepdims=True)
        mid[blk, :] = bm

    by_rows(mid_back)
    load_again = pltpu.make_async_copy(tok_hbm, TB, loc.at[0])
    load_again.start()
    pump(n_gu, PACE[5])

    per_o = hc // 256

    def back_att(i):
        yy, off = i // per_o, pl.multiple_of(lax.rem(i, per_o) * 256, 256)
        nf[:, cut(yy * hc + off, 256)] = dot_nn(BF[...], weight(yy, p.o_at + off, 256)).astype(bf16)

    loop(2 * per_o, back_att)
    T[...] = jnp.transpose(BF[...])

    def grad_out_tile(i):
        yy, off = i // per_o, pl.multiple_of(lax.rem(i, per_o) * 256, 256)
        put_weight(yy, p.o_at + off, 256, dot_nn(T[...], att[:, cut(yy * hc + off, 256)]))

    loop(2 * per_o, grad_out_tile)
    pump(n_gu + 1, PACE[6])

    stat_b[...] = jnp.zeros_like(stat_b)
    for h in range(p.heads):
        cols = slice(h * HEAD_DIM, (h + 1) * HEAD_DIM)
        inner = jnp.sum(nf[:, cols].astype(f32) * att[:, cols].astype(f32), axis=-1, keepdims=True)
        stat_b[...] = jnp.where(lane == h, inner, stat_b[...])
    log_rows = jnp.transpose(stat_a[...])[0 : p.heads, :]
    inner_rows = jnp.transpose(stat_b[...])[0 : p.heads, :]
    gains[8 : 8 + p.heads, 0:rows] = log_rows
    gains[8 : 8 + p.heads, rows : 2 * rows] = inner_rows
    build_mask(1)

    def attend_grad(h):
        yy, k_at, v_at, q_at = head_at(h)
        q = KVQ[yy, :, q_at]
        do = nf[:, pl.ds(pl.multiple_of(h * HEAD_DIM, HEAD_DIM), HEAD_DIM)]
        log_row = gains[pl.ds(8 + h, 1), 0:rows]
        inner_row = gains[pl.ds(8 + h, 1), rows : 2 * rows]

        def side(ref, place, hide):
            k, v = ref[yy, :, k_at], ref[yy, :, v_at]
            s = dot_nt(k, q) * log2_scale
            if hide:
                s = s + MK[...]
            prob = jnp.exp2(s - log_row)
            dv = dot_nn(prob.astype(bf16), do)
            ds = (prob * (dot_nt(v, do) - inner_row) * attn_scale).astype(bf16)
            dk = dot_nn(ds, q)
            dq = dot_tn(ds, k)
            ref[yy, :, v_at] = dv.astype(bf16)
            ref[yy, :, k_at] = rotated(dk, place, -1.0).astype(bf16)
            return dq

        DQ[...] = side(KVQ, own_place, True)

        @pl.when(second)
        def _():
            DQ[...] += side(KVp, old_place, False)

        KVQ[yy, :, q_at] = rotated(DQ[...], own_place, -1.0).astype(bf16)

    def grad_heads(lo, hi):
        loop(hi - lo, lambda h: attend_grad(h + lo))

    for i in range(4):
        grad_heads(i * p.heads // 4, (i + 1) * p.heads // 4)
        pump(n_gu + 1, PACE[7 + i])

    put_out.wait()

    back_send = remote(LO, KVp.at[0, :, pl.ds(0, width)], extra_s.at[0], extra_r.at[0], y_peer)

    @pl.when(second)
    def _():
        def old_back(zz):
            cols = pl.ds(pl.multiple_of(zz * (width // 4), width // 4), width // 4)
            LO[:, cols] = (
                dot_nt(KVp[0], weight(0, p.k_at, 2 * hc, zz)) + dot_nt(KVp[1], weight(1, p.k_at, 2 * hc, zz))
            ).astype(bf16)

        loop(4, old_back)
        back_send.start()

    def own_back(zz):
        cols = pl.ds(pl.multiple_of(zz * (width // 4), width // 4), width // 4)
        bff[:, cols] = dot_nt(KVQ[0], weight(0, p.k_at, p.kvq, zz)) + dot_nt(KVQ[1], weight(1, p.k_at, p.kvq, zz))

    loop(4, own_back)
    pump(n_gu + 1, PACE[11])
    T[...] = jnp.transpose(xo[...])
    tiles = p.kvq // 256

    def grad_kvq(i):
        yy, off = i // tiles, pl.multiple_of(lax.rem(i, tiles) * 256, 256)
        put_weight(yy, p.k_at + off, 256, dot_nn(T[...], KVQ[yy, :, pl.ds(off, 256)]))

    loop(2 * tiles, grad_kvq)

    @pl.when(second)
    def _():
        T[...] = jnp.transpose(xp[...])
        old_tiles = 2 * hc // 256

        def grad_old(i):
            yy, off = i // old_tiles, pl.multiple_of(lax.rem(i, old_tiles) * 256, 256)
            put_weight(
                yy, p.k_at + off, 256,
                weight(yy, p.k_at + off, 256).astype(f32) + dot_nn(T[...], KVp[yy, :, pl.ds(off, 256)]),
            )

        loop(2 * old_tiles, grad_old)

    pump(n_reduce - 1, PACE[12])
    load_again.wait()

    @pl.when(first)
    def _():
        back_send.wait_recv()

        def join(blk):
            bff[blk, :] += KVp[0, blk, pl.ds(0, width)].astype(f32)

        by_rows(join)

    def in_back(blk):
        t = TB[blk, :].astype(f32)
        scale = rms(t)
        e = bff[blk, :]
        mid[blk, :] = mid[blk, :] + norm_grad(t, scale, gains[0:1, :], e)
        dgains[0:1, :] += jnp.sum(t * scale * e, axis=0, keepdims=True)

    by_rows(in_back)
    put_ig = pltpu.make_async_copy(mid, ig_hbm, loc.at[0])
    put_ig.start()

    gain_cols = jnp.transpose(jnp.concatenate([dgains[...], jnp.zeros((LANES - 8, width), f32)], axis=0))
    put_weight(0, 0, LANES, gain_cols)
    put_weight(1, 0, LANES, gain_cols)
    pump(n_reduce, len(events) * 2)
    put_ig.wait()
    for i in (n_reduce - 2, n_reduce - 1):
        put_sum(i).wait()

    for j in range(n_reduce):
        for m in range(8):
            rs(j, m).wait_send()

    @pl.when(first)
    def _():
        for i in range(TOKEN_PIECES):
            tok_piece(i).wait_send()

    @pl.when(second)
    def _():
        back_send.wait_send()


def finish_layer(plan, out_hbm, ig_hbm, total_hbm, out_to, ig_to, gq, gk, gv, go, gg, gu, gd, g0, g1, g2, g3, bufs, sems):
    o_buf, i_buf, total = bufs
    load_sem, store_sem = sems
    hc, ff = plan.head_cols, plan.ff_cols
    cuts = ((0, plan.gu_at), (plan.gu_at, 2 * ff), (plan.d_at, ff))
    loads = [pltpu.make_async_copy(out_hbm, o_buf, load_sem.at[0]), pltpu.make_async_copy(ig_hbm, i_buf, load_sem.at[1])]
    for i, (at, size) in enumerate(cuts):
        cols = pl.ds(at, size)
        loads.append(pltpu.make_async_copy(total_hbm.at[:, cols], total.at[:, cols], load_sem.at[2 + i]))
    moves = [[(o_buf, out_to)], [(i_buf, ig_to)]]
    moves.append(
        [
            (total.at[:, pl.ds(at, hc)], to)
            for at, to in ((plan.k_at, gk), (plan.v_at, gv), (plan.q_at, gq), (plan.o_at, go))
        ]
    )
    moves.append(
        [
            (total.at[:, pl.ds(plan.gu_at + (2 * t + n) * LANES, LANES)], to.at[:, pl.ds(t * LANES, LANES)])
            for t in range(ff // LANES)
            for n, to in enumerate((gg, gu))
        ]
    )
    moves.append([(total.at[:, pl.ds(plan.d_at, ff)], gd)])
    stores = []
    for load in loads:
        load.start()
    for load, group in zip(loads, moves):
        load.wait()
        for src, to in group:
            stores.append(pltpu.make_async_copy(src, to, store_sem.at[len(stores)]))
            stores[-1].start()
    gains = jnp.transpose(total[:, 0:LANES])
    for i, ref in enumerate((g0, g1, g2, g3)):
        ref[...] = gains[i : i + 1, :]
    for store in stores:
        store.wait()


def fused_on_device(
    tokens,
    query_weight,
    key_weight,
    value_weight,
    out_weight,
    gate_weight,
    up_weight,
    down_weight,
    gain_attn_in,
    gain_attn_out,
    gain_ff_in,
    gain_ff_out,
    piece_starts,
    out_grad,
):
    rows, width = tokens.shape
    plan = Plan(rows, width, query_weight.shape[1], gate_weight.shape[1], query_weight.shape[0])
    gain_shard = jnp.stack([gain_attn_in, gain_attn_out, gain_ff_in, gain_ff_out]).astype(f32)
    half = rope_base ** (-(np.arange(HALF, dtype=np.float32) * 2.0) / HEAD_DIM)
    inverse = jnp.asarray(np.concatenate([half, half])[None].astype(np.float32))
    hc, ff, sr = plan.head_cols, plan.ff_cols, plan.shard_rows
    anywhere = pl.BlockSpec(memory_space=pl.ANY)
    in_vmem = pl.BlockSpec(memory_space=pltpu.VMEM)
    n_gather, n_reduce = len(plan.gather), len(plan.reduce)
    scratch = [
        pltpu.VMEM((2, 4, 2, 2, sr, plan.cols), bf16),
        pltpu.VMEM((2, rows, 3 * hc), bf16),
        pltpu.VMEM((2, rows, 2 * hc), bf16),
        pltpu.VMEM((rows, width), bf16),
        pltpu.VMEM((rows, width), bf16),
        pltpu.VMEM((width, rows), bf16),
        pltpu.VMEM((rows, 2 * hc), bf16),
        pltpu.VMEM((rows, width), f32),
        pltpu.VMEM((rows, width), f32),
        pltpu.VMEM((rows, width), f32),
        pltpu.VMEM((rows, width), bf16),
        pltpu.VMEM((2, rows, 2 * ff), bf16),
        pltpu.VMEM((2, rows, ff), bf16),
        pltpu.VMEM((rows, width), bf16),
        pltpu.VMEM((rows, width), bf16),
        pltpu.VMEM((rows, width), bf16),
        pltpu.VMEM((rows, rows), f32),
        pltpu.VMEM((8 + plan.heads, max(width, 2 * rows)), f32),
        pltpu.VMEM((8, width), f32),
        pltpu.VMEM((rows, LANES), f32),
        pltpu.VMEM((rows, LANES), f32),
        pltpu.VMEM((rows, HEAD_DIM), f32),
        pltpu.VMEM((2 * rows, LANES), f32),
        pltpu.VMEM((2 * rows, LANES), f32),
        pltpu.VMEM((2, 2, 4, 2, sr, 512), bf16),
        pltpu.VMEM((2, 2, 2, sr, 512), bf16),
        pltpu.VMEM((2, 2, 3, sr, 512), bf16),
        pltpu.VMEM((2, 2, sr, 512), bf16),
        pltpu.VMEM((2, 3, sr, 512), bf16),
        pltpu.VMEM((2, 3, sr, 512), bf16),
        pltpu.VMEM((max(1, REDUCE_LATE), 3, 2, 2, sr, 512), bf16),
        pltpu.VMEM((max(1, REDUCE_LATE), 2, sr, 512), bf16),
        pltpu.VMEM((max(1, REDUCE_LATE), sr, 512), bf16),
        pltpu.VMEM((2, sr, 512), f32),
        pltpu.SemaphoreType.DMA((n_gather, 8)),
        pltpu.SemaphoreType.DMA((n_gather, 8)),
        pltpu.SemaphoreType.DMA((n_reduce, 8)),
        pltpu.SemaphoreType.DMA((n_reduce, 8)),
        pltpu.SemaphoreType.DMA((4,)),
        pltpu.SemaphoreType.DMA((5 + 2 * (ff // LANES),)),
        pltpu.SemaphoreType.DMA((1 + TOKEN_PIECES,)),
        pltpu.SemaphoreType.DMA((1 + TOKEN_PIECES,)),
        pltpu.SemaphoreType.REGULAR((8,)),
    ]
    out, input_grad, total = pl.pallas_call(
        functools.partial(fused_layer, plan),
        out_shape=(
            jax.ShapeDtypeStruct((rows, width), bf16),
            jax.ShapeDtypeStruct((rows, width), f32),
            jax.ShapeDtypeStruct((sr, plan.cols), f32),
        ),
        in_specs=[anywhere] * 7 + [in_vmem] + [anywhere] * 2 + [pl.BlockSpec(memory_space=pltpu.SMEM), in_vmem],
        out_specs=(anywhere, anywhere, anywhere),
        scratch_shapes=scratch,
        compiler_params=pltpu.CompilerParams(
            collective_id=0, has_side_effects=True, vmem_limit_bytes=67043328
        ),
        name="fused_layer",
    )(
        key_weight, value_weight, query_weight, gate_weight, up_weight, out_weight.T, down_weight.T,
        gain_shard, tokens, out_grad, piece_starts, inverse,
    )

    def grad(*shape):
        return jax.ShapeDtypeStruct(shape, f32)

    outs = pl.pallas_call(
        functools.partial(finish_layer, plan),
        out_shape=(
            jax.ShapeDtypeStruct((rows, width), bf16),
            grad(rows, width),
            grad(sr, hc),
            grad(sr, hc),
            grad(sr, hc),
            grad(sr, hc),
            grad(sr, ff),
            grad(sr, ff),
            grad(sr, ff),
        )
        + (grad(1, sr),) * 4,
        in_specs=[anywhere] * 3,
        out_specs=(anywhere,) * 9 + (in_vmem,) * 4,
        scratch_shapes=[
            (
                pltpu.VMEM((rows, width), bf16),
                pltpu.VMEM((rows, width), f32),
                pltpu.VMEM((sr, plan.cols), f32),
            ),
            (pltpu.SemaphoreType.DMA((5,)), pltpu.SemaphoreType.DMA((7 + 2 * (ff // LANES),))),
        ],
        name="finish_layer",
    )(out, input_grad, total)
    outs = list(outs)
    outs[5], outs[8] = outs[5].T, outs[8].T
    return tuple(outs[:9]) + tuple(o[0] for o in outs[9:])


def fits_fused(mesh, tokens, query_weight, gate_weight, piece_starts):
    dp, tensor = mesh.shape["dp"], mesh.shape["tensor"]
    sequences, pieces = piece_starts.shape
    return (
        (dp, tensor, pieces, sequences) == (16, 2, 2, dp)
        and tokens.shape[0] % (dp * tensor * 256) == 0
        and tokens.shape[1] == query_weight.shape[1]
        and tokens.shape[1] % (dp * 16) == 0
        and query_weight.shape[1] % (tensor * 256) == 0
        and gate_weight.shape[1] % (tensor * LANES) == 0
    )


def solution(mesh):
    placed = (
        P(("dp", "tensor"), None),
        P("dp", "tensor"),
        P("dp", "tensor"),
        P("dp", "tensor"),
        P("tensor", "dp"),
        P("dp", "tensor"),
        P("dp", "tensor"),
        P("tensor", "dp"),
        P("dp"),
        P("dp"),
        P("dp"),
        P("dp"),
        P("dp", None),
        P(("dp", "tensor"), None),
    )
    def step(*arrays):
        fused = fits_fused(mesh, arrays[0], arrays[1], arrays[5], arrays[12])
        return place(fused_on_device if fused else on_device)(*arrays)

    def place(body):
        return jax.shard_map(
            body,
            mesh=mesh,
            in_specs=placed,
            out_specs=(
                P(("dp", "tensor"), None),
                P(("dp", "tensor"), None),
                P("dp", "tensor"),
                P("dp", "tensor"),
                P("dp", "tensor"),
                P("tensor", "dp"),
                P("dp", "tensor"),
                P("dp", "tensor"),
                P("tensor", "dp"),
                P("dp"),
                P("dp"),
                P("dp"),
                P("dp"),
            ),
            check_vma=False,
        )

    return step
```

```python
import functools
import math

import jax
import jax.numpy as jnp
import numpy as np
from jax import lax
from jax.experimental import pallas as pl
from jax.experimental.pallas import tpu as pltpu
from jax.sharding import PartitionSpec as P

HEAD_DIM = 128
PIECE = 256


norm_eps = 1e-06
rope_base = 50000.0
masked = -1e30


def rms_scale(values):
    return lax.rsqrt(jnp.mean(values * values, axis=-1, keepdims=True) + norm_eps)


def norm_back(values, scale, gain, incoming):
    weighted = gain * incoming
    row_inner = jnp.mean(values * weighted, axis=-1, keepdims=True)
    backward = scale * weighted - values * (scale * scale * scale) * row_inner
    return (backward, jnp.sum(values * scale * incoming, axis=0))


def rope_at(places):
    half_dim = HEAD_DIM // 2
    inverse = rope_base ** (-(jnp.arange(half_dim, dtype=jnp.float32) * 2.0) / HEAD_DIM)
    angles = places.astype(jnp.float32)[:, None, None] * inverse[None, None, :]
    return (jnp.cos(angles), jnp.sin(angles))


def rope_tables(count, length):
    return rope_at(jnp.arange(count, dtype=jnp.int32) % length)


def rotate(values, cosine, sine):
    half_dim = values.shape[-1] // 2
    lower_half = values[..., :half_dim]
    upper_half = values[..., half_dim:]
    return jnp.concatenate(
        [lower_half * cosine - upper_half * sine, upper_half * cosine + lower_half * sine], axis=-1
    )


def unrotate(grads, cosine, sine):
    half_dim = grads.shape[-1] // 2
    lower_half = grads[..., :half_dim]
    upper_half = grads[..., half_dim:]
    return jnp.concatenate(
        [lower_half * cosine + upper_half * sine, upper_half * cosine - lower_half * sine], axis=-1
    )


def piece_ids(starts, length):
    places = jnp.arange(length, dtype=jnp.int32)
    inside = (places[None, :, None] >= starts[:, None, :]) & (
        places[None, :, None] < starts[:, None, :] + PIECE
    )
    labels = jnp.arange(1, starts.shape[1] + 1, dtype=jnp.int32)
    return jnp.sum(jnp.where(inside, labels, 0), axis=2)


def visible(piece_id, offset, count):
    length = piece_id.shape[0]
    query_place = offset + jnp.arange(count, dtype=jnp.int32)
    key_place = jnp.arange(length, dtype=jnp.int32)
    query_ids = piece_id[offset : offset + count]
    return (key_place[None, :] <= query_place[:, None]) | (
        query_ids[:, None] == piece_id[None, :]
    ) & (query_ids[:, None] > 0)


def block_scores(queries, key_vecs, piece_id, offset, count):
    attn_scale = 1.0 / math.sqrt(queries.shape[-1])
    q_block = queries[offset : offset + count]
    scores = (
        jnp.einsum("qhd,khd->hqk", q_block, key_vecs, preferred_element_type=jnp.float32)
        * attn_scale
    )
    return (jnp.where(visible(piece_id, offset, count)[None], scores, masked), q_block)


def attend_one(seq_items):
    queries, key_vecs, values, piece_id = seq_items
    length = queries.shape[0]
    block_rows = min(512, length)
    outputs = []
    log_totals = []
    for offset in range(0, length, block_rows):
        logits, q_block = block_scores(queries, key_vecs, piece_id, offset, block_rows)
        row_max = jnp.max(logits, axis=-1, keepdims=True)
        log_total = row_max + jnp.log(jnp.sum(jnp.exp(logits - row_max), axis=-1, keepdims=True))
        probs = jnp.exp(logits - log_total).astype(jnp.bfloat16)
        mixed = jnp.einsum("hqk,khd->qhd", probs, values, preferred_element_type=jnp.float32)
        outputs.append(mixed.astype(jnp.bfloat16))
        log_totals.append(log_total)
    return (jnp.concatenate(outputs, axis=0), jnp.concatenate(log_totals, axis=1))


def attend_back(seq_items):
    queries, key_vecs, values, piece_id, log_totals, grad_mixed = seq_items
    length = queries.shape[0]
    block_rows = min(512, length)
    attn_scale = 1.0 / math.sqrt(queries.shape[-1])
    grad_keys = jnp.zeros(key_vecs.shape, jnp.float32)
    grad_values = jnp.zeros(values.shape, jnp.float32)
    grad_queries = []
    for offset in range(0, length, block_rows):
        logits, q_block = block_scores(queries, key_vecs, piece_id, offset, block_rows)
        probs = jnp.exp(logits - log_totals[:, offset : offset + block_rows])
        grad_block = grad_mixed[offset : offset + block_rows]
        grad_values = grad_values + jnp.einsum(
            "hqk,qhd->khd",
            probs.astype(jnp.bfloat16),
            grad_block,
            preferred_element_type=jnp.float32,
        )
        grad_probs = jnp.einsum(
            "qhd,khd->hqk", grad_block, values, preferred_element_type=jnp.float32
        )
        row_inner = jnp.sum(probs * grad_probs, axis=-1, keepdims=True)
        grad_scores = (probs * (grad_probs - row_inner) * attn_scale).astype(jnp.bfloat16)
        grad_queries.append(
            jnp.einsum("hqk,khd->qhd", grad_scores, key_vecs, preferred_element_type=jnp.float32)
        )
        grad_keys = grad_keys + jnp.einsum(
            "hqk,qhd->khd", grad_scores, q_block, preferred_element_type=jnp.float32
        )
    return (jnp.concatenate(grad_queries, axis=0), grad_keys, grad_values)


def times_trans(left, right):
    return lax.dot_general(
        left, right, (((1,), (1,)), ((), ())), preferred_element_type=jnp.float32
    )


def trans_times(left, right):
    return lax.dot_general(
        left, right, (((0,), (0,)), ((), ())), preferred_element_type=jnp.float32
    )


def fetch_weights(shards):
    gathered = (
        lax.all_gather(shards[0], "dp", axis=0, tiled=True),
        lax.all_gather(shards[1], "dp", axis=0, tiled=True),
        lax.all_gather(shards[2], "dp", axis=0, tiled=True),
        lax.all_gather(shards[3], "dp", axis=1, tiled=True),
        lax.all_gather(shards[4], "dp", axis=0, tiled=True),
        lax.all_gather(shards[5], "dp", axis=0, tiled=True),
        lax.all_gather(shards[6], "dp", axis=1, tiled=True),
        lax.all_gather(shards[7], "dp", axis=1, tiled=True),
    )
    return gathered


def gather_rows(normed):
    return lax.all_gather(normed, "tensor", axis=0, tiled=True)


def sum_rows(sum_terms):
    return lax.psum_scatter(sum_terms, "tensor", scatter_dimension=0, tiled=True)


def gather_grads(grad_terms):
    return lax.all_gather(grad_terms, "tensor", axis=0, tiled=True)


def sum_grads(grad_terms):
    return lax.psum_scatter(
        grad_terms.astype(jnp.bfloat16), "tensor", scatter_dimension=0, tiled=True
    ).astype(jnp.float32)


def by_sequence(values, seq_count):
    return values.reshape(seq_count, values.shape[0] // seq_count, values.shape[1], values.shape[2])


def attention_part(normed, gathered, cosine, sine, piece_id):
    whole_rows = gather_rows(normed)
    group_rows = whole_rows.shape[0]
    seq_count = piece_id.shape[0]

    def project(weight):
        return jnp.dot(whole_rows, weight, preferred_element_type=jnp.float32).reshape(
            group_rows, -1, HEAD_DIM
        )

    queries = rotate(project(gathered[0]), cosine, sine).astype(jnp.bfloat16)
    key_vecs = rotate(project(gathered[1]), cosine, sine).astype(jnp.bfloat16)
    values = project(gathered[2]).astype(jnp.bfloat16)
    outputs, log_totals = lax.map(
        attend_one,
        (
            by_sequence(queries, seq_count),
            by_sequence(key_vecs, seq_count),
            by_sequence(values, seq_count),
            piece_id,
        ),
    )
    return (whole_rows, queries, key_vecs, values, outputs.reshape(group_rows, -1), log_totals)


def feed_part(normed, gathered):
    whole_rows = gather_rows(normed)
    gate_pre = jnp.dot(whole_rows, gathered[4], preferred_element_type=jnp.float32)
    up_pre = jnp.dot(whole_rows, gathered[5], preferred_element_type=jnp.float32)
    hidden = (jax.nn.silu(gate_pre) * up_pre).astype(jnp.bfloat16)
    return (whole_rows, gate_pre, up_pre, hidden)


def on_device(
    tokens,
    query_weight,
    key_weight,
    value_weight,
    out_weight,
    gate_weight,
    up_weight,
    down_weight,
    gain_attn_in,
    gain_attn_out,
    gain_ff_in,
    gain_ff_out,
    piece_starts,
    out_grad,
):
    shards = (
        query_weight,
        key_weight,
        value_weight,
        out_weight,
        gate_weight,
        up_weight,
        down_weight,
        jnp.stack([gain_attn_in, gain_attn_out, gain_ff_in, gain_ff_out]),
    )
    gathered = fetch_weights(shards)
    gain_rows = gathered[7].astype(jnp.float32)
    tok_rows = tokens.astype(jnp.float32)
    seq_count = piece_starts.shape[0]
    own_rows = tokens.shape[0]
    group_rows = own_rows * lax.axis_size("tensor")
    length = group_rows // seq_count
    piece_id = piece_ids(piece_starts, length)
    incoming = out_grad.astype(jnp.float32)
    scale_in = rms_scale(tok_rows)
    normed_in = (tok_rows * scale_in * gain_rows[0]).astype(jnp.bfloat16)
    cosine, sine = rope_tables(group_rows, length)
    attn_parts = attention_part(normed_in, gathered, cosine, sine, piece_id)
    branch_attn = sum_rows(jnp.dot(attn_parts[4], gathered[3], preferred_element_type=jnp.float32))
    scale_attn = rms_scale(branch_attn)
    mid_rows = tok_rows + branch_attn * scale_attn * gain_rows[1]
    scale_mid = rms_scale(mid_rows)
    normed_ff = (mid_rows * scale_mid * gain_rows[2]).astype(jnp.bfloat16)
    feed_parts = feed_part(normed_ff, gathered)
    branch_ff = sum_rows(jnp.dot(feed_parts[3], gathered[6], preferred_element_type=jnp.float32))
    scale_ff = rms_scale(branch_ff)
    result = (mid_rows + branch_ff * scale_ff * gain_rows[3]).astype(jnp.bfloat16)
    gathered = fetch_weights(shards)
    feed_parts = feed_part(normed_ff, gathered)
    whole_ff, gate_pre, up_pre, hidden = feed_parts
    back_ff, gain_grad_ff_out = norm_back(branch_ff, scale_ff, gain_rows[3], incoming)
    wide_back_ff = gather_grads(back_ff.astype(jnp.bfloat16))
    grad_down = trans_times(hidden, wide_back_ff)
    back_hidden = times_trans(wide_back_ff, gathered[6])
    sigmoid_gate = jax.nn.sigmoid(gate_pre)
    back_gate = (
        back_hidden * up_pre * sigmoid_gate * (1.0 + gate_pre * (1.0 - sigmoid_gate))
    ).astype(jnp.bfloat16)
    back_up = (back_hidden * gate_pre * sigmoid_gate).astype(jnp.bfloat16)
    grad_gate = trans_times(whole_ff, back_gate)
    grad_up = trans_times(whole_ff, back_up)
    back_normed_ff = sum_grads(
        times_trans(back_gate, gathered[4]) + times_trans(back_up, gathered[5])
    )
    back_from_ff, gain_grad_ff_in = norm_back(mid_rows, scale_mid, gain_rows[2], back_normed_ff)
    back_mid = incoming + back_from_ff
    back_attn, gain_grad_attn_out = norm_back(branch_attn, scale_attn, gain_rows[1], back_mid)
    wide_back_attn = gather_grads(back_attn.astype(jnp.bfloat16))
    attn_parts = attention_part(normed_in, gathered, cosine, sine, piece_id)
    whole_in, queries, key_vecs, values, attended, log_totals = attn_parts
    grad_out = trans_times(attended, wide_back_attn)
    back_attended = times_trans(wide_back_attn, gathered[3]).astype(jnp.bfloat16)
    back_queries, back_keys, back_values = lax.map(
        attend_back,
        (
            by_sequence(queries, seq_count),
            by_sequence(key_vecs, seq_count),
            by_sequence(values, seq_count),
            piece_id,
            log_totals,
            by_sequence(back_attended.reshape(group_rows, -1, HEAD_DIM), seq_count),
        ),
    )
    back_queries = (
        unrotate(back_queries.reshape(group_rows, -1, HEAD_DIM), cosine, sine)
        .reshape(group_rows, -1)
        .astype(jnp.bfloat16)
    )
    back_keys = (
        unrotate(back_keys.reshape(group_rows, -1, HEAD_DIM), cosine, sine)
        .reshape(group_rows, -1)
        .astype(jnp.bfloat16)
    )
    back_values = back_values.reshape(group_rows, -1).astype(jnp.bfloat16)
    grad_query = trans_times(whole_in, back_queries)
    grad_key = trans_times(whole_in, back_keys)
    grad_value = trans_times(whole_in, back_values)
    back_normed_in = sum_grads(
        times_trans(back_queries, gathered[0])
        + times_trans(back_keys, gathered[1])
        + times_trans(back_values, gathered[2])
    )
    back_from_in, gain_grad_attn_in = norm_back(tok_rows, scale_in, gain_rows[0], back_normed_in)
    input_grad = back_mid + back_from_in
    weight_terms = (grad_query, grad_key, grad_value, grad_out, grad_gate, grad_up, grad_down)
    gain_grads = lax.psum(
        jnp.stack([gain_grad_attn_in, gain_grad_attn_out, gain_grad_ff_in, gain_grad_ff_out]),
        "tensor",
    )
    grad_sums = (
        lax.psum_scatter(
            weight_terms[0].astype(jnp.bfloat16), "dp", scatter_dimension=0, tiled=True
        ).astype(jnp.float32),
        lax.psum_scatter(
            weight_terms[1].astype(jnp.bfloat16), "dp", scatter_dimension=0, tiled=True
        ).astype(jnp.float32),
        lax.psum_scatter(
            weight_terms[2].astype(jnp.bfloat16), "dp", scatter_dimension=0, tiled=True
        ).astype(jnp.float32),
        lax.psum_scatter(
            weight_terms[3].astype(jnp.bfloat16), "dp", scatter_dimension=1, tiled=True
        ).astype(jnp.float32),
        lax.psum_scatter(
            weight_terms[4].astype(jnp.bfloat16), "dp", scatter_dimension=0, tiled=True
        ).astype(jnp.float32),
        lax.psum_scatter(
            weight_terms[5].astype(jnp.bfloat16), "dp", scatter_dimension=0, tiled=True
        ).astype(jnp.float32),
        lax.psum_scatter(
            weight_terms[6].astype(jnp.bfloat16), "dp", scatter_dimension=1, tiled=True
        ).astype(jnp.float32),
        lax.psum_scatter(
            gain_grads.astype(jnp.bfloat16), "dp", scatter_dimension=1, tiled=True
        ).astype(jnp.float32),
    )
    return (
        result,
        input_grad,
        grad_sums[0],
        grad_sums[1],
        grad_sums[2],
        grad_sums[3],
        grad_sums[4],
        grad_sums[5],
        grad_sums[6],
        grad_sums[7][0],
        grad_sums[7][1],
        grad_sums[7][2],
        grad_sums[7][3],
    )


LANES = 128
HALF = HEAD_DIM // 2
MESH = pl.DeviceIdType.MESH
GATHER_FIRST = (256, 384)
GATHER_DOWN = (512, 384, 256, 256)
REDUCE_DOWN = (512, 512)
REDUCE_LAST = (256, 256)
GATHER_LATE = 2
LATE_STEP = 0
REDUCE_LATE = 0
LATE_SLOTS = (0, 1, 6, 7, 8)
X_FIRST = (1, 2)
X_FIRST_SUM = (2, 2, 2, 2, 2, 2, 2, 2, 1, 1, 1, 1, 1, 1, 1, 1, 1, 1, 1, 1)
PACE = (1, 2, 3, 4, 5, 6, 7, 8, 9, 10, 11, 11, 11)
TOKEN_PIECES = 8
TOKENS_EARLY = 4
TOKENS_A_STEP = 1
f32 = jnp.float32
bf16 = jnp.bfloat16


class Plan:
    def __init__(self, rows, width, head_cols, ff_cols, shard_rows):
        self.rows = rows
        self.width = width
        self.head_cols = head_cols
        self.ff_cols = ff_cols
        self.shard_rows = shard_rows
        self.heads = 2 * head_cols // HEAD_DIM
        self.k_at = LANES
        self.v_at = self.k_at + head_cols
        self.q_at = self.v_at + head_cols
        self.o_at = self.q_at + head_cols
        self.gu_at = self.o_at + head_cols
        self.d_at = self.gu_at + 2 * ff_cols
        self.cols = self.d_at + ff_cols
        self.kvq = 3 * head_cols

        def cuts(start, total, sizes=()):
            pieces = []
            while total > 0:
                size = min(sizes[len(pieces)] if len(pieces) < len(sizes) else 512, total)
                pieces.append((start, size))
                start, total = start + size, total - size
            return pieces

        gu_cuts = cuts(self.gu_at, 2 * ff_cols)
        self.gather = (
            cuts(0, self.v_at, GATHER_FIRST)
            + [(self.v_at, head_cols), (self.q_at, head_cols), (self.o_at, head_cols)]
            + gu_cuts
            + cuts(self.d_at, ff_cols, GATHER_DOWN)
        )
        self.d_cuts = cuts(self.d_at, ff_cols, REDUCE_DOWN)
        self.gu_cuts = gu_cuts
        self.reduce = (
            self.d_cuts
            + self.gu_cuts
            + [(self.o_at, head_cols), (self.q_at, head_cols), (self.v_at, head_cols)]
            + cuts(self.k_at, head_cols, REDUCE_LAST)
            + [(0, LANES)]
        )
        down = len(self.gather) - len(cuts(self.d_at, ff_cols, GATHER_DOWN))
        self.gather_late = list(range(down, down + GATHER_LATE))
        self.gather_early = [k for k in range(len(self.gather)) if k not in self.gather_late]
        self.reduce_late = set(range(REDUCE_LATE))

    def held(self, at):
        early = [i + 3 for i, k in enumerate(self.gather_early) if self.gather[k][0] < at]
        late = [len(self.gather_early) + LATE_STEP + 1 for k in self.gather_late if self.gather[k][0] < at]
        return max(early + late + [0])

    def split(self, k):
        return X_FIRST[k % len(X_FIRST)]

    def split_sum(self, j):
        return X_FIRST_SUM[j % len(X_FIRST_SUM)]


def sigmoid(v):
    return 0.5 * jnp.tanh(0.5 * v) + 0.5


def dot_nn(left, right):
    return lax.dot_general(left, right, (((1,), (0,)), ((), ())), preferred_element_type=f32)


def dot_nt(left, right):
    return lax.dot_general(left, right, (((1,), (1,)), ((), ())), preferred_element_type=f32)


def dot_tn(left, right):
    return lax.dot_general(left, right, (((0,), (0,)), ((), ())), preferred_element_type=f32)


def fused_layer(
    plan,
    k_hbm, v_hbm, q_hbm, g_hbm, u_hbm, o_hbm, d_hbm, gain_shard, tok_hbm, og_hbm, starts_ref, inverse_ref,
    out_hbm, ig_hbm, gr_hbm,
    W, KVQ, KVp, xo, xp, T, att, ba, mid, bff, nf, GU, HID, BF, TB, LO, MK, gains, dgains, stat_a, stat_b, DQ, cos_ref, sin_ref,
    R1, R2A, R2B, R3A, R3B, R4, RQ1, RQ2, RQ3, ST,
    ag_s, ag_r, rs_s, rs_r, loc, pack_sem, extra_s, extra_r, credit,
):
    p = plan
    dp = lax.axis_index("dp")
    y = lax.axis_index("tensor")
    c = lax.rem(dp, 2)
    x = lax.rem(dp // 2, 2)
    z = dp // 4
    rows, width, hc, ff = p.rows, p.width, p.head_cols, p.ff_cols
    first = y == 0
    second = y == 1

    def dev(zz, xx, cc, yy):
        return (zz * 4 + xx * 2 + cc, yy)

    def up(step):
        return lax.rem(z + step, 4)

    core_peer = dev(z, x, 1 - c, y)
    x_peer = dev(z, 1 - x, c, y)
    y_peer = dev(z, x, c, 1 - y)
    z_peers = [dev(up(d), x, c, y) for d in (1, 2, 3)]
    z_sources = [dev(up(4 - d), x, c, y) for d in (1, 2, 3)]

    def remote(src, dst, send, recv, to):
        return pltpu.make_async_remote_copy(
            src_ref=src, dst_ref=dst, send_sem=send, recv_sem=recv, device_id=to, device_id_type=MESH
        )

    def cut(at, size):
        return pl.ds(at if isinstance(at, int) else pl.multiple_of(at, LANES), size)

    def weight(yy, at, size, zz=None):
        if zz is None:
            return W[yy, :, :, :, :, cut(at, size)].reshape(width, size)
        return W[yy, zz, :, :, :, cut(at, size)].reshape(width // 4, size)

    def put_weight(yy, at, size, value):
        W[yy, :, :, :, :, cut(at, size)] = value.astype(bf16).reshape(4, 2, 2, p.shard_rows, size)

    def rms(v):
        return lax.rsqrt(jnp.mean(v * v, axis=-1, keepdims=True) + norm_eps)

    def norm_grad(v, scale, gain, e):
        weighted = gain * e
        inner = jnp.mean(v * weighted, axis=-1, keepdims=True)
        return scale * weighted - v * (scale * scale * scale) * inner

    def by_rows(body, size=64):
        def step(i, carry):
            body(pl.ds(pl.multiple_of(i * size, size), size))
            return carry

        lax.fori_loop(0, rows // size, step, 0)

    def loop(count, body):
        def step(i, carry):
            body(i)
            return carry

        lax.fori_loop(0, count, step, 0)

    own_w = W.at[y, z, x, c]

    def ag(k, m):
        at, size = p.gather[k]
        cols = pl.ds(at, size)
        sem = (ag_s.at[k, m], ag_r.at[k, m])
        if k in p.gather_late:
            half = size // 2 // LANES * LANES
            cols_a, cols_b = pl.ds(at, half), pl.ds(at + half, size - half)
            if m < 3:
                ref = W.at[:, z, :, c, :, cols]
                return remote(ref, ref, *sem, z_peers[m])
            if m == 3:
                return remote(own_w.at[:, cols_a], W.at[y, z, x, c, :, cols_a], *sem, x_peer)
            if m == 4:
                return remote(own_w.at[:, cols_b], W.at[y, z, x, c, :, cols_b], *sem, y_peer)
            if m == 5:
                ref = W.at[y, z, :, c, :, cols_a]
                return remote(ref, ref, *sem, y_peer)
            if m == 6:
                ref = W.at[:, z, x, c, :, cols_b]
                return remote(ref, ref, *sem, x_peer)
        low, high = pl.ds(0, p.split(k)), pl.ds(p.split(k), 4 - p.split(k))
        if m < 3:
            return remote(own_w.at[:, cols], W.at[y, z, x, c, :, cols], *sem, z_peers[m])
        if m == 3:
            ref = W.at[y, low, x, c, :, cols]
            return remote(ref, ref, *sem, x_peer)
        if m == 4:
            ref = W.at[y, high, x, c, :, cols]
            return remote(ref, ref, *sem, y_peer)
        if m == 5:
            ref = W.at[y, low, :, c, :, cols]
            return remote(ref, ref, *sem, y_peer)
        if m == 6:
            ref = W.at[:, high, x, c, :, cols]
            return remote(ref, ref, *sem, x_peer)
        ref = W.at[:, :, :, c, :, cols]
        return remote(ref, ref, *sem, core_peer)

    n_gather = len(p.gather)
    n_early = len(p.gather_early)

    def ag_step(s):
        def early(i):
            return p.gather_early[i] if 0 <= i < n_early else None

        k = early(s)
        if k is not None:
            for m in (0, 1, 2):
                ag(k, m).wait_recv()
            ag(k, 3).start()
            ag(k, 4).start()
        k = early(s - 1)
        if k is not None:
            ag(k, 3).wait_recv()
            ag(k, 5).start()
            ag(k, 4).wait_recv()
            ag(k, 6).start()
        k = early(s - 2)
        if k is not None:
            ag(k, 5).wait_recv()
            ag(k, 6).wait_recv()
            ag(k, 7).start()
        k = early(s - 3)
        if k is not None:
            ag(k, 7).wait_recv()
        if s == n_early + LATE_STEP:
            for k in p.gather_late:
                for m in (0, 1, 2):
                    ag(k, m).wait_recv()
                ag(k, 7).start()
        if s == n_early + LATE_STEP + 1:
            for k in p.gather_late:
                ag(k, 7).wait_recv()

    steps = [0]

    def tok_piece(i):
        blk = pl.ds(i * (rows // TOKEN_PIECES), rows // TOKEN_PIECES)
        return remote(tok_hbm.at[blk, :], xp.at[blk, :], extra_s.at[1 + i], extra_r.at[1 + i], y_peer)

    def tok_send(i):
        @pl.when(first)
        def _():
            tok_piece(i).start()

    def ag_until(at, more=0):
        goal = max(p.held(at), steps[0] + more - 1)
        while steps[0] <= goal:
            ag_step(steps[0])
            for i in range(TOKENS_EARLY, TOKEN_PIECES):
                if (i - TOKENS_EARLY) // TOKENS_A_STEP == steps[0]:
                    tok_send(i)
            steps[0] += 1
            if steps[0] == 1:
                ag_late_turn()
            if steps[0] == 5:
                ag_late_z()

    def ag_late_turn():
        for k in p.gather_late:
            ag(k, 3).wait_recv()
            ag(k, 5).start()
            ag(k, 4).wait_recv()
            ag(k, 6).start()

    def ag_late_z():
        for k in p.gather_late:
            ag(k, 5).wait_recv()
            ag(k, 6).wait_recv()
            for m in (0, 1, 2):
                ag(k, m).start()

    load_tok = pltpu.make_async_copy(tok_hbm, TB, loc.at[0])
    load_tok.start()
    packing = []
    for src, at, size in (
        (k_hbm, p.k_at, hc), (v_hbm, p.v_at, hc), (q_hbm, p.q_at, hc), (o_hbm, p.o_at, hc), (d_hbm, p.d_at, ff)
    ):
        packing.append((src, own_w.at[:, pl.ds(at, size)]))
    for t in range(ff // LANES):
        for n, src in enumerate((g_hbm, u_hbm)):
            to = own_w.at[:, pl.ds(p.gu_at + (2 * t + n) * LANES, LANES)]
            packing.append((src.at[:, pl.ds(t * LANES, LANES)], to))
    packing = [pltpu.make_async_copy(src, to, pack_sem.at[i]) for i, (src, to) in enumerate(packing)]
    for copy in packing:
        copy.start()
    barrier = pltpu.get_barrier_semaphore()
    for peer in [core_peer, x_peer, y_peer] + z_peers:
        pl.semaphore_signal(barrier, inc=1, device_id=peer, device_id_type=MESH)
    count = gain_shard.shape[0]
    spread = jnp.concatenate([gain_shard[...], jnp.zeros((LANES - count, p.shard_rows), f32)], axis=0)
    W[y, z, x, c, :, pl.ds(0, LANES)] = jnp.transpose(spread).astype(bf16)
    for copy in packing:
        copy.wait()
    pl.semaphore_wait(barrier, 6)

    for k in p.gather_late:
        ag(k, 3).start()
        ag(k, 4).start()

    for k in p.gather_early:
        for m in (0, 1, 2):
            ag(k, m).start()
    for i in range(TOKENS_EARLY):
        tok_send(i)
    load_tok.wait()

    def tables(i):
        blk = pl.ds(pl.multiple_of(i * 64, 64), 64)
        place = (lax.broadcasted_iota(jnp.int32, (64, LANES), 0) + i * 64).astype(f32)
        angle = place * inverse_ref[...]
        cos_ref[blk, :] = jnp.cos(angle)
        turned = jnp.sin(angle)
        sin_ref[blk, :] = jnp.where(lax.broadcasted_iota(jnp.int32, (64, LANES), 1) < HALF, -turned, turned)

    loop(2 * rows // 64, tables)

    start = starts_ref[0, y] - y * rows

    def build_mask(query_dim):
        def body(blk):
            shape = (64, rows)
            r = lax.broadcasted_iota(jnp.int32, shape, 0) + blk.start
            s = lax.broadcasted_iota(jnp.int32, shape, 1)
            q_pos, k_pos = (r, s) if query_dim == 0 else (s, r)
            inside = (r >= start) & (r < start + PIECE) & (s >= start) & (s < start + PIECE)
            MK[blk, :] = jnp.where((k_pos <= q_pos) | inside, 0.0, masked)

        by_rows(body)

    build_mask(0)
    dgains[...] = jnp.zeros_like(dgains)

    ag_until(LANES)
    gains[0:8, 0:width] = jnp.transpose(weight(0, 0, LANES).astype(f32))[0:8, :]

    def norm_in(src, dst):
        def body(blk):
            t = src[blk, :].astype(f32)
            dst[blk, :] = (t * rms(t) * gains[0:1, :]).astype(bf16)

        by_rows(body)

    norm_in(TB, xo)

    def rotated(u, place, sign):
        return u * cos_ref[place, :] + sign * (pltpu.roll(u, HALF, 1) * sin_ref[place, :])

    def project(src, dst, at, place, turn):
        def run(yy, off):
            r = dot_nn(src[...], weight(yy, LANES + off, 256))
            for hh in range(2):
                u = r[:, hh * HEAD_DIM : (hh + 1) * HEAD_DIM]
                if turn:
                    u = rotated(u, place, 1.0)
                dst[yy, :, cut(off + hh * HEAD_DIM, HEAD_DIM)] = u.astype(bf16)

        per = hc // 256
        loop(2 * per, lambda i: run(i // per, pl.multiple_of(at + lax.rem(i, per) * 256, 256)))

    own_place = pl.ds(pl.multiple_of(y * rows, rows), rows)
    old_place = pl.ds(0, rows)
    ag_until(p.v_at)
    project(xo, KVQ, 0, own_place, True)
    ag_until(p.q_at)
    project(xo, KVQ, hc, own_place, False)

    @pl.when(second)
    def _():
        for i in range(TOKEN_PIECES):
            tok_piece(i).wait_recv()
        norm_in(xp, xp)

    ag_until(p.o_at)
    project(xo, KVQ, 2 * hc, own_place, True)

    @pl.when(second)
    def _():
        project(xp, KVp, 0, old_place, True)

    ag_until(p.gu_at)

    @pl.when(second)
    def _():
        project(xp, KVp, hc, old_place, False)

    ag_until(0, 1)

    per_y = hc // HEAD_DIM
    attn_scale = 1.0 / math.sqrt(HEAD_DIM)
    log2_scale = attn_scale * math.log2(math.e)
    lane = lax.broadcasted_iota(jnp.int32, (1, LANES), 1)

    def head_at(h):
        yy = h // per_y
        off = pl.multiple_of(lax.rem(h, per_y) * HEAD_DIM, HEAD_DIM)
        return yy, cut(off, HEAD_DIM), cut(off + hc, HEAD_DIM), cut(off + 2 * hc, HEAD_DIM)

    def attend(i, both):
        h = i // 2
        blk = pl.ds(pl.multiple_of(lax.rem(i, 2) * (rows // 2), rows // 2), rows // 2)
        yy, k_at, v_at, q_at = head_at(h)
        q = KVQ[yy, blk, q_at]
        s = dot_nt(q, KVQ[yy, :, k_at]) * log2_scale + MK[blk, :]
        top = jnp.max(s, axis=-1, keepdims=True)
        if both:
            s_old = dot_nt(q, KVp[yy, :, k_at]) * log2_scale
            top = jnp.maximum(top, jnp.max(s_old, axis=-1, keepdims=True))
        e = jnp.exp2(s - top)
        total = jnp.sum(e, axis=-1, keepdims=True)
        if both:
            e_old = jnp.exp2(s_old - top)
            total = total + jnp.sum(e_old, axis=-1, keepdims=True)
        inv = 1.0 / total
        o = dot_nn((e * inv).astype(bf16), KVQ[yy, :, v_at])
        if both:
            o = o + dot_nn((e_old * inv).astype(bf16), KVp[yy, :, v_at])
        att[blk, pl.ds(pl.multiple_of(h * HEAD_DIM, HEAD_DIM), HEAD_DIM)] = o.astype(bf16)
        stat = top + jnp.log2(total)
        stat_a[blk, :] = jnp.where(lane == h, stat, stat_a[blk, :])

    def attend_heads(lo, hi):
        @pl.when(first)
        def _():
            loop(2 * (hi - lo), lambda i: attend(i + 2 * lo, False))

        @pl.when(second)
        def _():
            loop(2 * (hi - lo), lambda i: attend(i + 2 * lo, True))

    stat_a[...] = jnp.zeros_like(stat_a)
    for h in range(0, p.heads, 2):
        attend_heads(h, h + 2)
        ag_until(0, 1)


    def o_proj(zz):
        cols = pl.ds(pl.multiple_of(zz * (width // 4), width // 4), width // 4)
        ba[:, cols] = dot_nt(att[:, 0:hc], weight(0, p.o_at, hc, zz)) + dot_nt(
            att[:, hc : 2 * hc], weight(1, p.o_at, hc, zz)
        )

    loop(4, o_proj)

    def mid_rows(blk):
        b = ba[blk, :]
        m = TB[blk, :].astype(f32) + b * rms(b) * gains[1:2, :]
        mid[blk, :] = m
        nf[blk, :] = (m * rms(m) * gains[2:3, :]).astype(bf16)

    by_rows(mid_rows)
    load_og = pltpu.make_async_copy(og_hbm, TB, loc.at[0])
    load_og.start()

    def gate_up(lo, hi):
        def run(i):
            yy = i // (hi - lo)
            t = lax.rem(i, hi - lo) + lo
            off = pl.multiple_of(t * 256, 256)
            r = dot_nn(nf[...], weight(yy, p.gu_at + off, 256))
            g, u = r[:, 0:LANES], r[:, LANES:256]
            GU[yy, :, pl.ds(off, 256)] = r.astype(bf16)
            HID[yy, :, pl.ds(pl.multiple_of(t * LANES, LANES), LANES)] = (
                g * sigmoid(g) * u
            ).astype(bf16)

        loop(2 * (hi - lo), run)

    ag_until(0, 1)
    tiles = 2 * ff // 256
    for lo in range(0, tiles, 2):
        hi = min(lo + 2, tiles)
        ag_until(p.gu_at + hi * 256)
        gate_up(lo, hi)

    def down_proj(lo, hi, more):
        def run(zz):
            cols = pl.ds(pl.multiple_of(zz * (width // 4), width // 4), width // 4)
            acc = dot_nt(HID[0, :, lo:hi], weight(0, p.d_at + lo, hi - lo, zz)) + dot_nt(
                HID[1, :, lo:hi], weight(1, p.d_at + lo, hi - lo, zz)
            )
            bff[:, cols] = bff[:, cols] + acc if more else acc

        loop(4, run)

    ready = 0
    for n, (at, size) in enumerate(p.gather[p.gather_late[0] :]):
        if n >= GATHER_LATE - 1:
            ag_until(at + size)
            down_proj(ready, at + size - p.d_at, ready > 0)
            ready = at + size - p.d_at

    load_og.wait()

    def out_rows(blk):
        b = bff[blk, :]
        scale = rms(b)
        e = TB[blk, :].astype(f32)
        LO[blk, :] = (mid[blk, :] + b * scale * gains[3:4, :]).astype(bf16)
        BF[blk, :] = norm_grad(b, scale, gains[3:4, :], e).astype(bf16)
        dgains[3:4, :] += jnp.sum(b * scale * e, axis=0, keepdims=True)

    by_rows(out_rows)
    put_out = pltpu.make_async_copy(LO, out_hbm, loc.at[1])
    put_out.start()

    for k in range(n_gather):
        for m in range(8):
            ag(k, m).wait_send()

    n_reduce = len(p.reduce)

    def rs_parts(j):
        at, size = p.reduce[j]
        half = size // 2 // LANES * LANES
        return (pl.ds(at, half), pl.ds(0, half)), (pl.ds(at + half, size - half), pl.ds(half, size - half))

    def rs(j, m):
        at, size = p.reduce[j]
        cols, slot, part = pl.ds(at, size), j % 2, pl.ds(0, size)
        sem = (rs_s.at[j, m], rs_r.at[j, m])
        if m == 0:
            return remote(W.at[:, :, :, 1 - c, :, cols], R1.at[slot, :, :, :, :, part], *sem, core_peer)
        d = m - 5
        if j in p.reduce_late:
            (cols_a, part_a), (cols_b, part_b) = rs_parts(j)
            if m == 1:
                return remote(W.at[1 - y, z, :, c, :, cols_a], RQ2.at[j, :, :, part_a], *sem, y_peer)
            if m == 2:
                return remote(W.at[:, z, 1 - x, c, :, cols_b], RQ2.at[j, :, :, part_b], *sem, x_peer)
            if m == 3:
                return remote(W.at[y, z, 1 - x, c, :, cols_a], RQ3.at[j, :, part_a], *sem, x_peer)
            if m == 4:
                return remote(W.at[1 - y, z, x, c, :, cols_b], RQ3.at[j, :, part_b], *sem, y_peer)
            return remote(W.at[:, up(d + 1), :, c, :, cols], RQ1.at[j, d, :, :, :, part], *sem, z_peers[d])
        low, high = pl.ds(0, p.split_sum(j)), pl.ds(p.split_sum(j), 4 - p.split_sum(j))
        if m == 1:
            return remote(W.at[1 - y, low, :, c, :, cols], R2A.at[slot, low, :, :, part], *sem, y_peer)
        if m == 2:
            return remote(W.at[:, high, 1 - x, c, :, cols], R2B.at[slot, :, pl.ds(0, 4 - p.split_sum(j)), :, part], *sem, x_peer)
        if m == 3:
            return remote(W.at[y, low, 1 - x, c, :, cols], R3A.at[slot, low, :, part], *sem, x_peer)
        if m == 4:
            return remote(W.at[1 - y, high, x, c, :, cols], R3B.at[slot, pl.ds(0, 4 - p.split_sum(j)), :, part], *sem, y_peer)
        return remote(W.at[y, up(d + 1), x, c, :, cols], R4.at[slot, d, :, part], *sem, z_peers[d])

    rs_sources = [core_peer, y_peer, x_peer, x_peer, y_peer] + z_sources
    n_late = len(p.reduce_late)

    def rs_first(m):
        return 2 if m == 0 else n_late + 2

    def rs_start(j, m):
        if j >= rs_first(m):
            pl.semaphore_wait(credit.at[m], 1)
        rs(j, m).start()

    def rs_used(j, m):
        if j + 2 < n_reduce and j + 2 >= rs_first(m):
            pl.semaphore_signal(credit.at[m], inc=1, device_id=rs_sources[m], device_id_type=MESH)

    finished = []

    def put_sum(i):
        at, size = p.reduce[finished[i]]
        return pltpu.make_async_copy(
            ST.at[i % 2, :, pl.ds(0, size)], gr_hbm.at[:, pl.ds(at, size)], loc.at[2 + i % 2]
        )

    def finish(j, total):
        i = len(finished)
        finished.append(j)
        if i >= 2:
            put_sum(i - 2).wait()
        ST[i % 2, :, pl.ds(0, p.reduce[j][1])] = total
        put_sum(i).start()

    def rs_core(j):
        at, size = p.reduce[j]
        cols, slot, part = pl.ds(at, size), j % 2, pl.ds(0, size)
        rs(j, 0).wait_recv()

        def add(i):
            a, b, d = i // 8, lax.rem(i // 2, 4), lax.rem(i, 2)
            W[a, b, d, c, :, cols] = W[a, b, d, c, :, cols] + R1[slot, a, b, d, :, part]

        loop(16, add)
        rs_used(j, 0)

    def rs_late_event(j, phase):
        at, size = p.reduce[j]
        cols, part = pl.ds(at, size), pl.ds(0, size)
        (cols_a, part_a), (cols_b, part_b) = rs_parts(j)
        if phase == 0:
            rs_start(j, 0)
        elif phase == 1:
            rs_core(j)
            for m in (5, 6, 7):
                rs_start(j, m)
        elif phase == 2:
            for m in (5, 6, 7):
                rs(j, m).wait_recv()

            def add_q(i):
                a, b = i // 2, lax.rem(i, 2)
                total = W[a, z, b, c, :, cols].astype(f32)
                for d in range(3):
                    total = total + RQ1[j, d, a, b, :, part].astype(f32)
                W[a, z, b, c, :, cols] = total.astype(bf16)

            loop(4, add_q)
            rs_start(j, 1)
            rs_start(j, 2)
        elif phase == 3:
            rs(j, 1).wait_recv()
            rs(j, 2).wait_recv()
            for d in range(2):
                W[y, z, d, c, :, cols_a] = W[y, z, d, c, :, cols_a] + RQ2[j, d, :, part_a]
                W[d, z, x, c, :, cols_b] = W[d, z, x, c, :, cols_b] + RQ2[j, d, :, part_b]
            rs_start(j, 3)
            rs_start(j, 4)
        else:
            rs(j, 3).wait_recv()
            rs(j, 4).wait_recv()
            finish(j, W[y, z, x, c, :, cols].astype(f32) + RQ3[j, :, part].astype(f32))

    def rs_event(j, phase):
        if j in p.reduce_late:
            rs_late_event(j, phase)
            return
        at, size = p.reduce[j]
        cols, slot, part = pl.ds(at, size), j % 2, pl.ds(0, size)
        n_low = p.split_sum(j)
        n_high = 4 - n_low
        if phase == 0:
            rs_start(j, 0)
        elif phase == 1:
            rs_core(j)
            rs_start(j, 1)
            rs_start(j, 2)
        elif phase == 2:
            rs(j, 1).wait_recv()

            def add_a(i):
                b, d = i // 2, lax.rem(i, 2)
                W[y, b, d, c, :, cols] = W[y, b, d, c, :, cols] + R2A[slot, b, d, :, part]

            loop(2 * n_low, add_a)
            rs_used(j, 1)
            rs_start(j, 3)
            rs(j, 2).wait_recv()

            def add_b(i):
                a, b = i // n_high, lax.rem(i, n_high)
                W[a, b + n_low, x, c, :, cols] = W[a, b + n_low, x, c, :, cols] + R2B[slot, a, b, :, part]

            loop(2 * n_high, add_b)
            rs_used(j, 2)
            rs_start(j, 4)
        elif phase == 3:
            rs(j, 3).wait_recv()
            for b in range(n_low):
                W[y, b, x, c, :, cols] = W[y, b, x, c, :, cols] + R3A[slot, b, :, part]
            rs_used(j, 3)
            rs(j, 4).wait_recv()
            for b in range(n_high):
                W[y, b + n_low, x, c, :, cols] = W[y, b + n_low, x, c, :, cols] + R3B[slot, b, :, part]
            rs_used(j, 4)
            for m in (5, 6, 7):
                rs_start(j, m)
        else:
            for m in (5, 6, 7):
                rs(j, m).wait_recv()
            total = W[y, z, x, c, :, cols].astype(f32)
            for d in range(3):
                total = total + R4[slot, d, :, part].astype(f32)
            for m in (5, 6, 7):
                rs_used(j, m)
            finish(j, total)

    def slot_of(j, phase):
        return j + (LATE_SLOTS[phase] if j in p.reduce_late else phase)

    events = sorted(
        ((j, phase) for j in range(n_reduce) for phase in range(5)), key=lambda e: (slot_of(*e), -e[0], e[1])
    )
    pending = list(events)

    def pump(ready, until):
        blocked = set()
        for j, phase in list(pending):
            if slot_of(j, phase) >= until:
                break
            if j >= ready or j in blocked:
                blocked.add(j)
            else:
                rs_event(j, phase)
                pending.remove((j, phase))

    def back_tile(yy, t, bh):
        off = pl.multiple_of(t * 256, 256)
        g = GU[yy, :, pl.ds(off, LANES)].astype(f32)
        u = GU[yy, :, cut(off + LANES, LANES)].astype(f32)
        s = sigmoid(g)
        GU[yy, :, pl.ds(off, LANES)] = (bh * u * s * (1.0 + g * (1.0 - s))).astype(bf16)
        GU[yy, :, cut(off + LANES, LANES)] = (bh * g * s).astype(bf16)

    pairs = ff // 256

    def back_hidden(lo, hi):
        def run(i):
            yy, t = i // (hi - lo), lax.rem(i, hi - lo) + lo
            bh = dot_nn(BF[...], weight(yy, p.d_at + pl.multiple_of(t * 256, 256), 256))
            back_tile(yy, 2 * t, bh[:, 0:LANES])
            back_tile(yy, 2 * t + 1, bh[:, LANES:256])

        loop(2 * (hi - lo), run)

    def grad_down(lo, hi):
        def run(i):
            yy, off = i // (hi - lo), pl.multiple_of((lax.rem(i, hi - lo) + lo) * 256, 256)
            put_weight(yy, p.d_at + off, 256, dot_nn(T[...], HID[yy, :, pl.ds(off, 256)]))

        loop(2 * (hi - lo), run)

    def back_hidden_last(yy):
        bh = dot_nn(BF[...], weight(yy, p.d_at + pairs * 256, LANES))
        back_tile(yy, jnp.int32(2 * pairs), bh)

    def grad_down_last(yy):
        put_weight(yy, p.d_at + pairs * 256, LANES, dot_nn(T[...], HID[yy, :, pl.ds(pairs * 256, LANES)]))

    n_d = len(p.d_cuts)
    n_gu = n_d + len(p.gu_cuts)
    first_pairs = p.d_cuts[0][1] // 256
    T[...] = jnp.transpose(BF[...])
    back_hidden(0, first_pairs)
    grad_down(0, first_pairs)
    pump(1, PACE[0])
    back_hidden(first_pairs, pairs)
    if ff % 256:
        loop(2, back_hidden_last)
    grad_down(first_pairs, pairs)
    if ff % 256:
        loop(2, grad_down_last)
    pump(n_d, PACE[1])

    def back_normed(zz):
        cols = pl.ds(pl.multiple_of(zz * (width // 4), width // 4), width // 4)
        acc = dot_nt(GU[0, :, 0:ff], weight(0, p.gu_at, ff, zz))
        acc = acc + dot_nt(GU[0, :, ff : 2 * ff], weight(0, p.gu_at + ff, ff, zz))
        acc = acc + dot_nt(GU[1, :, 0:ff], weight(1, p.gu_at, ff, zz))
        bff[:, cols] = acc + dot_nt(GU[1, :, ff : 2 * ff], weight(1, p.gu_at + ff, ff, zz))

    loop(2, back_normed)
    pump(n_d, PACE[1] + 1)
    loop(2, lambda i: back_normed(i + 2))
    pump(n_d, PACE[2])
    T[...] = jnp.transpose(nf[...])

    def grad_gate_up(lo, hi):
        def run(i):
            yy, off = i // (hi - lo), pl.multiple_of((lax.rem(i, hi - lo) + lo) * 256, 256)
            put_weight(yy, p.gu_at + off, 256, dot_nn(T[...], GU[yy, :, pl.ds(off, 256)]))

        loop(2 * (hi - lo), run)

    grad_gate_up(0, 4)
    pump(n_d + 2, PACE[3])
    grad_gate_up(4, 2 * ff // 256)
    pump(n_gu, PACE[4])

    def mid_back(blk):
        m = mid[blk, :]
        scale = rms(m)
        e = bff[blk, :]
        bm = TB[blk, :].astype(f32) + norm_grad(m, scale, gains[2:3, :], e)
        dgains[2:3, :] += jnp.sum(m * scale * e, axis=0, keepdims=True)
        b = ba[blk, :]
        scale_b = rms(b)
        BF[blk, :] = norm_grad(b, scale_b, gains[1:2, :], bm).astype(bf16)
        dgains[1:2, :] += jnp.sum(b * scale_b * bm, axis=0, keepdims=True)
        mid[blk, :] = bm

    by_rows(mid_back)
    load_again = pltpu.make_async_copy(tok_hbm, TB, loc.at[0])
    load_again.start()
    pump(n_gu, PACE[5])

    per_o = hc // 256

    def back_att(i):
        yy, off = i // per_o, pl.multiple_of(lax.rem(i, per_o) * 256, 256)
        nf[:, cut(yy * hc + off, 256)] = dot_nn(BF[...], weight(yy, p.o_at + off, 256)).astype(bf16)

    loop(2 * per_o, back_att)
    T[...] = jnp.transpose(BF[...])

    def grad_out_tile(i):
        yy, off = i // per_o, pl.multiple_of(lax.rem(i, per_o) * 256, 256)
        put_weight(yy, p.o_at + off, 256, dot_nn(T[...], att[:, cut(yy * hc + off, 256)]))

    loop(2 * per_o, grad_out_tile)
    pump(n_gu + 1, PACE[6])

    stat_b[...] = jnp.zeros_like(stat_b)
    for h in range(p.heads):
        cols = slice(h * HEAD_DIM, (h + 1) * HEAD_DIM)
        inner = jnp.sum(nf[:, cols].astype(f32) * att[:, cols].astype(f32), axis=-1, keepdims=True)
        stat_b[...] = jnp.where(lane == h, inner, stat_b[...])
    log_rows = jnp.transpose(stat_a[...])[0 : p.heads, :]
    inner_rows = jnp.transpose(stat_b[...])[0 : p.heads, :]
    gains[8 : 8 + p.heads, 0:rows] = log_rows
    gains[8 : 8 + p.heads, rows : 2 * rows] = inner_rows
    build_mask(1)

    def attend_grad(h):
        yy, k_at, v_at, q_at = head_at(h)
        q = KVQ[yy, :, q_at]
        do = nf[:, pl.ds(pl.multiple_of(h * HEAD_DIM, HEAD_DIM), HEAD_DIM)]
        log_row = gains[pl.ds(8 + h, 1), 0:rows]
        inner_row = gains[pl.ds(8 + h, 1), rows : 2 * rows]

        def side(ref, place, hide):
            k, v = ref[yy, :, k_at], ref[yy, :, v_at]
            s = dot_nt(k, q) * log2_scale
            if hide:
                s = s + MK[...]
            prob = jnp.exp2(s - log_row)
            dv = dot_nn(prob.astype(bf16), do)
            ds = (prob * (dot_nt(v, do) - inner_row) * attn_scale).astype(bf16)
            dk = dot_nn(ds, q)
            dq = dot_tn(ds, k)
            ref[yy, :, v_at] = dv.astype(bf16)
            ref[yy, :, k_at] = rotated(dk, place, -1.0).astype(bf16)
            return dq

        DQ[...] = side(KVQ, own_place, True)

        @pl.when(second)
        def _():
            DQ[...] += side(KVp, old_place, False)

        KVQ[yy, :, q_at] = rotated(DQ[...], own_place, -1.0).astype(bf16)

    def grad_heads(lo, hi):
        loop(hi - lo, lambda h: attend_grad(h + lo))

    for i in range(4):
        grad_heads(i * p.heads // 4, (i + 1) * p.heads // 4)
        pump(n_gu + 1, PACE[7 + i])

    put_out.wait()

    back_send = remote(LO, KVp.at[0, :, pl.ds(0, width)], extra_s.at[0], extra_r.at[0], y_peer)

    @pl.when(second)
    def _():
        def old_back(zz):
            cols = pl.ds(pl.multiple_of(zz * (width // 4), width // 4), width // 4)
            LO[:, cols] = (
                dot_nt(KVp[0], weight(0, p.k_at, 2 * hc, zz)) + dot_nt(KVp[1], weight(1, p.k_at, 2 * hc, zz))
            ).astype(bf16)

        loop(4, old_back)
        back_send.start()

    def own_back(zz):
        cols = pl.ds(pl.multiple_of(zz * (width // 4), width // 4), width // 4)
        bff[:, cols] = dot_nt(KVQ[0], weight(0, p.k_at, p.kvq, zz)) + dot_nt(KVQ[1], weight(1, p.k_at, p.kvq, zz))

    loop(4, own_back)
    pump(n_gu + 1, PACE[11])
    T[...] = jnp.transpose(xo[...])
    tiles = p.kvq // 256

    def grad_kvq(i):
        yy, off = i // tiles, pl.multiple_of(lax.rem(i, tiles) * 256, 256)
        put_weight(yy, p.k_at + off, 256, dot_nn(T[...], KVQ[yy, :, pl.ds(off, 256)]))

    loop(2 * tiles, grad_kvq)

    @pl.when(second)
    def _():
        T[...] = jnp.transpose(xp[...])
        old_tiles = 2 * hc // 256

        def grad_old(i):
            yy, off = i // old_tiles, pl.multiple_of(lax.rem(i, old_tiles) * 256, 256)
            put_weight(
                yy, p.k_at + off, 256,
                weight(yy, p.k_at + off, 256).astype(f32) + dot_nn(T[...], KVp[yy, :, pl.ds(off, 256)]),
            )

        loop(2 * old_tiles, grad_old)

    pump(n_reduce - 1, PACE[12])
    load_again.wait()

    @pl.when(first)
    def _():
        back_send.wait_recv()

        def join(blk):
            bff[blk, :] += KVp[0, blk, pl.ds(0, width)].astype(f32)

        by_rows(join)

    def in_back(blk):
        t = TB[blk, :].astype(f32)
        scale = rms(t)
        e = bff[blk, :]
        mid[blk, :] = mid[blk, :] + norm_grad(t, scale, gains[0:1, :], e)
        dgains[0:1, :] += jnp.sum(t * scale * e, axis=0, keepdims=True)

    by_rows(in_back)
    put_ig = pltpu.make_async_copy(mid, ig_hbm, loc.at[0])
    put_ig.start()

    gain_cols = jnp.transpose(jnp.concatenate([dgains[...], jnp.zeros((LANES - 8, width), f32)], axis=0))
    put_weight(0, 0, LANES, gain_cols)
    put_weight(1, 0, LANES, gain_cols)
    pump(n_reduce, len(events) * 2)
    put_ig.wait()
    for i in (n_reduce - 2, n_reduce - 1):
        put_sum(i).wait()

    for j in range(n_reduce):
        for m in range(8):
            rs(j, m).wait_send()

    @pl.when(first)
    def _():
        for i in range(TOKEN_PIECES):
            tok_piece(i).wait_send()

    @pl.when(second)
    def _():
        back_send.wait_send()


def finish_layer(plan, out_hbm, ig_hbm, total_hbm, out_to, ig_to, gq, gk, gv, go, gg, gu, gd, g0, g1, g2, g3, bufs, sems):
    o_buf, i_buf, total = bufs
    load_sem, store_sem = sems
    hc, ff = plan.head_cols, plan.ff_cols
    cuts = ((0, plan.gu_at), (plan.gu_at, 2 * ff), (plan.d_at, ff))
    loads = [pltpu.make_async_copy(out_hbm, o_buf, load_sem.at[0]), pltpu.make_async_copy(ig_hbm, i_buf, load_sem.at[1])]
    for i, (at, size) in enumerate(cuts):
        cols = pl.ds(at, size)
        loads.append(pltpu.make_async_copy(total_hbm.at[:, cols], total.at[:, cols], load_sem.at[2 + i]))
    moves = [[(o_buf, out_to)], [(i_buf, ig_to)]]
    moves.append(
        [
            (total.at[:, pl.ds(at, hc)], to)
            for at, to in ((plan.k_at, gk), (plan.v_at, gv), (plan.q_at, gq), (plan.o_at, go))
        ]
    )
    moves.append(
        [
            (total.at[:, pl.ds(plan.gu_at + (2 * t + n) * LANES, LANES)], to.at[:, pl.ds(t * LANES, LANES)])
            for t in range(ff // LANES)
            for n, to in enumerate((gg, gu))
        ]
    )
    moves.append([(total.at[:, pl.ds(plan.d_at, ff)], gd)])
    stores = []
    for load in loads:
        load.start()
    for load, group in zip(loads, moves):
        load.wait()
        for src, to in group:
            stores.append(pltpu.make_async_copy(src, to, store_sem.at[len(stores)]))
            stores[-1].start()
    gains = jnp.transpose(total[:, 0:LANES])
    for i, ref in enumerate((g0, g1, g2, g3)):
        ref[...] = gains[i : i + 1, :]
    for store in stores:
        store.wait()


def fused_on_device(
    tokens,
    query_weight,
    key_weight,
    value_weight,
    out_weight,
    gate_weight,
    up_weight,
    down_weight,
    gain_attn_in,
    gain_attn_out,
    gain_ff_in,
    gain_ff_out,
    piece_starts,
    out_grad,
):
    rows, width = tokens.shape
    plan = Plan(rows, width, query_weight.shape[1], gate_weight.shape[1], query_weight.shape[0])
    gain_shard = jnp.stack([gain_attn_in, gain_attn_out, gain_ff_in, gain_ff_out]).astype(f32)
    half = rope_base ** (-(np.arange(HALF, dtype=np.float32) * 2.0) / HEAD_DIM)
    inverse = jnp.asarray(np.concatenate([half, half])[None].astype(np.float32))
    hc, ff, sr = plan.head_cols, plan.ff_cols, plan.shard_rows
    anywhere = pl.BlockSpec(memory_space=pl.ANY)
    in_vmem = pl.BlockSpec(memory_space=pltpu.VMEM)
    n_gather, n_reduce = len(plan.gather), len(plan.reduce)
    scratch = [
        pltpu.VMEM((2, 4, 2, 2, sr, plan.cols), bf16),
        pltpu.VMEM((2, rows, 3 * hc), bf16),
        pltpu.VMEM((2, rows, 2 * hc), bf16),
        pltpu.VMEM((rows, width), bf16),
        pltpu.VMEM((rows, width), bf16),
        pltpu.VMEM((width, rows), bf16),
        pltpu.VMEM((rows, 2 * hc), bf16),
        pltpu.VMEM((rows, width), f32),
        pltpu.VMEM((rows, width), f32),
        pltpu.VMEM((rows, width), f32),
        pltpu.VMEM((rows, width), bf16),
        pltpu.VMEM((2, rows, 2 * ff), bf16),
        pltpu.VMEM((2, rows, ff), bf16),
        pltpu.VMEM((rows, width), bf16),
        pltpu.VMEM((rows, width), bf16),
        pltpu.VMEM((rows, width), bf16),
        pltpu.VMEM((rows, rows), f32),
        pltpu.VMEM((8 + plan.heads, max(width, 2 * rows)), f32),
        pltpu.VMEM((8, width), f32),
        pltpu.VMEM((rows, LANES), f32),
        pltpu.VMEM((rows, LANES), f32),
        pltpu.VMEM((rows, HEAD_DIM), f32),
        pltpu.VMEM((2 * rows, LANES), f32),
        pltpu.VMEM((2 * rows, LANES), f32),
        pltpu.VMEM((2, 2, 4, 2, sr, 512), bf16),
        pltpu.VMEM((2, 2, 2, sr, 512), bf16),
        pltpu.VMEM((2, 2, 3, sr, 512), bf16),
        pltpu.VMEM((2, 2, sr, 512), bf16),
        pltpu.VMEM((2, 3, sr, 512), bf16),
        pltpu.VMEM((2, 3, sr, 512), bf16),
        pltpu.VMEM((max(1, REDUCE_LATE), 3, 2, 2, sr, 512), bf16),
        pltpu.VMEM((max(1, REDUCE_LATE), 2, sr, 512), bf16),
        pltpu.VMEM((max(1, REDUCE_LATE), sr, 512), bf16),
        pltpu.VMEM((2, sr, 512), f32),
        pltpu.SemaphoreType.DMA((n_gather, 8)),
        pltpu.SemaphoreType.DMA((n_gather, 8)),
        pltpu.SemaphoreType.DMA((n_reduce, 8)),
        pltpu.SemaphoreType.DMA((n_reduce, 8)),
        pltpu.SemaphoreType.DMA((4,)),
        pltpu.SemaphoreType.DMA((5 + 2 * (ff // LANES),)),
        pltpu.SemaphoreType.DMA((1 + TOKEN_PIECES,)),
        pltpu.SemaphoreType.DMA((1 + TOKEN_PIECES,)),
        pltpu.SemaphoreType.REGULAR((8,)),
    ]
    out, input_grad, total = pl.pallas_call(
        functools.partial(fused_layer, plan),
        out_shape=(
            jax.ShapeDtypeStruct((rows, width), bf16),
            jax.ShapeDtypeStruct((rows, width), f32),
            jax.ShapeDtypeStruct((sr, plan.cols), f32),
        ),
        in_specs=[anywhere] * 7 + [in_vmem] + [anywhere] * 2 + [pl.BlockSpec(memory_space=pltpu.SMEM), in_vmem],
        out_specs=(anywhere, anywhere, anywhere),
        scratch_shapes=scratch,
        compiler_params=pltpu.CompilerParams(
            collective_id=0, has_side_effects=True, vmem_limit_bytes=67043328
        ),
        name="fused_layer",
    )(
        key_weight, value_weight, query_weight, gate_weight, up_weight, out_weight.T, down_weight.T,
        gain_shard, tokens, out_grad, piece_starts, inverse,
    )

    def grad(*shape):
        return jax.ShapeDtypeStruct(shape, f32)

    outs = pl.pallas_call(
        functools.partial(finish_layer, plan),
        out_shape=(
            jax.ShapeDtypeStruct((rows, width), bf16),
            grad(rows, width),
            grad(sr, hc),
            grad(sr, hc),
            grad(sr, hc),
            grad(sr, hc),
            grad(sr, ff),
            grad(sr, ff),
            grad(sr, ff),
        )
        + (grad(1, sr),) * 4,
        in_specs=[anywhere] * 3,
        out_specs=(anywhere,) * 9 + (in_vmem,) * 4,
        scratch_shapes=[
            (
                pltpu.VMEM((rows, width), bf16),
                pltpu.VMEM((rows, width), f32),
                pltpu.VMEM((sr, plan.cols), f32),
            ),
            (pltpu.SemaphoreType.DMA((5,)), pltpu.SemaphoreType.DMA((7 + 2 * (ff // LANES),))),
        ],
        name="finish_layer",
    )(out, input_grad, total)
    outs = list(outs)
    outs[5], outs[8] = outs[5].T, outs[8].T
    return tuple(outs[:9]) + tuple(o[0] for o in outs[9:])


def fits_fused(mesh, tokens, query_weight, gate_weight, piece_starts):
    dp, tensor = mesh.shape["dp"], mesh.shape["tensor"]
    sequences, pieces = piece_starts.shape
    return (
        (dp, tensor, pieces, sequences) == (16, 2, 2, dp)
        and tokens.shape[0] % (dp * tensor * 256) == 0
        and tokens.shape[1] == query_weight.shape[1]
        and tokens.shape[1] % (dp * 16) == 0
        and query_weight.shape[1] % (tensor * 256) == 0
        and gate_weight.shape[1] % (tensor * LANES) == 0
    )


def solution(mesh):
    placed = (
        P(("dp", "tensor"), None),
        P("dp", "tensor"),
        P("dp", "tensor"),
        P("dp", "tensor"),
        P("tensor", "dp"),
        P("dp", "tensor"),
        P("dp", "tensor"),
        P("tensor", "dp"),
        P("dp"),
        P("dp"),
        P("dp"),
        P("dp"),
        P("dp", None),
        P(("dp", "tensor"), None),
    )
    def step(*arrays):
        fused = fits_fused(mesh, arrays[0], arrays[1], arrays[5], arrays[12])
        return place(fused_on_device if fused else on_device)(*arrays)

    def place(body):
        return jax.shard_map(
            body,
            mesh=mesh,
            in_specs=placed,
            out_specs=(
                P(("dp", "tensor"), None),
                P(("dp", "tensor"), None),
                P("dp", "tensor"),
                P("dp", "tensor"),
                P("dp", "tensor"),
                P("tensor", "dp"),
                P("dp", "tensor"),
                P("dp", "tensor"),
                P("tensor", "dp"),
                P("dp"),
                P("dp"),
                P("dp"),
                P("dp"),
            ),
            check_vma=False,
        )

    return step
```

```python
import functools
import math

import jax
import jax.numpy as jnp
import numpy as np
from jax import lax
from jax.experimental import pallas as pl
from jax.experimental.pallas import tpu as pltpu
from jax.sharding import PartitionSpec as P

HEAD_DIM = 128
PIECE = 256


norm_eps = 1e-06
rope_base = 50000.0
masked = -1e30


def rms_scale(values):
    return lax.rsqrt(jnp.mean(values * values, axis=-1, keepdims=True) + norm_eps)


def norm_back(values, scale, gain, incoming):
    weighted = gain * incoming
    row_inner = jnp.mean(values * weighted, axis=-1, keepdims=True)
    backward = scale * weighted - values * (scale * scale * scale) * row_inner
    return (backward, jnp.sum(values * scale * incoming, axis=0))


def rope_at(places):
    half_dim = HEAD_DIM // 2
    inverse = rope_base ** (-(jnp.arange(half_dim, dtype=jnp.float32) * 2.0) / HEAD_DIM)
    angles = places.astype(jnp.float32)[:, None, None] * inverse[None, None, :]
    return (jnp.cos(angles), jnp.sin(angles))


def rope_tables(count, length):
    return rope_at(jnp.arange(count, dtype=jnp.int32) % length)


def rotate(values, cosine, sine):
    half_dim = values.shape[-1] // 2
    lower_half = values[..., :half_dim]
    upper_half = values[..., half_dim:]
    return jnp.concatenate(
        [lower_half * cosine - upper_half * sine, upper_half * cosine + lower_half * sine], axis=-1
    )


def unrotate(grads, cosine, sine):
    half_dim = grads.shape[-1] // 2
    lower_half = grads[..., :half_dim]
    upper_half = grads[..., half_dim:]
    return jnp.concatenate(
        [lower_half * cosine + upper_half * sine, upper_half * cosine - lower_half * sine], axis=-1
    )


def piece_ids(starts, length):
    places = jnp.arange(length, dtype=jnp.int32)
    inside = (places[None, :, None] >= starts[:, None, :]) & (
        places[None, :, None] < starts[:, None, :] + PIECE
    )
    labels = jnp.arange(1, starts.shape[1] + 1, dtype=jnp.int32)
    return jnp.sum(jnp.where(inside, labels, 0), axis=2)


def visible(piece_id, offset, count):
    length = piece_id.shape[0]
    query_place = offset + jnp.arange(count, dtype=jnp.int32)
    key_place = jnp.arange(length, dtype=jnp.int32)
    query_ids = piece_id[offset : offset + count]
    return (key_place[None, :] <= query_place[:, None]) | (
        query_ids[:, None] == piece_id[None, :]
    ) & (query_ids[:, None] > 0)


def block_scores(queries, key_vecs, piece_id, offset, count):
    attn_scale = 1.0 / math.sqrt(queries.shape[-1])
    q_block = queries[offset : offset + count]
    scores = (
        jnp.einsum("qhd,khd->hqk", q_block, key_vecs, preferred_element_type=jnp.float32)
        * attn_scale
    )
    return (jnp.where(visible(piece_id, offset, count)[None], scores, masked), q_block)


def attend_one(seq_items):
    queries, key_vecs, values, piece_id = seq_items
    length = queries.shape[0]
    block_rows = min(512, length)
    outputs = []
    log_totals = []
    for offset in range(0, length, block_rows):
        logits, q_block = block_scores(queries, key_vecs, piece_id, offset, block_rows)
        row_max = jnp.max(logits, axis=-1, keepdims=True)
        log_total = row_max + jnp.log(jnp.sum(jnp.exp(logits - row_max), axis=-1, keepdims=True))
        probs = jnp.exp(logits - log_total).astype(jnp.bfloat16)
        mixed = jnp.einsum("hqk,khd->qhd", probs, values, preferred_element_type=jnp.float32)
        outputs.append(mixed.astype(jnp.bfloat16))
        log_totals.append(log_total)
    return (jnp.concatenate(outputs, axis=0), jnp.concatenate(log_totals, axis=1))


def attend_back(seq_items):
    queries, key_vecs, values, piece_id, log_totals, grad_mixed = seq_items
    length = queries.shape[0]
    block_rows = min(512, length)
    attn_scale = 1.0 / math.sqrt(queries.shape[-1])
    grad_keys = jnp.zeros(key_vecs.shape, jnp.float32)
    grad_values = jnp.zeros(values.shape, jnp.float32)
    grad_queries = []
    for offset in range(0, length, block_rows):
        logits, q_block = block_scores(queries, key_vecs, piece_id, offset, block_rows)
        probs = jnp.exp(logits - log_totals[:, offset : offset + block_rows])
        grad_block = grad_mixed[offset : offset + block_rows]
        grad_values = grad_values + jnp.einsum(
            "hqk,qhd->khd",
            probs.astype(jnp.bfloat16),
            grad_block,
            preferred_element_type=jnp.float32,
        )
        grad_probs = jnp.einsum(
            "qhd,khd->hqk", grad_block, values, preferred_element_type=jnp.float32
        )
        row_inner = jnp.sum(probs * grad_probs, axis=-1, keepdims=True)
        grad_scores = (probs * (grad_probs - row_inner) * attn_scale).astype(jnp.bfloat16)
        grad_queries.append(
            jnp.einsum("hqk,khd->qhd", grad_scores, key_vecs, preferred_element_type=jnp.float32)
        )
        grad_keys = grad_keys + jnp.einsum(
            "hqk,qhd->khd", grad_scores, q_block, preferred_element_type=jnp.float32
        )
    return (jnp.concatenate(grad_queries, axis=0), grad_keys, grad_values)


def times_trans(left, right):
    return lax.dot_general(
        left, right, (((1,), (1,)), ((), ())), preferred_element_type=jnp.float32
    )


def trans_times(left, right):
    return lax.dot_general(
        left, right, (((0,), (0,)), ((), ())), preferred_element_type=jnp.float32
    )


def fetch_weights(shards):
    gathered = (
        lax.all_gather(shards[0], "dp", axis=0, tiled=True),
        lax.all_gather(shards[1], "dp", axis=0, tiled=True),
        lax.all_gather(shards[2], "dp", axis=0, tiled=True),
        lax.all_gather(shards[3], "dp", axis=1, tiled=True),
        lax.all_gather(shards[4], "dp", axis=0, tiled=True),
        lax.all_gather(shards[5], "dp", axis=0, tiled=True),
        lax.all_gather(shards[6], "dp", axis=1, tiled=True),
        lax.all_gather(shards[7], "dp", axis=1, tiled=True),
    )
    return gathered


def gather_rows(normed):
    return lax.all_gather(normed, "tensor", axis=0, tiled=True)


def sum_rows(sum_terms):
    return lax.psum_scatter(sum_terms, "tensor", scatter_dimension=0, tiled=True)


def gather_grads(grad_terms):
    return lax.all_gather(grad_terms, "tensor", axis=0, tiled=True)


def sum_grads(grad_terms):
    return lax.psum_scatter(
        grad_terms.astype(jnp.bfloat16), "tensor", scatter_dimension=0, tiled=True
    ).astype(jnp.float32)


def by_sequence(values, seq_count):
    return values.reshape(seq_count, values.shape[0] // seq_count, values.shape[1], values.shape[2])


def attention_part(normed, gathered, cosine, sine, piece_id):
    whole_rows = gather_rows(normed)
    group_rows = whole_rows.shape[0]
    seq_count = piece_id.shape[0]

    def project(weight):
        return jnp.dot(whole_rows, weight, preferred_element_type=jnp.float32).reshape(
            group_rows, -1, HEAD_DIM
        )

    queries = rotate(project(gathered[0]), cosine, sine).astype(jnp.bfloat16)
    key_vecs = rotate(project(gathered[1]), cosine, sine).astype(jnp.bfloat16)
    values = project(gathered[2]).astype(jnp.bfloat16)
    outputs, log_totals = lax.map(
        attend_one,
        (
            by_sequence(queries, seq_count),
            by_sequence(key_vecs, seq_count),
            by_sequence(values, seq_count),
            piece_id,
        ),
    )
    return (whole_rows, queries, key_vecs, values, outputs.reshape(group_rows, -1), log_totals)


def feed_part(normed, gathered):
    whole_rows = gather_rows(normed)
    gate_pre = jnp.dot(whole_rows, gathered[4], preferred_element_type=jnp.float32)
    up_pre = jnp.dot(whole_rows, gathered[5], preferred_element_type=jnp.float32)
    hidden = (jax.nn.silu(gate_pre) * up_pre).astype(jnp.bfloat16)
    return (whole_rows, gate_pre, up_pre, hidden)


def on_device(
    tokens,
    query_weight,
    key_weight,
    value_weight,
    out_weight,
    gate_weight,
    up_weight,
    down_weight,
    gain_attn_in,
    gain_attn_out,
    gain_ff_in,
    gain_ff_out,
    piece_starts,
    out_grad,
):
    shards = (
        query_weight,
        key_weight,
        value_weight,
        out_weight,
        gate_weight,
        up_weight,
        down_weight,
        jnp.stack([gain_attn_in, gain_attn_out, gain_ff_in, gain_ff_out]),
    )
    gathered = fetch_weights(shards)
    gain_rows = gathered[7].astype(jnp.float32)
    tok_rows = tokens.astype(jnp.float32)
    seq_count = piece_starts.shape[0]
    own_rows = tokens.shape[0]
    group_rows = own_rows * lax.axis_size("tensor")
    length = group_rows // seq_count
    piece_id = piece_ids(piece_starts, length)
    incoming = out_grad.astype(jnp.float32)
    scale_in = rms_scale(tok_rows)
    normed_in = (tok_rows * scale_in * gain_rows[0]).astype(jnp.bfloat16)
    cosine, sine = rope_tables(group_rows, length)
    attn_parts = attention_part(normed_in, gathered, cosine, sine, piece_id)
    branch_attn = sum_rows(jnp.dot(attn_parts[4], gathered[3], preferred_element_type=jnp.float32))
    scale_attn = rms_scale(branch_attn)
    mid_rows = tok_rows + branch_attn * scale_attn * gain_rows[1]
    scale_mid = rms_scale(mid_rows)
    normed_ff = (mid_rows * scale_mid * gain_rows[2]).astype(jnp.bfloat16)
    feed_parts = feed_part(normed_ff, gathered)
    branch_ff = sum_rows(jnp.dot(feed_parts[3], gathered[6], preferred_element_type=jnp.float32))
    scale_ff = rms_scale(branch_ff)
    result = (mid_rows + branch_ff * scale_ff * gain_rows[3]).astype(jnp.bfloat16)
    gathered = fetch_weights(shards)
    feed_parts = feed_part(normed_ff, gathered)
    whole_ff, gate_pre, up_pre, hidden = feed_parts
    back_ff, gain_grad_ff_out = norm_back(branch_ff, scale_ff, gain_rows[3], incoming)
    wide_back_ff = gather_grads(back_ff.astype(jnp.bfloat16))
    grad_down = trans_times(hidden, wide_back_ff)
    back_hidden = times_trans(wide_back_ff, gathered[6])
    sigmoid_gate = jax.nn.sigmoid(gate_pre)
    back_gate = (
        back_hidden * up_pre * sigmoid_gate * (1.0 + gate_pre * (1.0 - sigmoid_gate))
    ).astype(jnp.bfloat16)
    back_up = (back_hidden * gate_pre * sigmoid_gate).astype(jnp.bfloat16)
    grad_gate = trans_times(whole_ff, back_gate)
    grad_up = trans_times(whole_ff, back_up)
    back_normed_ff = sum_grads(
        times_trans(back_gate, gathered[4]) + times_trans(back_up, gathered[5])
    )
    back_from_ff, gain_grad_ff_in = norm_back(mid_rows, scale_mid, gain_rows[2], back_normed_ff)
    back_mid = incoming + back_from_ff
    back_attn, gain_grad_attn_out = norm_back(branch_attn, scale_attn, gain_rows[1], back_mid)
    wide_back_attn = gather_grads(back_attn.astype(jnp.bfloat16))
    attn_parts = attention_part(normed_in, gathered, cosine, sine, piece_id)
    whole_in, queries, key_vecs, values, attended, log_totals = attn_parts
    grad_out = trans_times(attended, wide_back_attn)
    back_attended = times_trans(wide_back_attn, gathered[3]).astype(jnp.bfloat16)
    back_queries, back_keys, back_values = lax.map(
        attend_back,
        (
            by_sequence(queries, seq_count),
            by_sequence(key_vecs, seq_count),
            by_sequence(values, seq_count),
            piece_id,
            log_totals,
            by_sequence(back_attended.reshape(group_rows, -1, HEAD_DIM), seq_count),
        ),
    )
    back_queries = (
        unrotate(back_queries.reshape(group_rows, -1, HEAD_DIM), cosine, sine)
        .reshape(group_rows, -1)
        .astype(jnp.bfloat16)
    )
    back_keys = (
        unrotate(back_keys.reshape(group_rows, -1, HEAD_DIM), cosine, sine)
        .reshape(group_rows, -1)
        .astype(jnp.bfloat16)
    )
    back_values = back_values.reshape(group_rows, -1).astype(jnp.bfloat16)
    grad_query = trans_times(whole_in, back_queries)
    grad_key = trans_times(whole_in, back_keys)
    grad_value = trans_times(whole_in, back_values)
    back_normed_in = sum_grads(
        times_trans(back_queries, gathered[0])
        + times_trans(back_keys, gathered[1])
        + times_trans(back_values, gathered[2])
    )
    back_from_in, gain_grad_attn_in = norm_back(tok_rows, scale_in, gain_rows[0], back_normed_in)
    input_grad = back_mid + back_from_in
    weight_terms = (grad_query, grad_key, grad_value, grad_out, grad_gate, grad_up, grad_down)
    gain_grads = lax.psum(
        jnp.stack([gain_grad_attn_in, gain_grad_attn_out, gain_grad_ff_in, gain_grad_ff_out]),
        "tensor",
    )
    grad_sums = (
        lax.psum_scatter(
            weight_terms[0].astype(jnp.bfloat16), "dp", scatter_dimension=0, tiled=True
        ).astype(jnp.float32),
        lax.psum_scatter(
            weight_terms[1].astype(jnp.bfloat16), "dp", scatter_dimension=0, tiled=True
        ).astype(jnp.float32),
        lax.psum_scatter(
            weight_terms[2].astype(jnp.bfloat16), "dp", scatter_dimension=0, tiled=True
        ).astype(jnp.float32),
        lax.psum_scatter(
            weight_terms[3].astype(jnp.bfloat16), "dp", scatter_dimension=1, tiled=True
        ).astype(jnp.float32),
        lax.psum_scatter(
            weight_terms[4].astype(jnp.bfloat16), "dp", scatter_dimension=0, tiled=True
        ).astype(jnp.float32),
        lax.psum_scatter(
            weight_terms[5].astype(jnp.bfloat16), "dp", scatter_dimension=0, tiled=True
        ).astype(jnp.float32),
        lax.psum_scatter(
            weight_terms[6].astype(jnp.bfloat16), "dp", scatter_dimension=1, tiled=True
        ).astype(jnp.float32),
        lax.psum_scatter(
            gain_grads.astype(jnp.bfloat16), "dp", scatter_dimension=1, tiled=True
        ).astype(jnp.float32),
    )
    return (
        result,
        input_grad,
        grad_sums[0],
        grad_sums[1],
        grad_sums[2],
        grad_sums[3],
        grad_sums[4],
        grad_sums[5],
        grad_sums[6],
        grad_sums[7][0],
        grad_sums[7][1],
        grad_sums[7][2],
        grad_sums[7][3],
    )


LANES = 128
HALF = HEAD_DIM // 2
MESH = pl.DeviceIdType.MESH
GATHER_FIRST = (256, 384)
GATHER_DOWN = (512, 384, 256, 256)
REDUCE_DOWN = (512, 512)
REDUCE_LAST = (256, 256)
GATHER_LATE = 2
LATE_STEP = 0
REDUCE_LATE = 1
LATE_SLOTS = (0, 1, 6, 7, 8)
X_FIRST = (1, 2)
X_FIRST_SUM = (2, 2, 2, 2, 2, 2, 2, 2, 1, 1, 1, 1, 1, 1, 1, 1, 1, 1, 1, 1)
PACE = (1, 2, 3, 4, 5, 6, 7, 8, 9, 10, 11, 12, 13)
TOKEN_PIECES = 8
TOKENS_EARLY = 4
TOKENS_A_STEP = 1
f32 = jnp.float32
bf16 = jnp.bfloat16


class Plan:
    def __init__(self, rows, width, head_cols, ff_cols, shard_rows):
        self.rows = rows
        self.width = width
        self.head_cols = head_cols
        self.ff_cols = ff_cols
        self.shard_rows = shard_rows
        self.heads = 2 * head_cols // HEAD_DIM
        self.k_at = LANES
        self.v_at = self.k_at + head_cols
        self.q_at = self.v_at + head_cols
        self.o_at = self.q_at + head_cols
        self.gu_at = self.o_at + head_cols
        self.d_at = self.gu_at + 2 * ff_cols
        self.cols = self.d_at + ff_cols
        self.kvq = 3 * head_cols

        def cuts(start, total, sizes=()):
            pieces = []
            while total > 0:
                size = min(sizes[len(pieces)] if len(pieces) < len(sizes) else 512, total)
                pieces.append((start, size))
                start, total = start + size, total - size
            return pieces

        gu_cuts = cuts(self.gu_at, 2 * ff_cols)
        self.gather = (
            cuts(0, self.v_at, GATHER_FIRST)
            + [(self.v_at, head_cols), (self.q_at, head_cols), (self.o_at, head_cols)]
            + gu_cuts
            + cuts(self.d_at, ff_cols, GATHER_DOWN)
        )
        self.d_cuts = cuts(self.d_at, ff_cols, REDUCE_DOWN)
        self.gu_cuts = gu_cuts
        self.reduce = (
            self.d_cuts
            + self.gu_cuts
            + [(self.o_at, head_cols), (self.q_at, head_cols), (self.v_at, head_cols)]
            + cuts(self.k_at, head_cols, REDUCE_LAST)
            + [(0, LANES)]
        )
        down = len(self.gather) - len(cuts(self.d_at, ff_cols, GATHER_DOWN))
        self.gather_late = list(range(down, down + GATHER_LATE))
        self.gather_early = [k for k in range(len(self.gather)) if k not in self.gather_late]
        self.reduce_late = set(range(REDUCE_LATE))

    def held(self, at):
        early = [i + 3 for i, k in enumerate(self.gather_early) if self.gather[k][0] < at]
        late = [len(self.gather_early) + LATE_STEP + 1 for k in self.gather_late if self.gather[k][0] < at]
        return max(early + late + [0])

    def split(self, k):
        return X_FIRST[k % len(X_FIRST)]

    def split_sum(self, j):
        return X_FIRST_SUM[j % len(X_FIRST_SUM)]


def sigmoid(v):
    return 0.5 * jnp.tanh(0.5 * v) + 0.5


def dot_nn(left, right):
    return lax.dot_general(left, right, (((1,), (0,)), ((), ())), preferred_element_type=f32)


def dot_nt(left, right):
    return lax.dot_general(left, right, (((1,), (1,)), ((), ())), preferred_element_type=f32)


def dot_tn(left, right):
    return lax.dot_general(left, right, (((0,), (0,)), ((), ())), preferred_element_type=f32)


def fused_layer(
    plan,
    k_hbm, v_hbm, q_hbm, g_hbm, u_hbm, o_hbm, d_hbm, gain_shard, tok_hbm, og_hbm, starts_ref, inverse_ref,
    out_hbm, ig_hbm, gr_hbm,
    W, KVQ, KVp, xo, xp, T, att, ba, mid, bff, nf, GU, HID, BF, TB, LO, MK, gains, dgains, stat_a, stat_b, DQ, cos_ref, sin_ref,
    R1, R2A, R2B, R3A, R3B, R4, RQ1, RQ2, RQ3, ST,
    ag_s, ag_r, rs_s, rs_r, loc, pack_sem, extra_s, extra_r, credit,
):
    p = plan
    dp = lax.axis_index("dp")
    y = lax.axis_index("tensor")
    c = lax.rem(dp, 2)
    x = lax.rem(dp // 2, 2)
    z = dp // 4
    rows, width, hc, ff = p.rows, p.width, p.head_cols, p.ff_cols
    first = y == 0
    second = y == 1

    def dev(zz, xx, cc, yy):
        return (zz * 4 + xx * 2 + cc, yy)

    def up(step):
        return lax.rem(z + step, 4)

    core_peer = dev(z, x, 1 - c, y)
    x_peer = dev(z, 1 - x, c, y)
    y_peer = dev(z, x, c, 1 - y)
    z_peers = [dev(up(d), x, c, y) for d in (1, 2, 3)]
    z_sources = [dev(up(4 - d), x, c, y) for d in (1, 2, 3)]

    def remote(src, dst, send, recv, to):
        return pltpu.make_async_remote_copy(
            src_ref=src, dst_ref=dst, send_sem=send, recv_sem=recv, device_id=to, device_id_type=MESH
        )

    def cut(at, size):
        return pl.ds(at if isinstance(at, int) else pl.multiple_of(at, LANES), size)

    def weight(yy, at, size, zz=None):
        if zz is None:
            return W[yy, :, :, :, :, cut(at, size)].reshape(width, size)
        return W[yy, zz, :, :, :, cut(at, size)].reshape(width // 4, size)

    def put_weight(yy, at, size, value):
        W[yy, :, :, :, :, cut(at, size)] = value.astype(bf16).reshape(4, 2, 2, p.shard_rows, size)

    def rms(v):
        return lax.rsqrt(jnp.mean(v * v, axis=-1, keepdims=True) + norm_eps)

    def norm_grad(v, scale, gain, e):
        weighted = gain * e
        inner = jnp.mean(v * weighted, axis=-1, keepdims=True)
        return scale * weighted - v * (scale * scale * scale) * inner

    def by_rows(body, size=64):
        def step(i, carry):
            body(pl.ds(pl.multiple_of(i * size, size), size))
            return carry

        lax.fori_loop(0, rows // size, step, 0)

    def loop(count, body):
        def step(i, carry):
            body(i)
            return carry

        lax.fori_loop(0, count, step, 0)

    own_w = W.at[y, z, x, c]

    def ag(k, m):
        at, size = p.gather[k]
        cols = pl.ds(at, size)
        sem = (ag_s.at[k, m], ag_r.at[k, m])
        if k in p.gather_late:
            half = size // 2 // LANES * LANES
            cols_a, cols_b = pl.ds(at, half), pl.ds(at + half, size - half)
            if m < 3:
                ref = W.at[:, z, :, c, :, cols]
                return remote(ref, ref, *sem, z_peers[m])
            if m == 3:
                return remote(own_w.at[:, cols_a], W.at[y, z, x, c, :, cols_a], *sem, x_peer)
            if m == 4:
                return remote(own_w.at[:, cols_b], W.at[y, z, x, c, :, cols_b], *sem, y_peer)
            if m == 5:
                ref = W.at[y, z, :, c, :, cols_a]
                return remote(ref, ref, *sem, y_peer)
            if m == 6:
                ref = W.at[:, z, x, c, :, cols_b]
                return remote(ref, ref, *sem, x_peer)
        low, high = pl.ds(0, p.split(k)), pl.ds(p.split(k), 4 - p.split(k))
        if m < 3:
            return remote(own_w.at[:, cols], W.at[y, z, x, c, :, cols], *sem, z_peers[m])
        if m == 3:
            ref = W.at[y, low, x, c, :, cols]
            return remote(ref, ref, *sem, x_peer)
        if m == 4:
            ref = W.at[y, high, x, c, :, cols]
            return remote(ref, ref, *sem, y_peer)
        if m == 5:
            ref = W.at[y, low, :, c, :, cols]
            return remote(ref, ref, *sem, y_peer)
        if m == 6:
            ref = W.at[:, high, x, c, :, cols]
            return remote(ref, ref, *sem, x_peer)
        ref = W.at[:, :, :, c, :, cols]
        return remote(ref, ref, *sem, core_peer)

    n_gather = len(p.gather)
    n_early = len(p.gather_early)

    def ag_step(s):
        def early(i):
            return p.gather_early[i] if 0 <= i < n_early else None

        k = early(s)
        if k is not None:
            for m in (0, 1, 2):
                ag(k, m).wait_recv()
            ag(k, 3).start()
            ag(k, 4).start()
        k = early(s - 1)
        if k is not None:
            ag(k, 3).wait_recv()
            ag(k, 5).start()
            ag(k, 4).wait_recv()
            ag(k, 6).start()
        k = early(s - 2)
        if k is not None:
            ag(k, 5).wait_recv()
            ag(k, 6).wait_recv()
            ag(k, 7).start()
        k = early(s - 3)
        if k is not None:
            ag(k, 7).wait_recv()
        if s == n_early + LATE_STEP:
            for k in p.gather_late:
                for m in (0, 1, 2):
                    ag(k, m).wait_recv()
                ag(k, 7).start()
        if s == n_early + LATE_STEP + 1:
            for k in p.gather_late:
                ag(k, 7).wait_recv()

    steps = [0]

    def tok_piece(i):
        blk = pl.ds(i * (rows // TOKEN_PIECES), rows // TOKEN_PIECES)
        return remote(tok_hbm.at[blk, :], xp.at[blk, :], extra_s.at[1 + i], extra_r.at[1 + i], y_peer)

    def tok_send(i):
        @pl.when(first)
        def _():
            tok_piece(i).start()

    def ag_until(at, more=0):
        goal = max(p.held(at), steps[0] + more - 1)
        while steps[0] <= goal:
            ag_step(steps[0])
            for i in range(TOKENS_EARLY, TOKEN_PIECES):
                if (i - TOKENS_EARLY) // TOKENS_A_STEP == steps[0]:
                    tok_send(i)
            steps[0] += 1
            if steps[0] == 1:
                ag_late_turn()
            if steps[0] == 5:
                ag_late_z()

    def ag_late_turn():
        for k in p.gather_late:
            ag(k, 3).wait_recv()
            ag(k, 5).start()
            ag(k, 4).wait_recv()
            ag(k, 6).start()

    def ag_late_z():
        for k in p.gather_late:
            ag(k, 5).wait_recv()
            ag(k, 6).wait_recv()
            for m in (0, 1, 2):
                ag(k, m).start()

    load_tok = pltpu.make_async_copy(tok_hbm, TB, loc.at[0])
    load_tok.start()
    packing = []
    for src, at, size in (
        (k_hbm, p.k_at, hc), (v_hbm, p.v_at, hc), (q_hbm, p.q_at, hc), (o_hbm, p.o_at, hc), (d_hbm, p.d_at, ff)
    ):
        packing.append((src, own_w.at[:, pl.ds(at, size)]))
    for t in range(ff // LANES):
        for n, src in enumerate((g_hbm, u_hbm)):
            to = own_w.at[:, pl.ds(p.gu_at + (2 * t + n) * LANES, LANES)]
            packing.append((src.at[:, pl.ds(t * LANES, LANES)], to))
    packing = [pltpu.make_async_copy(src, to, pack_sem.at[i]) for i, (src, to) in enumerate(packing)]
    for copy in packing:
        copy.start()
    barrier = pltpu.get_barrier_semaphore()
    for peer in [core_peer, x_peer, y_peer] + z_peers:
        pl.semaphore_signal(barrier, inc=1, device_id=peer, device_id_type=MESH)
    count = gain_shard.shape[0]
    spread = jnp.concatenate([gain_shard[...], jnp.zeros((LANES - count, p.shard_rows), f32)], axis=0)
    W[y, z, x, c, :, pl.ds(0, LANES)] = jnp.transpose(spread).astype(bf16)
    for copy in packing:
        copy.wait()
    pl.semaphore_wait(barrier, 6)

    for k in p.gather_late:
        ag(k, 3).start()
        ag(k, 4).start()

    for k in p.gather_early:
        for m in (0, 1, 2):
            ag(k, m).start()
    for i in range(TOKENS_EARLY):
        tok_send(i)
    load_tok.wait()

    def tables(i):
        blk = pl.ds(pl.multiple_of(i * 64, 64), 64)
        place = (lax.broadcasted_iota(jnp.int32, (64, LANES), 0) + i * 64).astype(f32)
        angle = place * inverse_ref[...]
        cos_ref[blk, :] = jnp.cos(angle)
        turned = jnp.sin(angle)
        sin_ref[blk, :] = jnp.where(lax.broadcasted_iota(jnp.int32, (64, LANES), 1) < HALF, -turned, turned)

    loop(2 * rows // 64, tables)

    start = starts_ref[0, y] - y * rows

    def build_mask(query_dim):
        def body(blk):
            shape = (64, rows)
            r = lax.broadcasted_iota(jnp.int32, shape, 0) + blk.start
            s = lax.broadcasted_iota(jnp.int32, shape, 1)
            q_pos, k_pos = (r, s) if query_dim == 0 else (s, r)
            inside = (r >= start) & (r < start + PIECE) & (s >= start) & (s < start + PIECE)
            MK[blk, :] = jnp.where((k_pos <= q_pos) | inside, 0.0, masked)

        by_rows(body)

    build_mask(0)
    dgains[...] = jnp.zeros_like(dgains)

    ag_until(LANES)
    gains[0:8, 0:width] = jnp.transpose(weight(0, 0, LANES).astype(f32))[0:8, :]

    def norm_in(src, dst):
        def body(blk):
            t = src[blk, :].astype(f32)
            dst[blk, :] = (t * rms(t) * gains[0:1, :]).astype(bf16)

        by_rows(body)

    norm_in(TB, xo)

    def rotated(u, place, sign):
        return u * cos_ref[place, :] + sign * (pltpu.roll(u, HALF, 1) * sin_ref[place, :])

    def project(src, dst, at, place, turn):
        def run(yy, off):
            r = dot_nn(src[...], weight(yy, LANES + off, 256))
            for hh in range(2):
                u = r[:, hh * HEAD_DIM : (hh + 1) * HEAD_DIM]
                if turn:
                    u = rotated(u, place, 1.0)
                dst[yy, :, cut(off + hh * HEAD_DIM, HEAD_DIM)] = u.astype(bf16)

        per = hc // 256
        loop(2 * per, lambda i: run(i // per, pl.multiple_of(at + lax.rem(i, per) * 256, 256)))

    own_place = pl.ds(pl.multiple_of(y * rows, rows), rows)
    old_place = pl.ds(0, rows)
    ag_until(p.v_at)
    project(xo, KVQ, 0, own_place, True)
    ag_until(p.q_at)
    project(xo, KVQ, hc, own_place, False)

    @pl.when(second)
    def _():
        for i in range(TOKEN_PIECES):
            tok_piece(i).wait_recv()
        norm_in(xp, xp)

    ag_until(p.o_at)
    project(xo, KVQ, 2 * hc, own_place, True)

    @pl.when(second)
    def _():
        project(xp, KVp, 0, old_place, True)

    ag_until(p.gu_at)

    @pl.when(second)
    def _():
        project(xp, KVp, hc, old_place, False)

    ag_until(0, 1)

    per_y = hc // HEAD_DIM
    attn_scale = 1.0 / math.sqrt(HEAD_DIM)
    log2_scale = attn_scale * math.log2(math.e)
    lane = lax.broadcasted_iota(jnp.int32, (1, LANES), 1)

    def head_at(h):
        yy = h // per_y
        off = pl.multiple_of(lax.rem(h, per_y) * HEAD_DIM, HEAD_DIM)
        return yy, cut(off, HEAD_DIM), cut(off + hc, HEAD_DIM), cut(off + 2 * hc, HEAD_DIM)

    def attend(i, both):
        h = i // 2
        blk = pl.ds(pl.multiple_of(lax.rem(i, 2) * (rows // 2), rows // 2), rows // 2)
        yy, k_at, v_at, q_at = head_at(h)
        q = KVQ[yy, blk, q_at]
        s = dot_nt(q, KVQ[yy, :, k_at]) * log2_scale + MK[blk, :]
        top = jnp.max(s, axis=-1, keepdims=True)
        if both:
            s_old = dot_nt(q, KVp[yy, :, k_at]) * log2_scale
            top = jnp.maximum(top, jnp.max(s_old, axis=-1, keepdims=True))
        e = jnp.exp2(s - top)
        total = jnp.sum(e, axis=-1, keepdims=True)
        if both:
            e_old = jnp.exp2(s_old - top)
            total = total + jnp.sum(e_old, axis=-1, keepdims=True)
        inv = 1.0 / total
        o = dot_nn((e * inv).astype(bf16), KVQ[yy, :, v_at])
        if both:
            o = o + dot_nn((e_old * inv).astype(bf16), KVp[yy, :, v_at])
        att[blk, pl.ds(pl.multiple_of(h * HEAD_DIM, HEAD_DIM), HEAD_DIM)] = o.astype(bf16)
        stat = top + jnp.log2(total)
        stat_a[blk, :] = jnp.where(lane == h, stat, stat_a[blk, :])

    def attend_heads(lo, hi):
        @pl.when(first)
        def _():
            loop(2 * (hi - lo), lambda i: attend(i + 2 * lo, False))

        @pl.when(second)
        def _():
            loop(2 * (hi - lo), lambda i: attend(i + 2 * lo, True))

    stat_a[...] = jnp.zeros_like(stat_a)
    for h in range(0, p.heads, 2):
        attend_heads(h, h + 2)
        ag_until(0, 1)


    def o_proj(zz):
        cols = pl.ds(pl.multiple_of(zz * (width // 4), width // 4), width // 4)
        ba[:, cols] = dot_nt(att[:, 0:hc], weight(0, p.o_at, hc, zz)) + dot_nt(
            att[:, hc : 2 * hc], weight(1, p.o_at, hc, zz)
        )

    loop(4, o_proj)

    def mid_rows(blk):
        b = ba[blk, :]
        m = TB[blk, :].astype(f32) + b * rms(b) * gains[1:2, :]
        mid[blk, :] = m
        nf[blk, :] = (m * rms(m) * gains[2:3, :]).astype(bf16)

    by_rows(mid_rows)
    load_og = pltpu.make_async_copy(og_hbm, TB, loc.at[0])
    load_og.start()

    def gate_up(lo, hi):
        def run(i):
            yy = i // (hi - lo)
            t = lax.rem(i, hi - lo) + lo
            off = pl.multiple_of(t * 256, 256)
            r = dot_nn(nf[...], weight(yy, p.gu_at + off, 256))
            g, u = r[:, 0:LANES], r[:, LANES:256]
            GU[yy, :, pl.ds(off, 256)] = r.astype(bf16)
            HID[yy, :, pl.ds(pl.multiple_of(t * LANES, LANES), LANES)] = (
                g * sigmoid(g) * u
            ).astype(bf16)

        loop(2 * (hi - lo), run)

    ag_until(0, 1)
    tiles = 2 * ff // 256
    for lo in range(0, tiles, 2):
        hi = min(lo + 2, tiles)
        ag_until(p.gu_at + hi * 256)
        gate_up(lo, hi)

    def down_proj(lo, hi, more):
        def run(zz):
            cols = pl.ds(pl.multiple_of(zz * (width // 4), width // 4), width // 4)
            acc = dot_nt(HID[0, :, lo:hi], weight(0, p.d_at + lo, hi - lo, zz)) + dot_nt(
                HID[1, :, lo:hi], weight(1, p.d_at + lo, hi - lo, zz)
            )
            bff[:, cols] = bff[:, cols] + acc if more else acc

        loop(4, run)

    ready = 0
    for n, (at, size) in enumerate(p.gather[p.gather_late[0] :]):
        if n >= GATHER_LATE - 1:
            ag_until(at + size)
            down_proj(ready, at + size - p.d_at, ready > 0)
            ready = at + size - p.d_at

    load_og.wait()

    def out_rows(blk):
        b = bff[blk, :]
        scale = rms(b)
        e = TB[blk, :].astype(f32)
        LO[blk, :] = (mid[blk, :] + b * scale * gains[3:4, :]).astype(bf16)
        BF[blk, :] = norm_grad(b, scale, gains[3:4, :], e).astype(bf16)
        dgains[3:4, :] += jnp.sum(b * scale * e, axis=0, keepdims=True)

    by_rows(out_rows)
    put_out = pltpu.make_async_copy(LO, out_hbm, loc.at[1])
    put_out.start()

    for k in range(n_gather):
        for m in range(8):
            ag(k, m).wait_send()

    n_reduce = len(p.reduce)

    def rs_parts(j):
        at, size = p.reduce[j]
        half = size // 2 // LANES * LANES
        return (pl.ds(at, half), pl.ds(0, half)), (pl.ds(at + half, size - half), pl.ds(half, size - half))

    def rs(j, m):
        at, size = p.reduce[j]
        cols, slot, part = pl.ds(at, size), j % 2, pl.ds(0, size)
        sem = (rs_s.at[j, m], rs_r.at[j, m])
        if m == 0:
            return remote(W.at[:, :, :, 1 - c, :, cols], R1.at[slot, :, :, :, :, part], *sem, core_peer)
        d = m - 5
        if j in p.reduce_late:
            (cols_a, part_a), (cols_b, part_b) = rs_parts(j)
            if m == 1:
                return remote(W.at[1 - y, z, :, c, :, cols_a], RQ2.at[j, :, :, part_a], *sem, y_peer)
            if m == 2:
                return remote(W.at[:, z, 1 - x, c, :, cols_b], RQ2.at[j, :, :, part_b], *sem, x_peer)
            if m == 3:
                return remote(W.at[y, z, 1 - x, c, :, cols_a], RQ3.at[j, :, part_a], *sem, x_peer)
            if m == 4:
                return remote(W.at[1 - y, z, x, c, :, cols_b], RQ3.at[j, :, part_b], *sem, y_peer)
            return remote(W.at[:, up(d + 1), :, c, :, cols], RQ1.at[j, d, :, :, :, part], *sem, z_peers[d])
        low, high = pl.ds(0, p.split_sum(j)), pl.ds(p.split_sum(j), 4 - p.split_sum(j))
        if m == 1:
            return remote(W.at[1 - y, low, :, c, :, cols], R2A.at[slot, low, :, :, part], *sem, y_peer)
        if m == 2:
            return remote(W.at[:, high, 1 - x, c, :, cols], R2B.at[slot, :, pl.ds(0, 4 - p.split_sum(j)), :, part], *sem, x_peer)
        if m == 3:
            return remote(W.at[y, low, 1 - x, c, :, cols], R3A.at[slot, low, :, part], *sem, x_peer)
        if m == 4:
            return remote(W.at[1 - y, high, x, c, :, cols], R3B.at[slot, pl.ds(0, 4 - p.split_sum(j)), :, part], *sem, y_peer)
        return remote(W.at[y, up(d + 1), x, c, :, cols], R4.at[slot, d, :, part], *sem, z_peers[d])

    rs_sources = [core_peer, y_peer, x_peer, x_peer, y_peer] + z_sources
    n_late = len(p.reduce_late)

    def rs_first(m):
        return 2 if m == 0 else n_late + 2

    def rs_start(j, m):
        if j >= rs_first(m):
            pl.semaphore_wait(credit.at[m], 1)
        rs(j, m).start()

    def rs_used(j, m):
        if j + 2 < n_reduce and j + 2 >= rs_first(m):
            pl.semaphore_signal(credit.at[m], inc=1, device_id=rs_sources[m], device_id_type=MESH)

    finished = []

    def put_sum(i):
        at, size = p.reduce[finished[i]]
        return pltpu.make_async_copy(
            ST.at[i % 2, :, pl.ds(0, size)], gr_hbm.at[:, pl.ds(at, size)], loc.at[2 + i % 2]
        )

    def finish(j, total):
        i = len(finished)
        finished.append(j)
        if i >= 2:
            put_sum(i - 2).wait()
        ST[i % 2, :, pl.ds(0, p.reduce[j][1])] = total
        put_sum(i).start()

    def rs_core(j):
        at, size = p.reduce[j]
        cols, slot, part = pl.ds(at, size), j % 2, pl.ds(0, size)
        rs(j, 0).wait_recv()

        def add(i):
            a, b, d = i // 8, lax.rem(i // 2, 4), lax.rem(i, 2)
            W[a, b, d, c, :, cols] = W[a, b, d, c, :, cols] + R1[slot, a, b, d, :, part]

        loop(16, add)
        rs_used(j, 0)

    def rs_late_event(j, phase):
        at, size = p.reduce[j]
        cols, part = pl.ds(at, size), pl.ds(0, size)
        (cols_a, part_a), (cols_b, part_b) = rs_parts(j)
        if phase == 0:
            rs_start(j, 0)
        elif phase == 1:
            rs_core(j)
            for m in (5, 6, 7):
                rs_start(j, m)
        elif phase == 2:
            for m in (5, 6, 7):
                rs(j, m).wait_recv()

            def add_q(i):
                a, b = i // 2, lax.rem(i, 2)
                total = W[a, z, b, c, :, cols].astype(f32)
                for d in range(3):
                    total = total + RQ1[j, d, a, b, :, part].astype(f32)
                W[a, z, b, c, :, cols] = total.astype(bf16)

            loop(4, add_q)
            rs_start(j, 1)
            rs_start(j, 2)
        elif phase == 3:
            rs(j, 1).wait_recv()
            rs(j, 2).wait_recv()
            for d in range(2):
                W[y, z, d, c, :, cols_a] = W[y, z, d, c, :, cols_a] + RQ2[j, d, :, part_a]
                W[d, z, x, c, :, cols_b] = W[d, z, x, c, :, cols_b] + RQ2[j, d, :, part_b]
            rs_start(j, 3)
            rs_start(j, 4)
        else:
            rs(j, 3).wait_recv()
            rs(j, 4).wait_recv()
            finish(j, W[y, z, x, c, :, cols].astype(f32) + RQ3[j, :, part].astype(f32))

    def rs_event(j, phase):
        if j in p.reduce_late:
            rs_late_event(j, phase)
            return
        at, size = p.reduce[j]
        cols, slot, part = pl.ds(at, size), j % 2, pl.ds(0, size)
        n_low = p.split_sum(j)
        n_high = 4 - n_low
        if phase == 0:
            rs_start(j, 0)
        elif phase == 1:
            rs_core(j)
            rs_start(j, 1)
            rs_start(j, 2)
        elif phase == 2:
            rs(j, 1).wait_recv()

            def add_a(i):
                b, d = i // 2, lax.rem(i, 2)
                W[y, b, d, c, :, cols] = W[y, b, d, c, :, cols] + R2A[slot, b, d, :, part]

            loop(2 * n_low, add_a)
            rs_used(j, 1)
            rs_start(j, 3)
            rs(j, 2).wait_recv()

            def add_b(i):
                a, b = i // n_high, lax.rem(i, n_high)
                W[a, b + n_low, x, c, :, cols] = W[a, b + n_low, x, c, :, cols] + R2B[slot, a, b, :, part]

            loop(2 * n_high, add_b)
            rs_used(j, 2)
            rs_start(j, 4)
        elif phase == 3:
            rs(j, 3).wait_recv()
            for b in range(n_low):
                W[y, b, x, c, :, cols] = W[y, b, x, c, :, cols] + R3A[slot, b, :, part]
            rs_used(j, 3)
            rs(j, 4).wait_recv()
            for b in range(n_high):
                W[y, b + n_low, x, c, :, cols] = W[y, b + n_low, x, c, :, cols] + R3B[slot, b, :, part]
            rs_used(j, 4)
            for m in (5, 6, 7):
                rs_start(j, m)
        else:
            for m in (5, 6, 7):
                rs(j, m).wait_recv()
            total = W[y, z, x, c, :, cols].astype(f32)
            for d in range(3):
                total = total + R4[slot, d, :, part].astype(f32)
            for m in (5, 6, 7):
                rs_used(j, m)
            finish(j, total)

    def slot_of(j, phase):
        return j + (LATE_SLOTS[phase] if j in p.reduce_late else phase)

    events = sorted(
        ((j, phase) for j in range(n_reduce) for phase in range(5)), key=lambda e: (slot_of(*e), -e[0], e[1])
    )
    pending = list(events)

    def pump(ready, until):
        blocked = set()
        for j, phase in list(pending):
            if slot_of(j, phase) >= until:
                break
            if j >= ready or j in blocked:
                blocked.add(j)
            else:
                rs_event(j, phase)
                pending.remove((j, phase))

    def back_tile(yy, t, bh):
        off = pl.multiple_of(t * 256, 256)
        g = GU[yy, :, pl.ds(off, LANES)].astype(f32)
        u = GU[yy, :, cut(off + LANES, LANES)].astype(f32)
        s = sigmoid(g)
        GU[yy, :, pl.ds(off, LANES)] = (bh * u * s * (1.0 + g * (1.0 - s))).astype(bf16)
        GU[yy, :, cut(off + LANES, LANES)] = (bh * g * s).astype(bf16)

    pairs = ff // 256

    def back_hidden(lo, hi):
        def run(i):
            yy, t = i // (hi - lo), lax.rem(i, hi - lo) + lo
            bh = dot_nn(BF[...], weight(yy, p.d_at + pl.multiple_of(t * 256, 256), 256))
            back_tile(yy, 2 * t, bh[:, 0:LANES])
            back_tile(yy, 2 * t + 1, bh[:, LANES:256])

        loop(2 * (hi - lo), run)

    def grad_down(lo, hi):
        def run(i):
            yy, off = i // (hi - lo), pl.multiple_of((lax.rem(i, hi - lo) + lo) * 256, 256)
            put_weight(yy, p.d_at + off, 256, dot_nn(T[...], HID[yy, :, pl.ds(off, 256)]))

        loop(2 * (hi - lo), run)

    def back_hidden_last(yy):
        bh = dot_nn(BF[...], weight(yy, p.d_at + pairs * 256, LANES))
        back_tile(yy, jnp.int32(2 * pairs), bh)

    def grad_down_last(yy):
        put_weight(yy, p.d_at + pairs * 256, LANES, dot_nn(T[...], HID[yy, :, pl.ds(pairs * 256, LANES)]))

    n_d = len(p.d_cuts)
    n_gu = n_d + len(p.gu_cuts)
    first_pairs = p.d_cuts[0][1] // 256
    T[...] = jnp.transpose(BF[...])
    back_hidden(0, first_pairs)
    grad_down(0, first_pairs)
    pump(1, PACE[0])
    back_hidden(first_pairs, pairs)
    if ff % 256:
        loop(2, back_hidden_last)
    grad_down(first_pairs, pairs)
    if ff % 256:
        loop(2, grad_down_last)
    pump(n_d, PACE[1])

    def back_normed(zz):
        cols = pl.ds(pl.multiple_of(zz * (width // 4), width // 4), width // 4)
        acc = dot_nt(GU[0, :, 0:ff], weight(0, p.gu_at, ff, zz))
        acc = acc + dot_nt(GU[0, :, ff : 2 * ff], weight(0, p.gu_at + ff, ff, zz))
        acc = acc + dot_nt(GU[1, :, 0:ff], weight(1, p.gu_at, ff, zz))
        bff[:, cols] = acc + dot_nt(GU[1, :, ff : 2 * ff], weight(1, p.gu_at + ff, ff, zz))

    loop(2, back_normed)
    pump(n_d, PACE[1] + 1)
    loop(2, lambda i: back_normed(i + 2))
    pump(n_d, PACE[2])
    T[...] = jnp.transpose(nf[...])

    def grad_gate_up(lo, hi):
        def run(i):
            yy, off = i // (hi - lo), pl.multiple_of((lax.rem(i, hi - lo) + lo) * 256, 256)
            put_weight(yy, p.gu_at + off, 256, dot_nn(T[...], GU[yy, :, pl.ds(off, 256)]))

        loop(2 * (hi - lo), run)

    grad_gate_up(0, 4)
    pump(n_d + 2, PACE[3])
    grad_gate_up(4, 2 * ff // 256)
    pump(n_gu, PACE[4])

    def mid_back(blk):
        m = mid[blk, :]
        scale = rms(m)
        e = bff[blk, :]
        bm = TB[blk, :].astype(f32) + norm_grad(m, scale, gains[2:3, :], e)
        dgains[2:3, :] += jnp.sum(m * scale * e, axis=0, keepdims=True)
        b = ba[blk, :]
        scale_b = rms(b)
        BF[blk, :] = norm_grad(b, scale_b, gains[1:2, :], bm).astype(bf16)
        dgains[1:2, :] += jnp.sum(b * scale_b * bm, axis=0, keepdims=True)
        mid[blk, :] = bm

    by_rows(mid_back)
    load_again = pltpu.make_async_copy(tok_hbm, TB, loc.at[0])
    load_again.start()
    pump(n_gu, PACE[5])

    per_o = hc // 256

    def back_att(i):
        yy, off = i // per_o, pl.multiple_of(lax.rem(i, per_o) * 256, 256)
        nf[:, cut(yy * hc + off, 256)] = dot_nn(BF[...], weight(yy, p.o_at + off, 256)).astype(bf16)

    loop(2 * per_o, back_att)
    T[...] = jnp.transpose(BF[...])

    def grad_out_tile(i):
        yy, off = i // per_o, pl.multiple_of(lax.rem(i, per_o) * 256, 256)
        put_weight(yy, p.o_at + off, 256, dot_nn(T[...], att[:, cut(yy * hc + off, 256)]))

    loop(2 * per_o, grad_out_tile)
    pump(n_gu + 1, PACE[6])

    stat_b[...] = jnp.zeros_like(stat_b)
    for h in range(p.heads):
        cols = slice(h * HEAD_DIM, (h + 1) * HEAD_DIM)
        inner = jnp.sum(nf[:, cols].astype(f32) * att[:, cols].astype(f32), axis=-1, keepdims=True)
        stat_b[...] = jnp.where(lane == h, inner, stat_b[...])
    log_rows = jnp.transpose(stat_a[...])[0 : p.heads, :]
    inner_rows = jnp.transpose(stat_b[...])[0 : p.heads, :]
    gains[8 : 8 + p.heads, 0:rows] = log_rows
    gains[8 : 8 + p.heads, rows : 2 * rows] = inner_rows
    build_mask(1)

    def attend_grad(h):
        yy, k_at, v_at, q_at = head_at(h)
        q = KVQ[yy, :, q_at]
        do = nf[:, pl.ds(pl.multiple_of(h * HEAD_DIM, HEAD_DIM), HEAD_DIM)]
        log_row = gains[pl.ds(8 + h, 1), 0:rows]
        inner_row = gains[pl.ds(8 + h, 1), rows : 2 * rows]

        def side(ref, place, hide):
            k, v = ref[yy, :, k_at], ref[yy, :, v_at]
            s = dot_nt(k, q) * log2_scale
            if hide:
                s = s + MK[...]
            prob = jnp.exp2(s - log_row)
            dv = dot_nn(prob.astype(bf16), do)
            ds = (prob * (dot_nt(v, do) - inner_row) * attn_scale).astype(bf16)
            dk = dot_nn(ds, q)
            dq = dot_tn(ds, k)
            ref[yy, :, v_at] = dv.astype(bf16)
            ref[yy, :, k_at] = rotated(dk, place, -1.0).astype(bf16)
            return dq

        DQ[...] = side(KVQ, own_place, True)

        @pl.when(second)
        def _():
            DQ[...] += side(KVp, old_place, False)

        KVQ[yy, :, q_at] = rotated(DQ[...], own_place, -1.0).astype(bf16)

    def grad_heads(lo, hi):
        loop(hi - lo, lambda h: attend_grad(h + lo))

    for i in range(4):
        grad_heads(i * p.heads // 4, (i + 1) * p.heads // 4)
        pump(n_gu + 1, PACE[7 + i])

    put_out.wait()

    back_send = remote(LO, KVp.at[0, :, pl.ds(0, width)], extra_s.at[0], extra_r.at[0], y_peer)

    @pl.when(second)
    def _():
        def old_back(zz):
            cols = pl.ds(pl.multiple_of(zz * (width // 4), width // 4), width // 4)
            LO[:, cols] = (
                dot_nt(KVp[0], weight(0, p.k_at, 2 * hc, zz)) + dot_nt(KVp[1], weight(1, p.k_at, 2 * hc, zz))
            ).astype(bf16)

        loop(4, old_back)
        back_send.start()

    def own_back(zz):
        cols = pl.ds(pl.multiple_of(zz * (width // 4), width // 4), width // 4)
        bff[:, cols] = dot_nt(KVQ[0], weight(0, p.k_at, p.kvq, zz)) + dot_nt(KVQ[1], weight(1, p.k_at, p.kvq, zz))

    loop(4, own_back)
    pump(n_gu + 1, PACE[11])
    T[...] = jnp.transpose(xo[...])
    tiles = p.kvq // 256

    def grad_kvq(i):
        yy, off = i // tiles, pl.multiple_of(lax.rem(i, tiles) * 256, 256)
        put_weight(yy, p.k_at + off, 256, dot_nn(T[...], KVQ[yy, :, pl.ds(off, 256)]))

    loop(2 * tiles, grad_kvq)

    @pl.when(second)
    def _():
        T[...] = jnp.transpose(xp[...])
        old_tiles = 2 * hc // 256

        def grad_old(i):
            yy, off = i // old_tiles, pl.multiple_of(lax.rem(i, old_tiles) * 256, 256)
            put_weight(
                yy, p.k_at + off, 256,
                weight(yy, p.k_at + off, 256).astype(f32) + dot_nn(T[...], KVp[yy, :, pl.ds(off, 256)]),
            )

        loop(2 * old_tiles, grad_old)

    pump(n_reduce - 1, PACE[12])
    load_again.wait()

    @pl.when(first)
    def _():
        back_send.wait_recv()

        def join(blk):
            bff[blk, :] += KVp[0, blk, pl.ds(0, width)].astype(f32)

        by_rows(join)

    def in_back(blk):
        t = TB[blk, :].astype(f32)
        scale = rms(t)
        e = bff[blk, :]
        mid[blk, :] = mid[blk, :] + norm_grad(t, scale, gains[0:1, :], e)
        dgains[0:1, :] += jnp.sum(t * scale * e, axis=0, keepdims=True)

    by_rows(in_back)
    put_ig = pltpu.make_async_copy(mid, ig_hbm, loc.at[0])
    put_ig.start()

    gain_cols = jnp.transpose(jnp.concatenate([dgains[...], jnp.zeros((LANES - 8, width), f32)], axis=0))
    put_weight(0, 0, LANES, gain_cols)
    put_weight(1, 0, LANES, gain_cols)
    pump(n_reduce, len(events) * 2)
    put_ig.wait()
    for i in (n_reduce - 2, n_reduce - 1):
        put_sum(i).wait()

    for j in range(n_reduce):
        for m in range(8):
            rs(j, m).wait_send()

    @pl.when(first)
    def _():
        for i in range(TOKEN_PIECES):
            tok_piece(i).wait_send()

    @pl.when(second)
    def _():
        back_send.wait_send()


def finish_layer(plan, out_hbm, ig_hbm, total_hbm, out_to, ig_to, gq, gk, gv, go, gg, gu, gd, g0, g1, g2, g3, bufs, sems):
    o_buf, i_buf, total = bufs
    load_sem, store_sem = sems
    hc, ff = plan.head_cols, plan.ff_cols
    cuts = ((0, plan.gu_at), (plan.gu_at, 2 * ff), (plan.d_at, ff))
    loads = [pltpu.make_async_copy(out_hbm, o_buf, load_sem.at[0]), pltpu.make_async_copy(ig_hbm, i_buf, load_sem.at[1])]
    for i, (at, size) in enumerate(cuts):
        cols = pl.ds(at, size)
        loads.append(pltpu.make_async_copy(total_hbm.at[:, cols], total.at[:, cols], load_sem.at[2 + i]))
    moves = [[(o_buf, out_to)], [(i_buf, ig_to)]]
    moves.append(
        [
            (total.at[:, pl.ds(at, hc)], to)
            for at, to in ((plan.k_at, gk), (plan.v_at, gv), (plan.q_at, gq), (plan.o_at, go))
        ]
    )
    moves.append(
        [
            (total.at[:, pl.ds(plan.gu_at + (2 * t + n) * LANES, LANES)], to.at[:, pl.ds(t * LANES, LANES)])
            for t in range(ff // LANES)
            for n, to in enumerate((gg, gu))
        ]
    )
    moves.append([(total.at[:, pl.ds(plan.d_at, ff)], gd)])
    stores = []
    for load in loads:
        load.start()
    for load, group in zip(loads, moves):
        load.wait()
        for src, to in group:
            stores.append(pltpu.make_async_copy(src, to, store_sem.at[len(stores)]))
            stores[-1].start()
    gains = jnp.transpose(total[:, 0:LANES])
    for i, ref in enumerate((g0, g1, g2, g3)):
        ref[...] = gains[i : i + 1, :]
    for store in stores:
        store.wait()


def fused_on_device(
    tokens,
    query_weight,
    key_weight,
    value_weight,
    out_weight,
    gate_weight,
    up_weight,
    down_weight,
    gain_attn_in,
    gain_attn_out,
    gain_ff_in,
    gain_ff_out,
    piece_starts,
    out_grad,
):
    rows, width = tokens.shape
    plan = Plan(rows, width, query_weight.shape[1], gate_weight.shape[1], query_weight.shape[0])
    gain_shard = jnp.stack([gain_attn_in, gain_attn_out, gain_ff_in, gain_ff_out]).astype(f32)
    half = rope_base ** (-(np.arange(HALF, dtype=np.float32) * 2.0) / HEAD_DIM)
    inverse = jnp.asarray(np.concatenate([half, half])[None].astype(np.float32))
    hc, ff, sr = plan.head_cols, plan.ff_cols, plan.shard_rows
    anywhere = pl.BlockSpec(memory_space=pl.ANY)
    in_vmem = pl.BlockSpec(memory_space=pltpu.VMEM)
    n_gather, n_reduce = len(plan.gather), len(plan.reduce)
    scratch = [
        pltpu.VMEM((2, 4, 2, 2, sr, plan.cols), bf16),
        pltpu.VMEM((2, rows, 3 * hc), bf16),
        pltpu.VMEM((2, rows, 2 * hc), bf16),
        pltpu.VMEM((rows, width), bf16),
        pltpu.VMEM((rows, width), bf16),
        pltpu.VMEM((width, rows), bf16),
        pltpu.VMEM((rows, 2 * hc), bf16),
        pltpu.VMEM((rows, width), f32),
        pltpu.VMEM((rows, width), f32),
        pltpu.VMEM((rows, width), f32),
        pltpu.VMEM((rows, width), bf16),
        pltpu.VMEM((2, rows, 2 * ff), bf16),
        pltpu.VMEM((2, rows, ff), bf16),
        pltpu.VMEM((rows, width), bf16),
        pltpu.VMEM((rows, width), bf16),
        pltpu.VMEM((rows, width), bf16),
        pltpu.VMEM((rows, rows), f32),
        pltpu.VMEM((8 + plan.heads, max(width, 2 * rows)), f32),
        pltpu.VMEM((8, width), f32),
        pltpu.VMEM((rows, LANES), f32),
        pltpu.VMEM((rows, LANES), f32),
        pltpu.VMEM((rows, HEAD_DIM), f32),
        pltpu.VMEM((2 * rows, LANES), f32),
        pltpu.VMEM((2 * rows, LANES), f32),
        pltpu.VMEM((2, 2, 4, 2, sr, 512), bf16),
        pltpu.VMEM((2, 2, 2, sr, 512), bf16),
        pltpu.VMEM((2, 2, 3, sr, 512), bf16),
        pltpu.VMEM((2, 2, sr, 512), bf16),
        pltpu.VMEM((2, 3, sr, 512), bf16),
        pltpu.VMEM((2, 3, sr, 512), bf16),
        pltpu.VMEM((max(1, REDUCE_LATE), 3, 2, 2, sr, 512), bf16),
        pltpu.VMEM((max(1, REDUCE_LATE), 2, sr, 512), bf16),
        pltpu.VMEM((max(1, REDUCE_LATE), sr, 512), bf16),
        pltpu.VMEM((2, sr, 512), f32),
        pltpu.SemaphoreType.DMA((n_gather, 8)),
        pltpu.SemaphoreType.DMA((n_gather, 8)),
        pltpu.SemaphoreType.DMA((n_reduce, 8)),
        pltpu.SemaphoreType.DMA((n_reduce, 8)),
        pltpu.SemaphoreType.DMA((4,)),
        pltpu.SemaphoreType.DMA((5 + 2 * (ff // LANES),)),
        pltpu.SemaphoreType.DMA((1 + TOKEN_PIECES,)),
        pltpu.SemaphoreType.DMA((1 + TOKEN_PIECES,)),
        pltpu.SemaphoreType.REGULAR((8,)),
    ]
    out, input_grad, total = pl.pallas_call(
        functools.partial(fused_layer, plan),
        out_shape=(
            jax.ShapeDtypeStruct((rows, width), bf16),
            jax.ShapeDtypeStruct((rows, width), f32),
            jax.ShapeDtypeStruct((sr, plan.cols), f32),
        ),
        in_specs=[anywhere] * 7 + [in_vmem] + [anywhere] * 2 + [pl.BlockSpec(memory_space=pltpu.SMEM), in_vmem],
        out_specs=(anywhere, anywhere, anywhere),
        scratch_shapes=scratch,
        compiler_params=pltpu.CompilerParams(
            collective_id=0, has_side_effects=True, vmem_limit_bytes=67043328
        ),
        name="fused_layer",
    )(
        key_weight, value_weight, query_weight, gate_weight, up_weight, out_weight.T, down_weight.T,
        gain_shard, tokens, out_grad, piece_starts, inverse,
    )

    def grad(*shape):
        return jax.ShapeDtypeStruct(shape, f32)

    outs = pl.pallas_call(
        functools.partial(finish_layer, plan),
        out_shape=(
            jax.ShapeDtypeStruct((rows, width), bf16),
            grad(rows, width),
            grad(sr, hc),
            grad(sr, hc),
            grad(sr, hc),
            grad(sr, hc),
            grad(sr, ff),
            grad(sr, ff),
            grad(sr, ff),
        )
        + (grad(1, sr),) * 4,
        in_specs=[anywhere] * 3,
        out_specs=(anywhere,) * 9 + (in_vmem,) * 4,
        scratch_shapes=[
            (
                pltpu.VMEM((rows, width), bf16),
                pltpu.VMEM((rows, width), f32),
                pltpu.VMEM((sr, plan.cols), f32),
            ),
            (pltpu.SemaphoreType.DMA((5,)), pltpu.SemaphoreType.DMA((7 + 2 * (ff // LANES),))),
        ],
        name="finish_layer",
    )(out, input_grad, total)
    outs = list(outs)
    outs[5], outs[8] = outs[5].T, outs[8].T
    return tuple(outs[:9]) + tuple(o[0] for o in outs[9:])


def fits_fused(mesh, tokens, query_weight, gate_weight, piece_starts):
    dp, tensor = mesh.shape["dp"], mesh.shape["tensor"]
    sequences, pieces = piece_starts.shape
    return (
        (dp, tensor, pieces, sequences) == (16, 2, 2, dp)
        and tokens.shape[0] % (dp * tensor * 256) == 0
        and tokens.shape[1] == query_weight.shape[1]
        and tokens.shape[1] % (dp * 16) == 0
        and query_weight.shape[1] % (tensor * 256) == 0
        and gate_weight.shape[1] % (tensor * LANES) == 0
    )


def solution(mesh):
    placed = (
        P(("dp", "tensor"), None),
        P("dp", "tensor"),
        P("dp", "tensor"),
        P("dp", "tensor"),
        P("tensor", "dp"),
        P("dp", "tensor"),
        P("dp", "tensor"),
        P("tensor", "dp"),
        P("dp"),
        P("dp"),
        P("dp"),
        P("dp"),
        P("dp", None),
        P(("dp", "tensor"), None),
    )
    def step(*arrays):
        fused = fits_fused(mesh, arrays[0], arrays[1], arrays[5], arrays[12])
        return place(fused_on_device if fused else on_device)(*arrays)

    def place(body):
        return jax.shard_map(
            body,
            mesh=mesh,
            in_specs=placed,
            out_specs=(
                P(("dp", "tensor"), None),
                P(("dp", "tensor"), None),
                P("dp", "tensor"),
                P("dp", "tensor"),
                P("dp", "tensor"),
                P("tensor", "dp"),
                P("dp", "tensor"),
                P("dp", "tensor"),
                P("tensor", "dp"),
                P("dp"),
                P("dp"),
                P("dp"),
                P("dp"),
            ),
            check_vma=False,
        )

    return step
```
